32 devices in a mesh: dp: 8 (over z, core), mp: 4 (over y, x).
Axes of the slice: x: 2, y: 2, z: 4, core: 2. Of those that a mesh axis runs over, the one named last changes fastest.
Arguments:
- x_in: bfloat16 [8, 1024, 2048], P('dp'), may hold values from -6 to 6
- lengths: int32 [8], P('dp'), may hold values from 512 to 1024, as said below
- gain_attn: bfloat16 [2048], P('dp'), may hold values from 0.5 to 1.5
- query_weight: bfloat16 [2048, 2048], P('dp', 'mp'), may hold values from -0.125 to 0.125
- key_projection_matrix: bfloat16 [2048, 4, 256], P('dp', None, 'mp'), may hold values from -0.125 to 0.125
- value_projection_matrix: bfloat16 [2048, 4, 256], P('dp', None, 'mp'), may hold values from -0.125 to 0.125
- out_weight: bfloat16 [2048, 2048], P('mp', 'dp'), may hold values from -0.75 to 0.75
- gain_ffn: bfloat16 [2048], P('dp'), may hold values from 0.5 to 1.5
- gate_weight: bfloat16 [2048, 8192], P('dp', 'mp'), may hold values from -0.125 to 0.125
- up_weight: bfloat16 [2048, 8192], P('dp', 'mp'), may hold values from -0.125 to 0.125
- down_weight: bfloat16 [8192, 2048], P('mp', 'dp'), may hold values from -0.0625 to 0.0625
- cotangent: bfloat16 [8, 1024, 2048], P('dp'), may hold values from -6 to 6
Outputs:
- layer_out: bfloat16 [8, 1024, 2048], P('dp')
- grad_input: float32 [8, 1024, 2048], P('dp')
- gain_attn_grad: float32 [2048], P('dp')
- query_grad: float32 [2048, 2048], P('dp', 'mp')
- key_projection_grad: float32 [2048, 4, 256], P('dp', None, 'mp')
- value_projection_grad: float32 [2048, 4, 256], P('dp', None, 'mp')
- out_grad: float32 [2048, 2048], P('mp', 'dp')
- gain_ffn_grad: float32 [2048], P('dp')
- gate_grad: float32 [2048, 8192], P('dp', 'mp')
- up_grad: float32 [2048, 8192], P('dp', 'mp')
- down_grad: float32 [8192, 2048], P('mp', 'dp')
The draws below stay inside these ranges and needn't reach their ends.
Inputs may be any that keep to these rules, and one draw needn't show every extreme that they name: A sequence's valid slots are its first lengths positions; in every draw some sequence fills all 1024 slots.
All inputs are finite; a program needn't handle non-finite values.
Results may differ from the reference program's by a relative error of at most 0.014.
Values may be sent and summed in bfloat16 or wider, within the bound.
No kernel may reach another device: no remote copies, remote signals or barrier semaphores. Data moves between devices by JAX's collectives and lax.ppermute only.
A program may use at most 256 MiB of HBM per device.

```python
import jax
import jax.numpy as jnp
from jax import lax

MODEL_WIDTH = 2048
QUERY_HEADS = 8
KEY_VALUE_HEADS = 4
HEAD_SIZE = 256
FF = 8192
SEQUENCE_SLOTS = 1024
SEQUENCE_COUNT = 8


def draw_lengths(key, part):
    key_vals = jax.random.fold_in(key, 11)
    key_pick = jax.random.fold_in(key, 12)
    drawn = jax.random.randint(key_vals, (SEQUENCE_COUNT,), SEQUENCE_SLOTS // 2, SEQUENCE_SLOTS + 1)
    chosen = jax.random.randint(key_pick, (), 0, SEQUENCE_COUNT)
    return jnp.where(jnp.arange(SEQUENCE_COUNT) == chosen, SEQUENCE_SLOTS, drawn).astype(jnp.int32)


def with_spikes(values, stream_key, source, target, blocks, factor):
    def block_of(axis_at):
        return (jnp.arange(values.shape[axis_at]) // (values.shape[axis_at] // blocks)).reshape((-1,) + (1,) * (values.ndim - 1 - axis_at))

    one_side = jax.random.permutation(stream_key, blocks)[block_of(target)]
    second = (block_of(target) + blocks // 2) % blocks
    return jnp.where((block_of(source) == one_side) | (block_of(source) == second), factor * values, values)


def block_levels(key, shape, pieces, least, largest):
    def one(dim, shards_of):
        steps = jax.random.uniform(jax.random.fold_in(jax.random.fold_in(key, 6), dim), (shards_of,), jnp.float32, least / len(pieces), largest / len(pieces))
        return jnp.repeat(jnp.exp(steps), shape[dim] // shards_of).reshape((-1,) + (1,) * (len(shape) - dim - 1))

    loudness = one(*pieces[0])
    for cut in pieces[1:]:
        loudness = loudness * one(*cut)
    return loudness


def centred(stream_key, dims, width, bound, shards=(), held_as=jnp.bfloat16):
    entries = width * jax.random.normal(stream_key, dims, jnp.float32)
    if shards:
        entries = entries * block_levels(stream_key, dims, shards, -0.22, 0.18)
    return jnp.clip(entries, -bound, bound).astype(held_as)


def noise_with(own_key, extent, scale, reach, shards, heavy, kind=jnp.bfloat16):
    values = scale * jax.random.normal(own_key, extent, jnp.float32)
    if shards:
        values = values * block_levels(own_key, extent, shards, -0.22, 0.18)
    return jnp.clip(with_spikes(values, jax.random.fold_in(own_key, 3), *heavy), -reach, reach).astype(kind)


def setup_inputs(seed: int = 0) -> dict:
    splits = jax.random.split(jax.random.key(seed), 13)
    return {
        "x_in": centred(splits[0], (SEQUENCE_COUNT, SEQUENCE_SLOTS, MODEL_WIDTH), 1.0, 6.0, ((0, 8),)),
        "lengths": draw_lengths(jax.random.fold_in(splits[12], 71), 0),
        "gain_attn": jnp.clip(1.0 + 0.1 * jax.random.normal(splits[2], (MODEL_WIDTH,), jnp.float32), 0.5, 1.5).astype(jnp.bfloat16),
        "query_weight": centred(splits[3], (MODEL_WIDTH, QUERY_HEADS * HEAD_SIZE), MODEL_WIDTH ** -0.5, 0.125, ((0, 8), (1, 4))),
        "key_projection_matrix": centred(splits[4], (MODEL_WIDTH, KEY_VALUE_HEADS, HEAD_SIZE), MODEL_WIDTH ** -0.5, 0.125, ((0, 8), (2, 4))),
        "value_projection_matrix": centred(splits[5], (MODEL_WIDTH, KEY_VALUE_HEADS, HEAD_SIZE), MODEL_WIDTH ** -0.5, 0.125, ((0, 8), (2, 4))),
        "out_weight": centred(splits[6], (QUERY_HEADS * HEAD_SIZE, MODEL_WIDTH), (QUERY_HEADS * HEAD_SIZE // 32) ** -0.5, 0.75, ((0, 4), (1, 8))),
        "gain_ffn": jnp.clip(1.0 + 0.1 * jax.random.normal(splits[7], (MODEL_WIDTH,), jnp.float32), 0.5, 1.5).astype(jnp.bfloat16),
        "gate_weight": centred(splits[8], (MODEL_WIDTH, FF), MODEL_WIDTH ** -0.5, 0.125, ((0, 8), (1, 4))),
        "up_weight": centred(splits[9], (MODEL_WIDTH, FF), MODEL_WIDTH ** -0.5, 0.125, ((0, 8), (1, 4))),
        "down_weight": centred(splits[10], (FF, MODEL_WIDTH), FF ** -0.5, 0.0625, ((0, 4), (1, 8))),
        "cotangent": noise_with(splits[11], (SEQUENCE_COUNT, SEQUENCE_SLOTS, MODEL_WIDTH), 1.0, 6.0, ((0, 8),), (0, 2, 8, 2.0)),
    }


@jax.custom_vjp
def reduced_precision(v):
    return lax.optimization_barrier(v.astype(jnp.bfloat16)).astype(jnp.float32)

@jax.custom_vjp
def reduced_precision_back(v):
    return v

def low_keep(v):
    return (reduced_precision(v), None)

def low_pass(kept, grad):
    return (grad,)

def back_keep(v):
    return (v, None)

def back_low(kept, grad):
    return (reduced_precision(grad),)
reduced_precision.defvjp(low_keep, low_pass)
reduced_precision_back.defvjp(back_keep, back_low)
eps_norm = 1e-06
rope_base = 1000042.0
neg_large = -1e+30
exact = lax.Precision.HIGHEST

def matrix_multiply(left, right):
    return jnp.dot(left, right, precision=exact, preferred_element_type=jnp.float32)

def rope_tables(slot_length, size):
    half_size = size // 2
    inv_freq = rope_base ** (-(jnp.arange(half_size, dtype=jnp.float32) * 2.0 / size))
    angles = jnp.arange(slot_length, dtype=jnp.float32)[:, None] * inv_freq[None, :]
    return (jnp.cos(angles), jnp.sin(angles))

def apply_rotation(values, cosine_lookup, sine_lookup):
    half_size = values.shape[-1] // 2
    first_half = values[..., :half_size]
    second_half = values[..., half_size:]
    cos_b = cosine_lookup[:, None, :]
    sin_b = sine_lookup[:, None, :]
    return jnp.concatenate([first_half * cos_b - second_half * sin_b, second_half * cos_b + first_half * sin_b], axis=-1)

def rms_gain(tok_rows, gain):
    factor = lax.rsqrt(lax.optimization_barrier(jnp.mean(tok_rows * tok_rows, axis=-1, keepdims=True)) + eps_norm)
    return tok_rows * factor * gain

def attend_one(packed):
    queries, keys_reduced, values_reduced, seq_len = packed
    query_group_width = QUERY_HEADS // KEY_VALUE_HEADS
    keys_rep = jnp.repeat(keys_reduced, query_group_width, axis=1)
    vals_rep = jnp.repeat(values_reduced, query_group_width, axis=1)
    raw_scores = reduced_precision_back(jnp.einsum('qhd,khd->hqk', queries, keys_rep, precision=exact))
    q_pos = jnp.arange(SEQUENCE_SLOTS)
    allowed = (q_pos[None, :] <= q_pos[:, None]) & (q_pos[None, :] < seq_len)
    scores = jnp.where(allowed[None], raw_scores * HEAD_SIZE ** (-0.5), neg_large)
    attn_probs = reduced_precision(jax.nn.softmax(scores, axis=-1))
    context = jnp.einsum('hqk,khd->qhd', attn_probs, vals_rep, precision=exact)
    return reduced_precision(reduced_precision_back(context))

def forward(tok_rows, gain_attn, query_weight, key_projection_matrix, value_projection_matrix, out_weight, gain_ffn, gate_weight, up_weight, down_weight, lengths):
    hidden_attention = reduced_precision(rms_gain(tok_rows, gain_attn))
    q_lin = reduced_precision_back(matrix_multiply(hidden_attention, query_weight))
    key_linear = reduced_precision_back(matrix_multiply(hidden_attention, key_projection_matrix.reshape(MODEL_WIDTH, KEY_VALUE_HEADS * HEAD_SIZE)))
    value_linear = reduced_precision_back(matrix_multiply(hidden_attention, value_projection_matrix.reshape(MODEL_WIDTH, KEY_VALUE_HEADS * HEAD_SIZE)))
    cosine_lookup, sine_lookup = rope_tables(SEQUENCE_SLOTS, HEAD_SIZE)
    queries = reduced_precision(apply_rotation(q_lin.reshape(SEQUENCE_COUNT, SEQUENCE_SLOTS, QUERY_HEADS, HEAD_SIZE), cosine_lookup, sine_lookup))
    keys_reduced = reduced_precision(apply_rotation(key_linear.reshape(SEQUENCE_COUNT, SEQUENCE_SLOTS, KEY_VALUE_HEADS, HEAD_SIZE), cosine_lookup, sine_lookup))
    values_reduced = reduced_precision(value_linear.reshape(SEQUENCE_COUNT, SEQUENCE_SLOTS, KEY_VALUE_HEADS, HEAD_SIZE))
    context = lax.map(jax.checkpoint(attend_one), (queries, keys_reduced, values_reduced, lengths))
    attn_rows = reduced_precision_back(matrix_multiply(context.reshape(SEQUENCE_COUNT * SEQUENCE_SLOTS, QUERY_HEADS * HEAD_SIZE), out_weight))
    mid_rows = tok_rows + attn_rows
    h_ffn = reduced_precision(rms_gain(mid_rows, gain_ffn))
    gate_proj = reduced_precision_back(matrix_multiply(h_ffn, gate_weight))
    up_proj = reduced_precision_back(matrix_multiply(h_ffn, up_weight))
    hidden = reduced_precision(jax.nn.silu(gate_proj) * up_proj)
    return mid_rows + reduced_precision_back(matrix_multiply(hidden, down_weight))

def reference(x_in, lengths, gain_attn, query_weight, key_projection_matrix, value_projection_matrix, out_weight, gain_ffn, gate_weight, up_weight, down_weight, cotangent):
    tok_rows = x_in.astype(jnp.float32).reshape(SEQUENCE_COUNT * SEQUENCE_SLOTS, MODEL_WIDTH)
    params = [p.astype(jnp.float32) for p in (gain_attn, query_weight, key_projection_matrix, value_projection_matrix, out_weight, gain_ffn, gate_weight, up_weight, down_weight)]
    valid_mask = (jnp.arange(SEQUENCE_SLOTS)[None, :] < lengths[:, None]).astype(jnp.float32)
    grad_o = (cotangent.astype(jnp.float32) * valid_mask[:, :, None]).reshape(SEQUENCE_COUNT * SEQUENCE_SLOTS, MODEL_WIDTH)

    def wrapped(rows_in, g_a, w_q, w_k, w_v, w_o, g_f, w_g, w_u, w_d):
        return forward(rows_in, g_a, w_q, w_k, w_v, w_o, g_f, w_g, w_u, w_d, lengths)
    out_rows, pull_back = jax.vjp(wrapped, tok_rows, *params)
    all_grads = pull_back(grad_o)
    return (out_rows.reshape(SEQUENCE_COUNT, SEQUENCE_SLOTS, MODEL_WIDTH).astype(jnp.bfloat16), all_grads[0].reshape(SEQUENCE_COUNT, SEQUENCE_SLOTS, MODEL_WIDTH), all_grads[1], all_grads[2], all_grads[3], all_grads[4], all_grads[5], all_grads[6], all_grads[7], all_grads[8], all_grads[9])
```

```python
import jax
import jax.numpy as jnp
from jax import lax
from jax.sharding import PartitionSpec as P

QUERY_HEADS = 8
KEY_VALUE_HEADS = 4
HEAD_SIZE = 256

eps_norm = 1e-06
rope_base = 1000042.0
neg_large = -1e30
bf16 = jnp.bfloat16
f32 = jnp.float32


def rope_tables(slot_length, size):
    half_size = size // 2
    inv_freq = rope_base ** (-(jnp.arange(half_size, dtype=f32) * 2.0 / size))
    angles = jnp.arange(slot_length, dtype=f32)[:, None] * inv_freq[None, :]
    return (jnp.cos(angles), jnp.sin(angles))


def rotate(values, cos_b, sin_b):
    half = values.shape[-1] // 2
    a, b = values[..., :half], values[..., half:]
    return jnp.concatenate([a * cos_b - b * sin_b, b * cos_b + a * sin_b], axis=-1)


def rotate_back(grads, cos_b, sin_b):
    half = grads.shape[-1] // 2
    a, b = grads[..., :half], grads[..., half:]
    return jnp.concatenate([a * cos_b + b * sin_b, b * cos_b - a * sin_b], axis=-1)


def mm(left, right):
    return lax.dot_general(left, right, (((1,), (0,)), ((), ())), preferred_element_type=f32)


def mm_t(left, right):
    return lax.dot_general(left, right, (((1,), (1,)), ((), ())), preferred_element_type=f32)


def mm_rows(left, right):
    return lax.dot_general(left, right, (((0,), (0,)), ((), ())), preferred_element_type=f32)


OVER_X = [(0, 1), (1, 0), (2, 3), (3, 2)]
OVER_Y = [(0, 2), (2, 0), (1, 3), (3, 1)]


def pick(blocks, which):
    return lax.dynamic_index_in_dim(blocks, which, 0, keepdims=False)


def scatter_rows(product, lefts, width):
    mp_size = lax.axis_size("mp")
    rows = lefts[0].shape[0]
    here = rows // mp_size
    if mp_size != 4:
        part = jnp.concatenate([product(lefts, 0), product(lefts, 1)], axis=1).astype(bf16)
        return lax.psum_scatter(part, "mp", scatter_dimension=0, tiled=True).astype(f32)
    me = lax.axis_index("mp")
    x, y = me % 2, me // 2
    half = width // 2

    def rows_x(which):
        return [
            lax.dynamic_index_in_dim(v.reshape(2, 2, here, v.shape[1]), which, 1, keepdims=False).reshape(
                2 * here, v.shape[1]
            )
            for v in lefts
        ]

    def rows_y(which):
        return [
            lax.dynamic_index_in_dim(v.reshape(2, 2 * here, v.shape[1]), which, 0, keepdims=False)
            for v in lefts
        ]

    away_a = lax.ppermute(product(rows_x(1 - x), 0).astype(bf16), "mp", OVER_X)
    away_b = lax.ppermute(product(rows_y(1 - y), 1).astype(bf16), "mp", OVER_Y)
    sum_a = (product(rows_x(x), 0) + away_a.astype(f32)).reshape(2, here, half)
    sum_b = (product(rows_y(y), 1) + away_b.astype(f32)).reshape(2, here, half)
    last_a = lax.ppermute(pick(sum_a, 1 - y).astype(bf16), "mp", OVER_Y)
    last_b = lax.ppermute(pick(sum_b, 1 - x).astype(bf16), "mp", OVER_X)
    return jnp.concatenate(
        [pick(sum_a, y) + last_a.astype(f32), pick(sum_b, x) + last_b.astype(f32)], axis=1
    )


def gather_rows(block):
    mp_size = lax.axis_size("mp")
    if mp_size != 4:
        return lax.all_gather(block, "mp", axis=0, tiled=True)
    me = lax.axis_index("mp")
    x, y = me % 2, me // 2
    here, width = block.shape
    half = width // 2
    own_a, own_b = block[:, :half], block[:, half:]

    def both(own, other, low):
        return jnp.where(low, own, other), jnp.where(low, other, own)

    got_a = lax.ppermute(own_a, "mp", OVER_Y)
    got_b = lax.ppermute(own_b, "mp", OVER_X)
    pair_a = jnp.stack(both(own_a, got_a, y == 0))
    pair_b = jnp.stack(both(own_b, got_b, x == 0))
    far_a = lax.ppermute(pair_a, "mp", OVER_X)
    far_b = lax.ppermute(pair_b, "mp", OVER_Y)
    all_a = jnp.stack(both(pair_a, far_a, x == 0), axis=1)
    all_b = jnp.stack(both(pair_b, far_b, y == 0), axis=0)
    return jnp.concatenate(
        [all_a.reshape(4 * here, half), all_b.reshape(4 * here, half)], axis=1
    )


def mask_block(first_row, block_rows, slots, seq_len):
    q_pos = first_row + jnp.arange(block_rows)
    k_pos = jnp.arange(slots)
    return (k_pos[None, :] <= q_pos[:, None]) & (k_pos[None, :] < seq_len)


def attend(queries, keys, values, seq_len, factor):
    slots = keys.shape[0]
    block_rows = min(512, slots)
    parts, totals = [], []
    for first_row in range(0, slots, block_rows):
        upto = first_row + block_rows
        raw = jnp.einsum(
            "qhd,kd->hqk", queries[first_row:upto], keys[:upto], preferred_element_type=f32
        )
        allowed = mask_block(first_row, block_rows, upto, seq_len)
        scores = jnp.where(allowed[None], raw * factor, neg_large)
        row_max = jnp.max(scores, axis=-1, keepdims=True)
        exps = jnp.exp(scores - row_max)
        total = jnp.sum(exps, axis=-1, keepdims=True)
        probs = (exps / total).astype(bf16)
        parts.append(
            jnp.einsum("hqk,kd->qhd", probs, values[:upto], preferred_element_type=f32).astype(bf16)
        )
        totals.append((row_max + jnp.log(total))[..., 0])
    return jnp.concatenate(parts, axis=0), jnp.concatenate(totals, axis=1)


def attend_back(queries, keys, values, grad_ctx, log_total, seq_len, factor):
    slots = keys.shape[0]
    block_rows = min(512, slots)
    dq_parts = []
    d_keys = jnp.zeros(keys.shape, f32)
    d_values = jnp.zeros(values.shape, f32)
    for first_row in range(0, slots, block_rows):
        upto = first_row + block_rows
        q_block = queries[first_row:upto]
        g_block = grad_ctx[first_row:upto]
        raw = jnp.einsum("qhd,kd->hqk", q_block, keys[:upto], preferred_element_type=f32)
        allowed = mask_block(first_row, block_rows, upto, seq_len)
        scores = jnp.where(allowed[None], raw * factor, neg_large)
        probs = jnp.exp(scores - log_total[:, first_row:upto, None])
        grad_p = jnp.einsum("qhd,kd->hqk", g_block, values[:upto], preferred_element_type=f32)
        inner = jnp.sum(probs * grad_p, axis=-1, keepdims=True)
        grad_s = (probs * (grad_p - inner) * factor).astype(bf16)
        dq_parts.append(
            jnp.einsum("hqk,kd->qhd", grad_s, keys[:upto], preferred_element_type=f32)
        )
        dk = jnp.einsum("hqk,qhd->kd", grad_s, q_block, preferred_element_type=f32)
        dv = jnp.einsum("hqk,qhd->kd", probs.astype(bf16), g_block, preferred_element_type=f32)
        d_keys = d_keys.at[:upto].add(dk)
        d_values = d_values.at[:upto].add(dv)
    return jnp.concatenate(dq_parts, axis=0), d_keys, d_values


def spread_heads(block):
    mp_size = lax.axis_size("mp")
    rows, heads, part = block.shape
    send = jnp.repeat(block, mp_size // heads, axis=1)
    got = lax.all_to_all(send, "mp", 1, 1, tiled=True)
    return got.reshape(rows, mp_size * part)


def collect_heads(block, heads):
    mp_size = lax.axis_size("mp")
    rows, size = block.shape
    got = lax.all_to_all(block.reshape(rows, mp_size, size // mp_size), "mp", 1, 1, tiled=True)
    got = got.reshape(rows, heads, mp_size // heads, size // mp_size)
    return jnp.sum(got.astype(f32), axis=2)


def gather_dp(block):
    return lax.all_gather(block, "dp", axis=0, tiled=True)


def reduce_dp(block):
    return lax.psum_scatter(block, "dp", scatter_dimension=0, tiled=True)


def local(
    x_in,
    lengths,
    gain_attn,
    query_weight,
    key_projection_matrix,
    value_projection_matrix,
    out_weight,
    gain_ffn,
    gate_weight,
    up_weight,
    down_weight,
    cotangent,
):
    _, slots, width = x_in.shape
    mp_size = lax.axis_size("mp")
    me = lax.axis_index("mp")
    heads_here = query_weight.shape[1] // HEAD_SIZE
    q_cols = query_weight.shape[1]
    factor = HEAD_SIZE ** (-0.5)
    here = slots // mp_size
    seq_len = lengths[0]
    cos_t, sin_t = rope_tables(slots, HEAD_SIZE)

    kv_block = jnp.concatenate(
        [spread_heads(key_projection_matrix), spread_heads(value_projection_matrix)], axis=1
    )
    gains = lax.all_gather(jnp.stack([gain_attn, gain_ffn]), "dp", axis=1, tiled=True).astype(f32)
    g_attn, g_ffn = gains[0], gains[1]
    w_q = gather_dp(query_weight)
    w_kv = gather_dp(kv_block)
    w_o = gather_dp(out_weight.T)
    w_g = gather_dp(gate_weight)
    w_u = gather_dp(up_weight)
    w_d = gather_dp(down_weight.T)

    tok = x_in[0].astype(f32)
    r1 = lax.rsqrt(jnp.mean(tok * tok, axis=-1, keepdims=True) + eps_norm)
    h_attn = (tok * r1 * g_attn).astype(bf16)
    cos_h, sin_h = cos_t[:, None, :], sin_t[:, None, :]
    queries = rotate(
        mm(h_attn, w_q).reshape(slots, heads_here, HEAD_SIZE), cos_h, sin_h
    ).astype(bf16)
    kv_lin = mm(h_attn, w_kv)
    keys = rotate(kv_lin[:, :HEAD_SIZE], cos_t, sin_t).astype(bf16)
    values = kv_lin[:, HEAD_SIZE:].astype(bf16)
    context, log_total = attend(queries, keys, values, seq_len, factor)
    context = context.reshape(slots, q_cols)

    half = width // 2

    def product_out(lefts, which):
        return mm_t(lefts[0], w_o[which * half : (which + 1) * half])

    attn_rows = scatter_rows(product_out, [context], width)
    tok_here = lax.dynamic_slice_in_dim(x_in[0], me * here, here, 0).astype(f32)
    mid = tok_here + attn_rows
    r2 = lax.rsqrt(jnp.mean(mid * mid, axis=-1, keepdims=True) + eps_norm)
    n2 = mid * r2
    h_ffn = gather_rows((n2 * g_ffn).astype(bf16))

    gate = mm(h_ffn, w_g)
    up = mm(h_ffn, w_u)
    sig = jax.nn.sigmoid(gate)
    hidden = (gate * sig * up).astype(bf16)

    valid = (jnp.arange(slots)[:, None] < seq_len).astype(bf16)
    grad_low = cotangent[0] * valid
    down_grad = mm_rows(grad_low, hidden).astype(bf16)
    down_out = reduce_dp(down_grad)

    d_hidden = mm(grad_low, w_d)
    d_gate = (d_hidden * up * sig * (1.0 + gate * (1.0 - sig))).astype(bf16)
    d_up = (d_hidden * gate * sig).astype(bf16)

    def product_h2(lefts, which):
        cols = slice(which * half, (which + 1) * half)
        return mm_t(lefts[0], w_g[cols]) + mm_t(lefts[1], w_u[cols])

    d_h2 = scatter_rows(product_h2, [d_gate, d_up], width)
    gate_out = reduce_dp(mm_rows(h_ffn, d_gate).astype(bf16))
    up_out = reduce_dp(mm_rows(h_ffn, d_up).astype(bf16))

    gain_ffn_part = jnp.sum(d_h2 * n2, axis=0)
    e2 = d_h2 * g_ffn
    grad_here = lax.dynamic_slice_in_dim(grad_low, me * here, here, 0).astype(f32)
    g1 = grad_here + r2 * (e2 - n2 * jnp.mean(e2 * n2, axis=-1, keepdims=True))
    g1_low = gather_rows(g1.astype(bf16))

    def product_ffn(lefts, which):
        return mm_t(lefts[0], w_d[which * half : (which + 1) * half])

    ffn_rows = scatter_rows(product_ffn, [hidden], width)
    layer_out = gather_rows((mid + ffn_rows).astype(bf16))

    d_context = mm(g1_low, w_o).astype(bf16).reshape(slots, heads_here, HEAD_SIZE)
    out_out = reduce_dp(mm_rows(g1_low, context).astype(bf16))
    dq, dk, dv = attend_back(
        queries, keys, values, d_context, log_total, seq_len, factor
    )
    d_q = rotate_back(dq, cos_h, sin_h).astype(bf16).reshape(slots, q_cols)
    d_kv = jnp.concatenate([rotate_back(dk, cos_t, sin_t), dv], axis=1).astype(bf16)
    q_out = reduce_dp(mm_rows(h_attn, d_q).astype(bf16))
    kv_out = reduce_dp(mm_rows(h_attn, d_kv).astype(bf16))

    def product_h1(lefts, which):
        cols = slice(which * half, (which + 1) * half)
        return mm_t(lefts[0], w_q[cols]) + mm_t(lefts[1], w_kv[cols])

    d_h1 = scatter_rows(product_h1, [d_q, d_kv], width)
    r1_here = lax.dynamic_slice_in_dim(r1, me * here, here, 0)
    n1 = tok_here * r1_here
    gain_attn_part = jnp.sum(d_h1 * n1, axis=0)
    e1 = d_h1 * g_attn
    grad_in = g1 + r1_here * (e1 - n1 * jnp.mean(e1 * n1, axis=-1, keepdims=True))
    grad_input = gather_rows(grad_in.astype(bf16)).astype(f32)

    gain_parts = lax.psum(jnp.stack([gain_attn_part, gain_ffn_part]), ("dp", "mp"))
    rows_here = gain_attn.shape[0]
    gain_grads = lax.dynamic_slice_in_dim(
        gain_parts, lax.axis_index("dp") * rows_here, rows_here, 1
    )
    key_grad = collect_heads(kv_out[:, :HEAD_SIZE], KEY_VALUE_HEADS)
    value_grad = collect_heads(kv_out[:, HEAD_SIZE:], KEY_VALUE_HEADS)
    return (
        layer_out[None],
        grad_input[None],
        gain_grads[0],
        q_out.astype(f32),
        key_grad,
        value_grad,
        out_out.T.astype(f32),
        gain_grads[1],
        gate_out.astype(f32),
        up_out.astype(f32),
        down_out.T.astype(f32),
    )


def solution(mesh):
    return jax.shard_map(
        local,
        mesh=mesh,
        in_specs=(
            P("dp", None, None),
            P("dp"),
            P("dp"),
            P("dp", "mp"),
            P("dp", None, "mp"),
            P("dp", None, "mp"),
            P("mp", "dp"),
            P("dp"),
            P("dp", "mp"),
            P("dp", "mp"),
            P("mp", "dp"),
            P("dp", None, None),
        ),
        out_specs=(
            P("dp", None, None),
            P("dp", None, None),
            P("dp"),
            P("dp", "mp"),
            P("dp", None, "mp"),
            P("dp", None, "mp"),
            P("mp", "dp"),
            P("dp"),
            P("dp", "mp"),
            P("dp", "mp"),
            P("mp", "dp"),
        ),
        check_vma=False,
    )
```

```python
import jax
import jax.numpy as jnp
from jax import lax
from jax.experimental import pallas as pl
from jax.experimental.pallas import tpu as pltpu
from jax.sharding import Mesh, PartitionSpec as P

QUERY_HEADS = 8
KEY_VALUE_HEADS = 4
HEAD_SIZE = 256

eps_norm = 1e-06
rope_base = 1000042.0
neg_large = -1e30
bf16 = jnp.bfloat16
f32 = jnp.float32


def rope_tables(slot_length, size):
    half_size = size // 2
    inv_freq = rope_base ** (-(jnp.arange(half_size, dtype=f32) * 2.0 / size))
    angles = jnp.arange(slot_length, dtype=f32)[:, None] * inv_freq[None, :]
    return (jnp.cos(angles), jnp.sin(angles))


def rotate(values, cos_b, sin_b):
    half = values.shape[-1] // 2
    a, b = values[..., :half], values[..., half:]
    return jnp.concatenate([a * cos_b - b * sin_b, b * cos_b + a * sin_b], axis=-1)


def rotate_back(grads, cos_b, sin_b):
    half = grads.shape[-1] // 2
    a, b = grads[..., :half], grads[..., half:]
    return jnp.concatenate([a * cos_b + b * sin_b, b * cos_b - a * sin_b], axis=-1)


def mm(left, right):
    return lax.dot_general(left, right, (((1,), (0,)), ((), ())), preferred_element_type=f32)


def mm_t(left, right):
    return lax.dot_general(left, right, (((1,), (1,)), ((), ())), preferred_element_type=f32)


def mm_rows(left, right):
    return lax.dot_general(left, right, (((0,), (0,)), ((), ())), preferred_element_type=f32)


DP = ("z", "core")
OVER_X = [(0, 1), (1, 0), (2, 3), (3, 2)]
OVER_Y = [(0, 2), (2, 0), (1, 3), (3, 1)]
OVER_CORE = [(0, 1), (1, 0)]


def send_x(v):
    return lax.ppermute(v, "mp", OVER_X)


def send_y(v):
    return lax.ppermute(v, "mp", OVER_Y)


def send_core(v):
    return lax.ppermute(v, "core", OVER_CORE)


def square():
    return lax.axis_size("mp") == 4


def after(value, *earlier):
    return lax.optimization_barrier((value,) + earlier)[0]


def relative_rows(v):
    if not square():
        return v
    me = lax.axis_index("mp")
    here = v.shape[0] // 4
    return jnp.concatenate(
        [lax.dynamic_slice_in_dim(v, jnp.bitwise_xor(me, m) * here, here, 0) for m in (0, 2, 1, 3)]
    )


def sequence_rows(v):
    if not square():
        return v
    me = lax.axis_index("mp")
    here = v.shape[0] // 4
    out = []
    for m in range(4):
        away = jnp.bitwise_xor(me, m)
        slot = (away % 2) * 2 + away // 2
        out.append(lax.dynamic_slice_in_dim(v, slot * here, here, 0))
    return jnp.concatenate(out)


def scatter_rows(blocks, hold=()):
    if not square():
        part = blocks(0, 4).astype(bf16)
        return lax.psum_scatter(part, "mp", scatter_dimension=0, tiled=True).astype(f32)
    far = blocks(2, 4)
    here = far.shape[0] // 2
    half = far.shape[1] // 2
    low = far.astype(bf16)
    if hold:
        low = after(low, *hold)
    p1 = send_x(low[here:, :half])
    q1 = send_y(low[here:, half:])
    p2 = send_x(low[:here, :half])
    near = blocks(0, 2)
    q2 = send_y(near[here:, half:].astype(bf16))
    q3 = send_y((near[here:, :half] + p1.astype(f32)).astype(bf16))
    p3 = send_x((far[:here, half:] + q1.astype(f32)).astype(bf16))
    own = near[:here]
    return jnp.concatenate(
        [
            own[:, :half] + p2.astype(f32) + q3.astype(f32),
            own[:, half:] + p3.astype(f32) + q2.astype(f32),
        ],
        axis=1,
    )


def assemble_kernel(slots_ref, own, x_a, x_b, y_a, y_b, d_a, d_b, out_ref):
    half = x_a.shape[1]
    step = pl.program_id(0)

    @pl.when(step == 0)
    def _():
        out_ref[...] = own[...].astype(out_ref.dtype)

    for i, (a, b) in enumerate([(y_a, y_b), (x_a, x_b), (d_a, d_b)]):

        @pl.when(step == i + 1)
        def _(a=a, b=b):
            out_ref[:, :half] = a[...].astype(out_ref.dtype)
            out_ref[:, half:] = b[...].astype(out_ref.dtype)


def assemble(slots, pieces, dtype):
    here, width = pieces[0].shape
    half = pieces[1].shape[1]
    return pl.pallas_call(
        assemble_kernel,
        name="assemble",
        grid_spec=pltpu.PrefetchScalarGridSpec(
            num_scalar_prefetch=1,
            grid=(4,),
            in_specs=[pl.BlockSpec((here, width), lambda i, s: (0, 0))]
            + [pl.BlockSpec((here, half), lambda i, s: (0, 0))] * 6,
            out_specs=pl.BlockSpec((here, width), lambda i, s: (s[i], 0)),
        ),
        out_shape=jax.ShapeDtypeStruct((4 * here, width), dtype),
        cost_estimate=pl.CostEstimate(flops=0, transcendentals=0, bytes_accessed=20 * here * width),
        compiler_params=pltpu.CompilerParams(vmem_limit_bytes=40 << 20),
    )(slots, *pieces)


def gather_rows(block, relative, dtype=bf16):
    if not square():
        return lax.all_gather(block, "mp", axis=0, tiled=True).astype(dtype)
    half = block.shape[1] // 2
    own_a, own_b = block[:, :half], block[:, half:]
    y_a = send_y(own_a)
    x_b = send_x(own_b)
    y_b = send_y(own_b)
    x_a = send_x(own_a)
    d_a = send_x(y_a)
    d_b = send_y(x_b)
    steps = jnp.arange(4, dtype=jnp.int32)
    if not relative:
        me = lax.axis_index("mp").astype(jnp.int32)
        steps = jnp.bitwise_xor(me, jnp.array([0, 2, 1, 3], jnp.int32))
    return assemble(steps, [block, x_a, x_b, y_a, y_b, d_a, d_b], dtype)


def sum_all(v):
    if not square() or lax.axis_size("z") != 4:
        return lax.psum(v, DP + ("mp",))
    v = v + send_x(v)
    v = v + send_y(v)
    v = v + send_core(v)
    v = v + lax.ppermute(v, "z", [(0, 1), (1, 0), (2, 3), (3, 2)])
    return v + lax.ppermute(v, "z", [(0, 3), (3, 0), (1, 2), (2, 1)])


def mask_block(first_row, block_rows, slots, seq_len):
    q_pos = first_row + jnp.arange(block_rows)
    k_pos = jnp.arange(slots)
    return (k_pos[None, :] <= q_pos[:, None]) & (k_pos[None, :] < seq_len)


def attend(queries, keys, values, seq_len, factor):
    slots = keys.shape[0]
    block_rows = min(512, slots)
    parts, totals = [], []
    for first_row in range(0, slots, block_rows):
        upto = first_row + block_rows
        raw = jnp.einsum(
            "qhd,kd->hqk", queries[first_row:upto], keys[:upto], preferred_element_type=f32
        )
        allowed = mask_block(first_row, block_rows, upto, seq_len)
        scores = jnp.where(allowed[None], raw * factor, neg_large)
        row_max = jnp.max(scores, axis=-1, keepdims=True)
        exps = jnp.exp(scores - row_max)
        total = jnp.sum(exps, axis=-1, keepdims=True)
        probs = (exps / total).astype(bf16)
        parts.append(
            jnp.einsum("hqk,kd->qhd", probs, values[:upto], preferred_element_type=f32).astype(bf16)
        )
        totals.append((row_max + jnp.log(total))[..., 0])
    return jnp.concatenate(parts, axis=0), jnp.concatenate(totals, axis=1)


def attend_back(queries, keys, values, grad_ctx, log_total, seq_len, factor):
    slots = keys.shape[0]
    block_rows = min(512, slots)
    dq_parts = []
    d_keys = jnp.zeros(keys.shape, f32)
    d_values = jnp.zeros(values.shape, f32)
    for first_row in range(0, slots, block_rows):
        upto = first_row + block_rows
        q_block = queries[first_row:upto]
        g_block = grad_ctx[first_row:upto]
        raw = jnp.einsum("qhd,kd->hqk", q_block, keys[:upto], preferred_element_type=f32)
        allowed = mask_block(first_row, block_rows, upto, seq_len)
        scores = jnp.where(allowed[None], raw * factor, neg_large)
        probs = jnp.exp(scores - log_total[:, first_row:upto, None])
        grad_p = jnp.einsum("qhd,kd->hqk", g_block, values[:upto], preferred_element_type=f32)
        inner = jnp.sum(probs * grad_p, axis=-1, keepdims=True)
        grad_s = (probs * (grad_p - inner) * factor).astype(bf16)
        dq_parts.append(
            jnp.einsum("hqk,kd->qhd", grad_s, keys[:upto], preferred_element_type=f32)
        )
        dk = jnp.einsum("hqk,qhd->kd", grad_s, q_block, preferred_element_type=f32)
        dv = jnp.einsum("hqk,qhd->kd", probs.astype(bf16), g_block, preferred_element_type=f32)
        d_keys = d_keys.at[:upto].add(dk)
        d_values = d_values.at[:upto].add(dv)
    return jnp.concatenate(dq_parts, axis=0), d_keys, d_values


def spread_heads(block):
    mp_size = lax.axis_size("mp")
    rows, n, heads, part = block.shape
    send = jnp.repeat(block, mp_size // heads, axis=2)
    got = lax.all_to_all(send, "mp", 2, 2, tiled=True)
    return got.reshape(rows, n * mp_size * part)


def collect_heads(block, heads):
    mp_size = lax.axis_size("mp")
    rows, n, size = block.shape
    part = size // mp_size
    got = lax.all_to_all(block.reshape(rows, n, mp_size, part), "mp", 2, 2, tiled=True)
    return jnp.sum(got.reshape(rows, n, heads, mp_size // heads, part).astype(f32), axis=3)


def gather_dp(block):
    return lax.all_gather(block, DP, axis=0, tiled=True)


def reduce_dp(block):
    return lax.psum_scatter(block, DP, scatter_dimension=0, tiled=True)


def gather_z(block):
    return lax.all_gather(block, "z", axis=0, tiled=True)


def reduce_z(block):
    return lax.psum_scatter(block, "z", scatter_dimension=0, tiled=True)


def to_core(block):
    rows, n, cols = block.shape
    core = lax.axis_index("core")
    m = cols // 2
    own = lax.dynamic_slice_in_dim(block, core * m, m, 2).reshape(rows, n * m)
    away = lax.dynamic_slice_in_dim(block, (1 - core) * m, m, 2).reshape(rows, n * m)
    got = send_core(away)
    return jnp.concatenate([jnp.where(core == 0, own, got), jnp.where(core == 0, got, own)])


def from_core(block, n):
    rows = block.shape[0] // 2
    m = block.shape[1] // n
    core = lax.axis_index("core")
    own = lax.dynamic_slice_in_dim(block, core * rows, rows, 0)
    away = lax.dynamic_slice_in_dim(block, (1 - core) * rows, rows, 0)
    got = send_core(away)
    low, high = jnp.where(core == 0, own, got), jnp.where(core == 0, got, own)
    return [
        jnp.concatenate([low[:, i * m : (i + 1) * m], high[:, i * m : (i + 1) * m]], axis=1)
        for i in range(n)
    ]


def ffn_forward_kernel(mine_ref, away_ref, g_ref, u_ref, hidden_ref, factor_ref):
    def run(h_ref):
        h = h_ref[...]
        gate = jnp.dot(h, g_ref[...], preferred_element_type=f32)
        up = jnp.dot(h, u_ref[...], preferred_element_type=f32)
        sig = 1.0 / (1.0 + jnp.exp(-gate))
        silu = gate * sig
        hidden_ref[...] = (silu * up).astype(bf16)
        factor_ref[0] = (up * sig * (1.0 + gate - silu)).astype(bf16)
        factor_ref[1] = silu.astype(bf16)

    pl.when(pl.program_id(0) == 0)(lambda: run(mine_ref))
    pl.when(pl.program_id(0) == 1)(lambda: run(away_ref))


def tile(size, most):
    while size % most:
        most //= 2
    return most


def ffn_forward(mine, away, w_gu):
    rows, width = mine.shape
    ff = w_gu.shape[1] // 2
    tn = tile(ff, 256)
    return pl.pallas_call(
        ffn_forward_kernel,
        name="ffn_forward",
        grid=(2, ff // tn),
        in_specs=[
            pl.BlockSpec((rows, width), lambda i, j: (0, 0)),
            pl.BlockSpec((rows, width), lambda i, j: (0, 0)),
            pl.BlockSpec((width, tn), lambda i, j: (0, j)),
            pl.BlockSpec((width, tn), lambda i, j: (0, j + ff // tn)),
        ],
        out_specs=[
            pl.BlockSpec((rows, tn), lambda i, j: (i, j)),
            pl.BlockSpec((2, rows, tn), lambda i, j: (0, i, j)),
        ],
        out_shape=[
            jax.ShapeDtypeStruct((2 * rows, ff), bf16),
            jax.ShapeDtypeStruct((2, 2 * rows, ff), bf16),
        ],
        cost_estimate=pl.CostEstimate(
            flops=8 * rows * width * ff,
            transcendentals=2 * rows * ff,
            bytes_accessed=4 * (rows * width + width * ff + 3 * rows * ff),
        ),
        compiler_params=pltpu.CompilerParams(vmem_limit_bytes=56 << 20),
    )(mine, away, w_gu, w_gu)


def rows_product_kernel(mine_ref, away_ref, right_mine_ref, right_away_ref, out_ref):
    def dot(left, right):
        return lax.dot_general(
            left[...], right[...], (((0,), (0,)), ((), ())), preferred_element_type=f32
        )

    out_ref[...] = (dot(mine_ref, right_mine_ref) + dot(away_ref, right_away_ref)).astype(bf16)


def rows_product(mine, away, right):
    rows, width = mine.shape
    cols = right.shape[1]
    tm = tile(width, 256)
    return pl.pallas_call(
        rows_product_kernel,
        name="rows_product",
        grid=(width // tm,),
        in_specs=[
            pl.BlockSpec((rows, tm), lambda i: (0, i)),
            pl.BlockSpec((rows, tm), lambda i: (0, i)),
            pl.BlockSpec((rows, cols), lambda i: (0, 0)),
            pl.BlockSpec((rows, cols), lambda i: (1, 0)),
        ],
        out_specs=pl.BlockSpec((tm, cols), lambda i: (i, 0)),
        out_shape=jax.ShapeDtypeStruct((width, cols), bf16),
        cost_estimate=pl.CostEstimate(
            flops=4 * rows * width * cols,
            transcendentals=0,
            bytes_accessed=4 * rows * (width + cols) + 2 * width * cols,
        ),
        compiler_params=pltpu.CompilerParams(vmem_limit_bytes=56 << 20),
    )(mine, away, right, right)


def ffn_backward_kernel(grad_ref, d_ref, factor_ref, out_ref, d_hidden_ref):
    @pl.when(pl.program_id(2) == 0)
    def _():
        d_hidden_ref[...] = jnp.dot(grad_ref[...], d_ref[...], preferred_element_type=f32)

    out_ref[...] = (d_hidden_ref[...] * factor_ref[0].astype(f32)).astype(bf16)


def ffn_backward(grad, w_d, factors):
    rows, width = grad.shape
    ff = w_d.shape[1]
    tm, tn = tile(rows, 1024), tile(ff, 512)
    return pl.pallas_call(
        ffn_backward_kernel,
        name="ffn_backward",
        grid=(rows // tm, ff // tn, 2),
        in_specs=[
            pl.BlockSpec((tm, width), lambda i, j, k: (i, 0)),
            pl.BlockSpec((width, tn), lambda i, j, k: (0, j)),
            pl.BlockSpec((1, tm, tn), lambda i, j, k: (k, i, j)),
        ],
        out_specs=pl.BlockSpec((tm, tn), lambda i, j, k: (i, j + k * (ff // tn))),
        out_shape=jax.ShapeDtypeStruct((rows, 2 * ff), bf16),
        scratch_shapes=[pltpu.VMEM((tm, tn), f32)],
        cost_estimate=pl.CostEstimate(
            flops=2 * rows * width * ff, transcendentals=0, bytes_accessed=2 * (rows * width + width * ff + 4 * rows * ff)
        ),
        compiler_params=pltpu.CompilerParams(vmem_limit_bytes=56 << 20),
    )(grad, w_d, factors)


def local(
    x_in,
    lengths,
    gain_attn,
    query_weight,
    key_projection_matrix,
    value_projection_matrix,
    out_weight,
    gain_ffn,
    gate_weight,
    up_weight,
    down_weight,
    cotangent,
):
    _, slots, width = x_in.shape
    mp_size = lax.axis_size("mp")
    me = lax.axis_index("mp")
    heads_here = query_weight.shape[1] // HEAD_SIZE
    q_cols = query_weight.shape[1]
    factor = HEAD_SIZE ** (-0.5)
    here = slots // mp_size
    quarter = slots // 4
    seq_len = lengths[0]
    cos_t, sin_t = rope_tables(slots, HEAD_SIZE)

    def own_rows(v):
        return lax.dynamic_slice_in_dim(v, me * here, here, 0)

    w_o = gather_dp(out_weight.T)
    kv_block = spread_heads(jnp.stack([key_projection_matrix, value_projection_matrix], axis=1))
    w_qkv = gather_dp(jnp.concatenate([query_weight, kv_block], axis=1))
    gains = lax.all_gather(jnp.stack([gain_attn, gain_ffn]), DP, axis=1, tiled=True).astype(f32)
    g_attn, g_ffn = gains[0], gains[1]
    ffn_block = to_core(jnp.stack([gate_weight, up_weight, down_weight.T], axis=1))
    ff = ffn_block.shape[1] // 3
    w_gu = gather_z(ffn_block[:, : 2 * ff])
    w_d = gather_z(ffn_block[:, 2 * ff :])

    tok = x_in[0].astype(f32)
    r1 = lax.rsqrt(jnp.mean(tok * tok, axis=-1, keepdims=True) + eps_norm)
    h_attn = (tok * r1 * g_attn).astype(bf16)
    valid = (jnp.arange(slots)[:, None] < seq_len).astype(bf16)
    grad_low = cotangent[0] * valid
    grad_mine = relative_rows(grad_low)
    grad_all = jnp.concatenate([grad_mine, send_core(grad_mine)])
    cos_h, sin_h = cos_t[:, None, :], sin_t[:, None, :]
    qkv = mm(h_attn, w_qkv)
    queries = rotate(
        qkv[:, :q_cols].reshape(slots, heads_here, HEAD_SIZE), cos_h, sin_h
    ).astype(bf16)
    keys = rotate(qkv[:, q_cols : q_cols + HEAD_SIZE], cos_t, sin_t).astype(bf16)
    values = qkv[:, q_cols + HEAD_SIZE :].astype(bf16)
    context, log_total = attend(queries, keys, values, seq_len, factor)
    context = relative_rows(context.reshape(slots, q_cols))

    attn_rows = scatter_rows(lambda i, j: mm_t(context[i * quarter : j * quarter], w_o))
    tok_here = own_rows(x_in[0]).astype(f32)
    mid = tok_here + attn_rows
    r2 = lax.rsqrt(jnp.mean(mid * mid, axis=-1, keepdims=True) + eps_norm)
    n2 = mid * r2
    h_mine = gather_rows((n2 * g_ffn).astype(bf16), True)
    h_away = send_core(h_mine)

    hidden, factors = ffn_forward(h_mine, h_away, w_gu)
    down_grad = mm_rows(grad_all, hidden).astype(bf16)
    down_out = reduce_z(down_grad)
    d_gu = ffn_backward(grad_all, w_d, factors)

    def with_core(left, product):
        away_high = send_core(product(left[slots + 2 * quarter :]).astype(bf16)).astype(f32)
        away_low = send_core(product(left[slots : slots + 2 * quarter]).astype(bf16)).astype(f32)

        def blocks(i, j):
            mine = product(left[i * quarter : j * quarter])
            if j - i == 4:
                return mine + jnp.concatenate([away_low, away_high])
            return mine + (away_high if i else away_low)

        return blocks

    d_h2 = scatter_rows(with_core(d_gu, lambda v: mm_t(v, w_gu)))
    gu_out = reduce_z(rows_product(h_mine, h_away, d_gu))

    gain_ffn_part = jnp.sum(d_h2 * n2, axis=0)
    e2 = d_h2 * g_ffn
    g1 = own_rows(grad_low).astype(f32) + r2 * (e2 - n2 * jnp.mean(e2 * n2, axis=-1, keepdims=True))
    g1_low = gather_rows(g1.astype(bf16), True)

    ffn_rows = scatter_rows(with_core(hidden, lambda v: mm_t(v, w_d)), hold=(g1_low,))
    layer_out = gather_rows((mid + ffn_rows).astype(bf16), False)

    d_context = sequence_rows(mm(g1_low, w_o).astype(bf16)).reshape(slots, heads_here, HEAD_SIZE)
    out_out = reduce_dp(mm_rows(g1_low, context).astype(bf16))
    dq, dk, dv = attend_back(queries, keys, values, d_context, log_total, seq_len, factor)
    d_q = rotate_back(dq, cos_h, sin_h).reshape(slots, q_cols)
    d_qkv = jnp.concatenate([d_q, rotate_back(dk, cos_t, sin_t), dv], axis=1).astype(bf16)
    qkv_out = reduce_dp(mm_rows(h_attn, d_qkv).astype(bf16))

    d_qkv_rel = relative_rows(d_qkv)
    d_h1 = scatter_rows(lambda i, j: mm_t(d_qkv_rel[i * quarter : j * quarter], w_qkv))
    r1_here = own_rows(r1)
    n1 = tok_here * r1_here
    gain_attn_part = jnp.sum(d_h1 * n1, axis=0)
    e1 = d_h1 * g_attn
    grad_in = g1 + r1_here * (e1 - n1 * jnp.mean(e1 * n1, axis=-1, keepdims=True))
    grad_input = gather_rows(grad_in.astype(bf16), False, f32)

    rows_here = gain_attn.shape[0]

    def gain_grad(part):
        total = sum_all(part.reshape(-1, 128)).reshape(-1)
        return lax.dynamic_slice_in_dim(total, lax.axis_index(DP) * rows_here, rows_here, 0)

    gate_out, up_out = from_core(gu_out, 2)
    (down_out,) = from_core(down_out, 1)
    kv_grad = collect_heads(
        qkv_out[:, q_cols:].reshape(rows_here, 2, HEAD_SIZE), KEY_VALUE_HEADS
    )
    return (
        layer_out[None],
        grad_input[None],
        gain_grad(gain_attn_part),
        qkv_out[:, :q_cols].astype(f32),
        kv_grad[:, 0],
        kv_grad[:, 1],
        out_out.T.astype(f32),
        gain_grad(gain_ffn_part),
        gate_out.astype(f32),
        up_out.astype(f32),
        down_out.T.astype(f32),
    )


def solution(mesh):
    dp_size, mp_size = mesh.shape["dp"], mesh.shape["mp"]
    split = Mesh(mesh.devices.reshape(dp_size // 2, 2, mp_size), ("z", "core", "mp"))
    return jax.shard_map(
        local,
        mesh=split,
        in_specs=(
            P(DP, None, None),
            P(DP),
            P(DP),
            P(DP, "mp"),
            P(DP, None, "mp"),
            P(DP, None, "mp"),
            P("mp", DP),
            P(DP),
            P(DP, "mp"),
            P(DP, "mp"),
            P("mp", DP),
            P(DP, None, None),
        ),
        out_specs=(
            P(DP, None, None),
            P(DP, None, None),
            P(DP),
            P(DP, "mp"),
            P(DP, None, "mp"),
            P(DP, None, "mp"),
            P("mp", DP),
            P(DP),
            P(DP, "mp"),
            P(DP, "mp"),
            P("mp", DP),
        ),
        check_vma=False,
    )
```

```python
import functools

import jax
import jax.numpy as jnp
from jax import lax
from jax.experimental import pallas as pl
from jax.experimental.pallas import tpu as pltpu
from jax.sharding import Mesh, PartitionSpec as P

QUERY_HEADS = 8
KEY_VALUE_HEADS = 4
HEAD_SIZE = 256

eps_norm = 1e-06
rope_base = 1000042.0
neg_large = -1e30
bf16 = jnp.bfloat16
f32 = jnp.float32


def rope_tables(slot_length, size):
    half_size = size // 2
    inv_freq = rope_base ** (-(jnp.arange(half_size, dtype=f32) * 2.0 / size))
    angles = jnp.arange(slot_length, dtype=f32)[:, None] * inv_freq[None, :]
    return (jnp.cos(angles), jnp.sin(angles))


def rotate(values, cos_b, sin_b):
    half = values.shape[-1] // 2
    a, b = values[..., :half], values[..., half:]
    return jnp.concatenate([a * cos_b - b * sin_b, b * cos_b + a * sin_b], axis=-1)


def rotate_back(grads, cos_b, sin_b):
    half = grads.shape[-1] // 2
    a, b = grads[..., :half], grads[..., half:]
    return jnp.concatenate([a * cos_b + b * sin_b, b * cos_b - a * sin_b], axis=-1)


def mm(left, right):
    return lax.dot_general(left, right, (((1,), (0,)), ((), ())), preferred_element_type=f32)


def mm_t(left, right):
    return lax.dot_general(left, right, (((1,), (1,)), ((), ())), preferred_element_type=f32)


def mm_rows(left, right):
    return lax.dot_general(left, right, (((0,), (0,)), ((), ())), preferred_element_type=f32)


DP = ("z", "core")
OVER_X = [(0, 1), (1, 0), (2, 3), (3, 2)]
OVER_Y = [(0, 2), (2, 0), (1, 3), (3, 1)]
OVER_CORE = [(0, 1), (1, 0)]


def send_x(v):
    return lax.ppermute(v, "mp", OVER_X)


def send_y(v):
    return lax.ppermute(v, "mp", OVER_Y)


def send_core(v):
    return lax.ppermute(v, "core", OVER_CORE)


def square():
    return lax.axis_size("mp") == 4


def tie(*values):
    return lax.optimization_barrier(values)


def block_orders():
    steps = jnp.arange(4, dtype=jnp.int32)
    if not square():
        return steps, steps
    me = lax.axis_index("mp").astype(jnp.int32)
    away = jnp.bitwise_xor(me, steps)
    return jnp.bitwise_xor(me, jnp.array([0, 2, 1, 3], jnp.int32)), (away % 2) * 2 + away // 2


def tile(size, most):
    while size % most:
        most //= 2
    return most


def column_product_kernel(left_ref, right_ref, out_ref):
    out_ref[...] = mm(left_ref[...], right_ref[...]).astype(out_ref.dtype)


def column_product(left, right, first, cols, dtype):
    rows, depth = left.shape
    tn = tile(cols, 256)
    return pl.pallas_call(
        column_product_kernel,
        name="column_product",
        grid=(cols // tn,),
        in_specs=[
            pl.BlockSpec((rows, depth), lambda j: (0, 0)),
            pl.BlockSpec((depth, tn), lambda j: (0, first // tn + j)),
        ],
        out_specs=pl.BlockSpec((rows, tn), lambda j: (0, j)),
        out_shape=jax.ShapeDtypeStruct((rows, cols), dtype),
        cost_estimate=pl.CostEstimate(
            flops=2 * rows * depth * cols, transcendentals=0, bytes_accessed=2 * (rows + cols) * depth + 4 * rows * cols
        ),
        compiler_params=pltpu.CompilerParams(vmem_limit_bytes=56 << 20),
    )(left, right)


def transposed_product_kernel(groups, added, left_ref, right_ref, *refs):
    outs = refs[-sum(len(g) for g in groups) :]
    steps = pl.num_programs(0) // len(groups)
    if len(left_ref.shape) == 2:
        total = mm_t(left_ref[...], right_ref[...])
    else:
        depth = left_ref.shape[2]
        total = mm_t(left_ref[0], right_ref[:, :depth]) + mm_t(left_ref[1], right_ref[:, depth:])
    if added:
        total = total + refs[0][...].astype(f32)
    size = total.shape[0] // 4
    for i, group in enumerate(groups):

        @pl.when(pl.program_id(0) // steps == i)
        def _(first=sum(len(g) for g in groups[:i]), group=group):
            for out, blocks in zip(outs[first : first + len(group)], group):
                for place, block in enumerate(blocks):
                    part = total[block * size : (block + 1) * size]
                    out[place * size : (place + 1) * size] = part.astype(out.dtype)


def transposed_product(left, sequence, rows, right, first, groups, add=None, earlier=()):
    depth = left.shape[-1]
    pair = left.ndim == 3
    deep = 2 * depth if pair else depth
    cols = right.shape[0] // len(groups)
    tn = tile(cols, 512)
    steps = cols // tn
    size = rows // 4
    adds = [] if add is None else [add]

    def at(i):
        return lambda j: (0, jnp.clip(j - i * steps, 0, steps - 1))

    return pl.pallas_call(
        functools.partial(transposed_product_kernel, groups, add is not None),
        name="transposed_product",
        grid=(len(groups) * steps,),
        in_specs=[
            pl.BlockSpec((2, rows, depth), lambda j: (0, sequence, 0))
            if pair
            else pl.BlockSpec((rows, depth), lambda j: (sequence, 0)),
            pl.BlockSpec((tn, deep), lambda j: (j, first // deep)),
        ]
        + [pl.BlockSpec((rows, tn), lambda j: (0, j))] * len(adds)
        + [pl.BlockSpec(memory_space=pl.ANY)] * len(earlier),
        out_specs=[
            pl.BlockSpec((len(blocks) * size, tn), at(i))
            for i, group in enumerate(groups)
            for blocks in group
        ],
        out_shape=[
            jax.ShapeDtypeStruct((len(blocks) * size, cols), f32 if blocks == (0,) else bf16)
            for group in groups
            for blocks in group
        ],
        cost_estimate=pl.CostEstimate(
            flops=2 * rows * deep * right.shape[0],
            transcendentals=0,
            bytes_accessed=2 * (rows + right.shape[0]) * deep + 2 * rows * right.shape[0],
        ),
        compiler_params=pltpu.CompilerParams(vmem_limit_bytes=56 << 20),
    )(left, right, *adds, *earlier)


WHOLE = (((0, 1, 2, 3),),)
PIECES = (((0,), (1,), (2, 3)), ((0,), (2,), (1, 3)))


def away_product(left, right, rows, earlier=()):
    return transposed_product(left, 1, rows, right, 0, WHOLE, earlier=earlier)[0]


def scatter_product(left, right, first, rows, add=None, earlier=()):
    groups = PIECES if square() else WHOLE
    return transposed_product(left, 0, rows, right, first, groups, add, earlier)


def scatter_near(pieces):
    if not square():
        return ()
    return send_x(pieces[2]), send_y(pieces[5])


def scatter_middle(pieces, near):
    if not square():
        return ()
    own_a, y_a, _, own_b, x_b, _ = pieces
    size = own_a.shape[0]
    return (
        (y_a.astype(f32) + near[0][size:].astype(f32)).astype(bf16),
        (x_b.astype(f32) + near[1][size:].astype(f32)).astype(bf16),
    )


def scatter_far(middle):
    if not square():
        return ()
    return send_y(middle[0]), send_x(middle[1])


def scatter_end(pieces, near, far):
    if not square():
        return lax.psum_scatter(pieces[0], "mp", scatter_dimension=0, tiled=True).astype(f32)
    size = pieces[0].shape[0]
    kept = [
        own + got[:size].astype(f32) + last.astype(f32)
        for own, got, last in zip((pieces[0], pieces[3]), near, far)
    ]
    return jnp.concatenate(kept, axis=1)


def scatter_rows(pieces):
    near = scatter_near(pieces)
    return scatter_end(pieces, near, scatter_far(scatter_middle(pieces, near)))


def assemble_kernel(order_ref, own, over_x, over_y, diag_a, diag_b, out_ref):
    half = diag_a.shape[1]
    for i, ref in enumerate([own, over_y, over_x]):

        @pl.when(pl.program_id(0) == i)
        def _(ref=ref):
            out_ref[...] = ref[...].astype(out_ref.dtype)

    @pl.when(pl.program_id(0) == 3)
    def _():
        out_ref[:, :half] = diag_a[...].astype(out_ref.dtype)
        out_ref[:, half:] = diag_b[...].astype(out_ref.dtype)


def assemble(order, pieces, dtype):
    here, width = pieces[0].shape
    return pl.pallas_call(
        assemble_kernel,
        name="assemble",
        grid_spec=pltpu.PrefetchScalarGridSpec(
            num_scalar_prefetch=1,
            grid=(4,),
            in_specs=[pl.BlockSpec((here, piece.shape[1]), lambda i, s: (0, 0)) for piece in pieces],
            out_specs=pl.BlockSpec((here, width), lambda i, s: (s[i], 0)),
        ),
        out_shape=jax.ShapeDtypeStruct((4 * here, width), dtype),
        cost_estimate=pl.CostEstimate(flops=0, transcendentals=0, bytes_accessed=20 * here * width),
        compiler_params=pltpu.CompilerParams(vmem_limit_bytes=40 << 20),
    )(order, *pieces)


def exchange_near(block):
    if not square():
        return (lax.all_gather(block, "mp", axis=0, tiled=True),)
    return send_x(block), send_y(block)


def exchange_middle(near):
    if not square():
        return ()
    half = near[0].shape[1] // 2
    return near[1][:, :half], near[0][:, half:]


def exchange_far(middle):
    if not square():
        return ()
    return send_x(middle[0]), send_y(middle[1])


def exchange_rows(block):
    near = exchange_near(block)
    return (block, *near, *exchange_far(exchange_middle(near)))


def join_rows(pieces, relative, dtype=bf16):
    if not square():
        return pieces[1].astype(dtype)
    order = jnp.arange(4, dtype=jnp.int32) if relative else block_orders()[0]
    return assemble(order, pieces, dtype)


def sum_mp(v):
    if not square():
        return lax.psum(v, "mp")
    v = v + send_x(v)
    return v + send_y(v)


def allowed_block(i, size, seq_len):
    shape = (size, (i + 1) * size)
    q_pos = i * size + lax.broadcasted_iota(jnp.int32, shape, 0)
    k_pos = lax.broadcasted_iota(jnp.int32, shape, 1)
    return (k_pos <= q_pos) & (k_pos < seq_len)


def probabilities(queries, keys, i, size, seq_len):
    factor = HEAD_SIZE ** (-0.5)
    scores = mm_t(queries, keys) * factor
    scores = jnp.where(allowed_block(i, size, seq_len), scores, neg_large)
    exps = jnp.exp(scores - jnp.max(scores, axis=-1, keepdims=True))
    return exps * (1.0 / jnp.sum(exps, axis=-1, keepdims=True))


def block_rows(order_ref, i, size):
    return pl.ds(pl.multiple_of(order_ref[i] * size, size), size)


def load_keys(order_ref, k_ref, v_ref, cos_ref, sin_ref, keys, values, size):
    for i in range(keys.shape[0] // size):
        rows = block_rows(order_ref, i, size)
        here = pl.ds(i * size, size)
        keys[here] = rotate(k_ref[rows], cos_ref[here], sin_ref[here]).astype(bf16)
        values[here] = v_ref[rows].astype(bf16)


def attention_forward_kernel(
    order_ref, len_ref, q_ref, k_ref, v_ref, cos_ref, sin_ref, out_ref, keys, values
):
    blocks = order_ref.shape[0]
    size = keys.shape[0] // blocks
    seq_len = len_ref[0]

    @pl.when(pl.program_id(0) == 0)
    def _():
        load_keys(order_ref, k_ref, v_ref, cos_ref, sin_ref, keys, values, size)

    for i in range(blocks):
        rows = block_rows(order_ref, i, size)
        here = pl.ds(i * size, size)
        upto = (i + 1) * size
        queries = rotate(q_ref[rows], cos_ref[here], sin_ref[here]).astype(bf16)
        probs = probabilities(queries, keys[:upto], i, size, seq_len).astype(bf16)
        out_ref[rows] = mm(probs, values[:upto]).astype(bf16)


def attention_backward_kernel(
    order_ref, len_ref, q_ref, k_ref, v_ref, cos_ref, sin_ref, g_ref, out_ref, keys, values, d_keys, d_values
):
    blocks = order_ref.shape[0]
    size = keys.shape[0] // blocks
    seq_len = len_ref[0]
    step = pl.program_id(0)
    heads = pl.num_programs(0) - 2
    factor = HEAD_SIZE ** (-0.5)

    @pl.when(step == 0)
    def _():
        load_keys(order_ref, k_ref, v_ref, cos_ref, sin_ref, keys, values, size)
        d_keys[...] = jnp.zeros_like(d_keys)
        d_values[...] = jnp.zeros_like(d_values)

    @pl.when(step < heads)
    def _():
        for i in range(blocks):
            rows = block_rows(order_ref, i, size)
            here = pl.ds(i * size, size)
            upto = (i + 1) * size
            cos_b, sin_b = cos_ref[here], sin_ref[here]
            queries = rotate(q_ref[rows], cos_b, sin_b).astype(bf16)
            grads = g_ref[rows]
            probs = probabilities(queries, keys[:upto], i, size, seq_len)
            d_values[:upto] += mm_rows(probs.astype(bf16), grads)
            d_probs = mm_t(grads, values[:upto])
            inner = jnp.sum(probs * d_probs, axis=-1, keepdims=True)
            d_scores = (probs * (d_probs - inner) * factor).astype(bf16)
            d_keys[:upto] += mm_rows(d_scores, queries)
            out_ref[rows] = rotate_back(mm(d_scores, keys[:upto]), cos_b, sin_b).astype(bf16)

    @pl.when(step == heads)
    def _():
        for i in range(blocks):
            here = pl.ds(i * size, size)
            out_ref[block_rows(order_ref, i, size)] = rotate_back(
                d_keys[here], cos_ref[here], sin_ref[here]
            ).astype(bf16)

    @pl.when(step == heads + 1)
    def _():
        for i in range(blocks):
            out_ref[block_rows(order_ref, i, size)] = d_values[pl.ds(i * size, size)].astype(bf16)


def attention_specs(slots, heads):
    half = HEAD_SIZE // 2
    return [
        pl.BlockSpec((slots, HEAD_SIZE), lambda h, o, n: (0, jnp.minimum(h, heads - 1))),
        pl.BlockSpec((slots, HEAD_SIZE), lambda h, o, n: (0, heads)),
        pl.BlockSpec((slots, HEAD_SIZE), lambda h, o, n: (0, heads + 1)),
        pl.BlockSpec((slots, half), lambda h, o, n: (0, 0)),
        pl.BlockSpec((slots, half), lambda h, o, n: (0, 0)),
    ]


def attention_forward(order, length, qkv, tables):
    slots = qkv.shape[0]
    heads = qkv.shape[1] // HEAD_SIZE - 2
    return pl.pallas_call(
        attention_forward_kernel,
        name="attention_forward",
        grid_spec=pltpu.PrefetchScalarGridSpec(
            num_scalar_prefetch=2,
            grid=(heads,),
            in_specs=attention_specs(slots, heads),
            out_specs=pl.BlockSpec((slots, HEAD_SIZE), lambda h, o, n: (0, h)),
            scratch_shapes=[pltpu.VMEM((slots, HEAD_SIZE), bf16)] * 2,
        ),
        out_shape=jax.ShapeDtypeStruct((slots, heads * HEAD_SIZE), bf16),
        cost_estimate=pl.CostEstimate(
            flops=3 * heads * slots * slots * HEAD_SIZE,
            transcendentals=heads * slots * slots,
            bytes_accessed=8 * slots * HEAD_SIZE * (heads + 2),
        ),
        compiler_params=pltpu.CompilerParams(vmem_limit_bytes=56 << 20),
    )(order, length, qkv, qkv, qkv, *tables)


def attention_backward(order, length, qkv, tables, d_context):
    slots = qkv.shape[0]
    heads = qkv.shape[1] // HEAD_SIZE - 2
    return pl.pallas_call(
        attention_backward_kernel,
        name="attention_backward",
        grid_spec=pltpu.PrefetchScalarGridSpec(
            num_scalar_prefetch=2,
            grid=(heads + 2,),
            in_specs=attention_specs(slots, heads)
            + [pl.BlockSpec((slots, HEAD_SIZE), lambda h, o, n: (0, jnp.minimum(h, heads - 1)))],
            out_specs=pl.BlockSpec((slots, HEAD_SIZE), lambda h, o, n: (0, h)),
            scratch_shapes=[pltpu.VMEM((slots, HEAD_SIZE), bf16)] * 2
            + [pltpu.VMEM((slots, HEAD_SIZE), f32)] * 2,
        ),
        out_shape=jax.ShapeDtypeStruct((slots, (heads + 2) * HEAD_SIZE), bf16),
        cost_estimate=pl.CostEstimate(
            flops=7 * heads * slots * slots * HEAD_SIZE,
            transcendentals=heads * slots * slots,
            bytes_accessed=8 * slots * HEAD_SIZE * (heads + 2),
        ),
        compiler_params=pltpu.CompilerParams(vmem_limit_bytes=56 << 20),
    )(order, length, qkv, qkv, qkv, *tables, d_context)


def attention_products_kernel(g1_ref, context_ref, h_ref, d_qkv_ref, *refs):
    out_ref = refs[-1]
    cols = context_ref.shape[1]
    out_ref[:, :cols] = mm_rows(g1_ref[...], context_ref[...]).astype(bf16)
    out_ref[:, cols:] = mm_rows(h_ref[...], d_qkv_ref[...]).astype(bf16)


def attention_products(g1, context, h, d_qkv, *earlier):
    rows, width = g1.shape
    cols, more = context.shape[1], d_qkv.shape[1]
    tm = tile(width, 512)
    return pl.pallas_call(
        attention_products_kernel,
        name="attention_products",
        grid=(width // tm,),
        in_specs=[
            pl.BlockSpec((rows, tm), lambda i: (0, i)),
            pl.BlockSpec((rows, cols), lambda i: (0, 0)),
            pl.BlockSpec((rows, tm), lambda i: (0, i)),
            pl.BlockSpec((rows, more), lambda i: (0, 0)),
        ]
        + [pl.BlockSpec(memory_space=pl.ANY)] * len(earlier),
        out_specs=pl.BlockSpec((tm, cols + more), lambda i: (i, 0)),
        out_shape=jax.ShapeDtypeStruct((width, cols + more), bf16),
        cost_estimate=pl.CostEstimate(
            flops=2 * rows * width * (cols + more),
            transcendentals=0,
            bytes_accessed=4 * rows * width + 2 * (rows + width) * (cols + more),
        ),
        compiler_params=pltpu.CompilerParams(vmem_limit_bytes=56 << 20),
    )(g1, context, h, d_qkv, *earlier)


def prepare_kernel(order_ref, len_ref, x_ref, grad_ref, x_out, grad_out):
    size = x_ref.shape[0]
    first = order_ref[pl.program_id(0)] * size
    pos = first + lax.broadcasted_iota(jnp.int32, (size, 1), 0)
    x_out[...] = x_ref[...]
    grad_out[...] = jnp.where(pos < len_ref[0], grad_ref[...].astype(f32), 0.0).astype(bf16)


def prepare(order, length, x_in, cotangent):
    slots, width = x_in.shape
    size = slots // 4
    source = pl.BlockSpec((size, width), lambda i, o, n: (o[i], 0))
    target = pl.BlockSpec((size, width), lambda i, o, n: (i, 0))
    return pl.pallas_call(
        prepare_kernel,
        name="prepare",
        grid_spec=pltpu.PrefetchScalarGridSpec(
            num_scalar_prefetch=2, grid=(4,), in_specs=[source] * 2, out_specs=[target] * 2
        ),
        out_shape=[jax.ShapeDtypeStruct(x_in.shape, bf16)] * 2,
        cost_estimate=pl.CostEstimate(flops=0, transcendentals=0, bytes_accessed=8 * slots * width),
        compiler_params=pltpu.CompilerParams(vmem_limit_bytes=40 << 20),
    )(order, length, x_in, cotangent)


def spread_heads(block):
    mp_size = lax.axis_size("mp")
    rows, n, heads, part = block.shape
    send = jnp.repeat(block, mp_size // heads, axis=2)
    got = lax.all_to_all(send, "mp", 2, 2, tiled=True)
    return got.reshape(rows, n * mp_size * part)


def collect_heads(block, heads):
    mp_size = lax.axis_size("mp")
    rows, n, size = block.shape
    part = size // mp_size
    got = lax.all_to_all(block.reshape(rows, n, mp_size, part), "mp", 2, 2, tiled=True)
    return jnp.sum(got.reshape(rows, n, heads, mp_size // heads, part).astype(f32), axis=3)


def gather_dp(block):
    return lax.all_gather(block, DP, axis=0, tiled=True)


def reduce_dp(block):
    return lax.psum_scatter(block, DP, scatter_dimension=0, tiled=True)


def gather_z(block):
    return lax.all_gather(block, "z", axis=0, tiled=True)


def reduce_z(block):
    return lax.psum_scatter(block, "z", scatter_dimension=0, tiled=True)


def to_core(block):
    rows, n, cols = block.shape
    core = lax.axis_index("core")
    m = cols // 2
    own = lax.dynamic_slice_in_dim(block, core * m, m, 2).reshape(rows, n * m)
    away = lax.dynamic_slice_in_dim(block, (1 - core) * m, m, 2).reshape(rows, n * m)
    got = send_core(away)
    return jnp.concatenate([jnp.where(core == 0, own, got), jnp.where(core == 0, got, own)])


def own_half_kernel(transpose, core_ref, own_ref, got_ref, *refs):
    out_ref = refs[-1]
    value = jnp.where(pl.program_id(0) == core_ref[0], own_ref[...].astype(f32), got_ref[...].astype(f32))
    out_ref[...] = value.T if transpose else value


def from_core(block, n, transpose=False, earlier=()):
    rows = block.shape[0] // 2
    m = block.shape[1] // n
    core = lax.axis_index("core").astype(jnp.int32)
    got = send_core(lax.dynamic_slice_in_dim(block, (1 - core) * rows, rows, 0))
    out_block = (m, rows) if transpose else (rows, m)
    out_shape = (2 * m, rows) if transpose else (rows, 2 * m)
    return [
        pl.pallas_call(
            functools.partial(own_half_kernel, transpose),
            name="own_half",
            grid_spec=pltpu.PrefetchScalarGridSpec(
                num_scalar_prefetch=1,
                grid=(2,),
                in_specs=[
                    pl.BlockSpec((rows, m), lambda h, c, i=i: (c[0], i)),
                    pl.BlockSpec((rows, m), lambda h, c, i=i: (0, i)),
                ]
                + [pl.BlockSpec(memory_space=pl.ANY)] * len(earlier),
                out_specs=pl.BlockSpec(out_block, lambda h, c: (h, 0) if transpose else (0, h)),
            ),
            out_shape=jax.ShapeDtypeStruct(out_shape, f32),
            cost_estimate=pl.CostEstimate(flops=0, transcendentals=0, bytes_accessed=12 * rows * m),
            compiler_params=pltpu.CompilerParams(vmem_limit_bytes=40 << 20),
        )(core.reshape(1), block, got, *earlier)
        for i in range(n)
    ]


def ffn_forward_kernel(mine_ref, away_ref, g_ref, u_ref, hidden_ref, factor_ref):
    def run(h_ref):
        h = h_ref[...]
        gate = jnp.dot(h, g_ref[...], preferred_element_type=f32)
        up = jnp.dot(h, u_ref[...], preferred_element_type=f32)
        sig = 1.0 / (1.0 + jnp.exp(-gate))
        silu = gate * sig
        hidden_ref[...] = (silu * up).astype(bf16)
        factor_ref[0] = (up * sig * (1.0 + gate - silu)).astype(bf16)
        factor_ref[1] = silu.astype(bf16)

    pl.when(pl.program_id(0) == 0)(lambda: run(mine_ref))
    pl.when(pl.program_id(0) == 1)(lambda: run(away_ref))


def ffn_forward(mine, away, w_gu):
    rows, width = mine.shape
    ff = w_gu.shape[1] // 2
    tn = tile(ff, 256)
    return pl.pallas_call(
        ffn_forward_kernel,
        name="ffn_forward",
        grid=(2, ff // tn),
        in_specs=[
            pl.BlockSpec((rows, width), lambda i, j: (0, 0)),
            pl.BlockSpec((rows, width), lambda i, j: (0, 0)),
            pl.BlockSpec((width, tn), lambda i, j: (0, j)),
            pl.BlockSpec((width, tn), lambda i, j: (0, j + ff // tn)),
        ],
        out_specs=[
            pl.BlockSpec((rows, tn), lambda i, j: (i, j)),
            pl.BlockSpec((2, rows, tn), lambda i, j: (0, i, j)),
        ],
        out_shape=[
            jax.ShapeDtypeStruct((2 * rows, ff), bf16),
            jax.ShapeDtypeStruct((2, 2 * rows, ff), bf16),
        ],
        cost_estimate=pl.CostEstimate(
            flops=8 * rows * width * ff,
            transcendentals=2 * rows * ff,
            bytes_accessed=4 * (rows * width + width * ff + 3 * rows * ff),
        ),
        compiler_params=pltpu.CompilerParams(vmem_limit_bytes=56 << 20),
    )(mine, away, w_gu, w_gu)


def rows_product_kernel(mine_ref, away_ref, right_mine_ref, right_away_ref, *refs):
    out_ref = refs[-1]
    cols = right_mine_ref.shape[2]
    for i in range(2):
        out_ref[:, i * cols : (i + 1) * cols] = (
            mm_rows(mine_ref[...], right_mine_ref[i]) + mm_rows(away_ref[...], right_away_ref[i])
        ).astype(bf16)


def rows_product(mine, away, right, part, parts, into=None, earlier=()):
    rows, width = mine.shape
    cols = 2 * right.shape[2]
    tm = tile(width // parts, 256)
    steps = width // parts // tm
    more = ([] if into is None else [into]) + list(earlier)
    return pl.pallas_call(
        rows_product_kernel,
        name="rows_product",
        grid=(steps,),
        in_specs=[
            pl.BlockSpec((rows, tm), lambda i: (0, part * steps + i)),
            pl.BlockSpec((rows, tm), lambda i: (0, part * steps + i)),
            pl.BlockSpec((2, rows, cols // 2), lambda i: (0, 0, 0)),
            pl.BlockSpec((2, rows, cols // 2), lambda i: (0, 1, 0)),
        ]
        + [pl.BlockSpec(memory_space=pl.ANY)] * len(more),
        out_specs=pl.BlockSpec((tm, cols), lambda i: (part * steps + i, 0)),
        out_shape=jax.ShapeDtypeStruct((width, cols), bf16),
        input_output_aliases={} if into is None else {4: 0},
        cost_estimate=pl.CostEstimate(
            flops=4 * rows * width * cols // parts,
            transcendentals=0,
            bytes_accessed=(4 * rows * width + 2 * width * cols) // parts + 4 * rows * cols,
        ),
        compiler_params=pltpu.CompilerParams(vmem_limit_bytes=56 << 20),
    )(mine, away, right, right, *more)


def ffn_backward_kernel(grad_ref, d_ref, factor_ref, earlier_ref, out_ref):
    d_hidden = mm(grad_ref[...], d_ref[...])
    for i in range(2):
        out_ref[i] = (d_hidden * factor_ref[i].astype(f32)).astype(bf16)


def ffn_backward(grad, w_d, factors, earlier):
    rows, width = grad.shape
    ff = w_d.shape[1]
    tm, tn = tile(rows, 1024), tile(ff, 256)
    return pl.pallas_call(
        ffn_backward_kernel,
        name="ffn_backward",
        grid=(rows // tm, ff // tn),
        in_specs=[
            pl.BlockSpec((tm, width), lambda i, j: (i, 0)),
            pl.BlockSpec((width, tn), lambda i, j: (0, j)),
            pl.BlockSpec((2, tm, tn), lambda i, j: (0, i, j)),
            pl.BlockSpec(memory_space=pl.ANY),
        ],
        out_specs=pl.BlockSpec((2, tm, tn), lambda i, j: (0, i, j)),
        out_shape=jax.ShapeDtypeStruct((2, rows, ff), bf16),
        cost_estimate=pl.CostEstimate(
            flops=2 * rows * width * ff, transcendentals=0, bytes_accessed=2 * (rows * width + width * ff + 4 * rows * ff)
        ),
        compiler_params=pltpu.CompilerParams(vmem_limit_bytes=56 << 20),
    )(grad, w_d, factors, earlier)


def local(
    x_in,
    lengths,
    gain_attn,
    query_weight,
    key_projection_matrix,
    value_projection_matrix,
    out_weight,
    gain_ffn,
    gate_weight,
    up_weight,
    down_weight,
    cotangent,
):
    _, slots, width = x_in.shape
    mp_size = lax.axis_size("mp")
    me = lax.axis_index("mp")
    q_cols = query_weight.shape[1]
    here = slots // mp_size
    quarter = slots // 4
    tables = rope_tables(slots, HEAD_SIZE)
    sequence_block, relative_place = block_orders()

    def own_rows(v):
        return v[:here] if square() else lax.dynamic_slice_in_dim(v, me * here, here, 0)

    x_rel, grad_mine = prepare(sequence_block, lengths, x_in[0], cotangent[0])
    kv_block = spread_heads(jnp.stack([key_projection_matrix, value_projection_matrix], axis=1))
    w_attn = gather_dp(jnp.concatenate([query_weight, kv_block, out_weight.T], axis=1))
    o_first = q_cols + 2 * HEAD_SIZE
    ffn_block = to_core(jnp.stack([gate_weight, up_weight, down_weight.T], axis=1))
    ff = ffn_block.shape[1] // 3
    w_gu = gather_z(ffn_block[:, : 2 * ff])
    w_d = gather_z(ffn_block[:, 2 * ff :])
    gains = lax.all_gather(jnp.stack([gain_attn, gain_ffn]), DP, axis=1, tiled=True).astype(f32)
    g_attn, g_ffn = gains[0], gains[1]

    tok = x_rel.astype(f32)
    r1 = lax.rsqrt(jnp.mean(tok * tok, axis=-1, keepdims=True) + eps_norm)
    h_attn = (tok * r1 * g_attn).astype(bf16)
    grad_all = jnp.concatenate([grad_mine, send_core(grad_mine)])
    qkv = column_product(h_attn, w_attn, 0, o_first, f32)
    context = attention_forward(relative_place, lengths, qkv, tables)

    attn_rows = scatter_rows(scatter_product(context, w_attn, o_first, slots))
    tok_here = own_rows(x_rel).astype(f32)
    mid = tok_here + attn_rows
    r2 = lax.rsqrt(jnp.mean(mid * mid, axis=-1, keepdims=True) + eps_norm)
    n2 = mid * r2
    h_mine = join_rows(exchange_rows((n2 * g_ffn).astype(bf16)), True)
    h_away = send_core(h_mine)

    hidden, factors = ffn_forward(h_mine, h_away, w_gu)
    down_grad = mm_rows(grad_all, hidden).astype(bf16)
    down_out = reduce_z(down_grad)

    ffn_away = away_product(hidden, w_d, slots, (down_grad,))
    ffn_add = send_core(ffn_away)
    d_gu = ffn_backward(grad_all, w_d, factors, ffn_away)
    gu_grad = rows_product(h_mine, h_away, d_gu, 0, 1, earlier=(d_gu,))
    gu_out = reduce_z(gu_grad)
    ffn_pieces = scatter_product(hidden, w_d, 0, slots, ffn_add, (gu_grad,))
    ffn_near = scatter_near(ffn_pieces)
    h2_away = away_product(d_gu, w_gu, slots, (ffn_pieces[-1],))
    h2_add = send_core(h2_away)
    ffn_middle = scatter_middle(ffn_pieces, ffn_near)
    ffn_far = scatter_far(ffn_middle)
    h2_pieces = scatter_product(d_gu, w_gu, 0, slots, h2_add)
    h2_pieces, ffn_far = tie(h2_pieces, ffn_far)
    ffn_rows = scatter_end(ffn_pieces, ffn_near, ffn_far)
    d_h2 = scatter_rows(h2_pieces)

    e2 = d_h2 * g_ffn
    g1 = own_rows(grad_mine).astype(f32) + r2 * (e2 - n2 * jnp.mean(e2 * n2, axis=-1, keepdims=True))
    g1_low = join_rows(exchange_rows(g1.astype(bf16)), True)

    layer_block, g1_low = tie((mid + ffn_rows).astype(bf16), g1_low)
    layer_near = exchange_near(layer_block)
    d_context = column_product(g1_low, w_attn, o_first, q_cols, bf16)
    d_qkv = attention_backward(relative_place, lengths, qkv, tables, d_context)
    layer_middle = exchange_middle(layer_near)
    attn_grads = attention_products(g1_low, context, h_attn, d_qkv, *layer_middle)
    attn_out = reduce_dp(attn_grads)
    layer_far = exchange_far(layer_middle)
    h1_pieces = scatter_product(d_qkv, w_attn, 0, slots, earlier=(attn_grads,))
    h1_pieces, layer_far = tie(h1_pieces, layer_far)
    layer_out = join_rows((layer_block, *layer_near, *layer_far), False)
    d_h1 = scatter_rows(h1_pieces)
    r1_here = own_rows(r1)
    n1 = tok_here * r1_here
    e1 = d_h1 * g_attn
    grad_in = g1 + r1_here * (e1 - n1 * jnp.mean(e1 * n1, axis=-1, keepdims=True))
    grad_pieces = exchange_rows(grad_in.astype(bf16))

    rows_here = gain_attn.shape[0]

    (down_out,) = from_core(down_out, 1, True)
    gate_out, up_out = from_core(gu_out, 2, earlier=(down_out,))
    out_out, q_out = attn_out[:, :q_cols], attn_out[:, q_cols : 2 * q_cols].astype(f32)
    kv_out = attn_out[:, 2 * q_cols :]
    kv_grad = collect_heads(kv_out.reshape(rows_here, 2, HEAD_SIZE), KEY_VALUE_HEADS)

    def row_sums(*pairs):
        return sum(jnp.sum(w.astype(f32) * g.astype(f32), axis=1) for w, g in pairs)

    gain_sums = sum_mp(
        jnp.stack(
            [
                row_sums((query_weight, q_out), (kv_block, kv_out)),
                row_sums((gate_weight, gate_out), (up_weight, up_out)),
            ]
        )
    )
    gain_attn_grad = gain_sums[0] / gain_attn.astype(f32)
    gain_ffn_grad = gain_sums[1] / gain_ffn.astype(f32)
    grad_pieces, kv_grad, down_out, gate_out, up_out = tie(
        grad_pieces, kv_grad, down_out, gate_out, up_out
    )
    grad_input = join_rows(grad_pieces, False, f32)
    return (
        layer_out[None],
        grad_input[None],
        gain_attn_grad,
        q_out,
        kv_grad[:, 0],
        kv_grad[:, 1],
        out_out.T.astype(f32),
        gain_ffn_grad,
        gate_out,
        up_out,
        down_out,
    )


def solution(mesh):
    dp_size, mp_size = mesh.shape["dp"], mesh.shape["mp"]
    split = Mesh(mesh.devices.reshape(dp_size // 2, 2, mp_size), ("z", "core", "mp"))
    return jax.shard_map(
        local,
        mesh=split,
        in_specs=(
            P(DP, None, None),
            P(DP),
            P(DP),
            P(DP, "mp"),
            P(DP, None, "mp"),
            P(DP, None, "mp"),
            P("mp", DP),
            P(DP),
            P(DP, "mp"),
            P(DP, "mp"),
            P("mp", DP),
            P(DP, None, None),
        ),
        out_specs=(
            P(DP, None, None),
            P(DP, None, None),
            P(DP),
            P(DP, "mp"),
            P(DP, None, "mp"),
            P(DP, None, "mp"),
            P("mp", DP),
            P(DP),
            P(DP, "mp"),
            P(DP, "mp"),
            P("mp", DP),
        ),
        check_vma=False,
    )
```

```python
import functools

import jax
import jax.numpy as jnp
from jax import lax
from jax.experimental import pallas as pl
from jax.experimental.pallas import tpu as pltpu
from jax.sharding import Mesh, PartitionSpec as P

QUERY_HEADS = 8
KEY_VALUE_HEADS = 4
HEAD_SIZE = 256

eps_norm = 1e-06
rope_base = 1000042.0
neg_large = -1e30
bf16 = jnp.bfloat16
f32 = jnp.float32


def rope_tables(slot_length, size):
    half_size = size // 2
    inv_freq = rope_base ** (-(jnp.arange(half_size, dtype=f32) * 2.0 / size))
    angles = jnp.arange(slot_length, dtype=f32)[:, None] * inv_freq[None, :]
    return (jnp.cos(angles), jnp.sin(angles))


def rotate(values, cos_b, sin_b):
    half = values.shape[-1] // 2
    a, b = values[..., :half], values[..., half:]
    return jnp.concatenate([a * cos_b - b * sin_b, b * cos_b + a * sin_b], axis=-1)


def rotate_back(grads, cos_b, sin_b):
    half = grads.shape[-1] // 2
    a, b = grads[..., :half], grads[..., half:]
    return jnp.concatenate([a * cos_b + b * sin_b, b * cos_b - a * sin_b], axis=-1)


def mm(left, right):
    return lax.dot_general(left, right, (((1,), (0,)), ((), ())), preferred_element_type=f32)


def mm_t(left, right):
    return lax.dot_general(left, right, (((1,), (1,)), ((), ())), preferred_element_type=f32)


def mm_rows(left, right):
    return lax.dot_general(left, right, (((0,), (0,)), ((), ())), preferred_element_type=f32)


DP = ("z", "core")
OVER_X = [(0, 1), (1, 0), (2, 3), (3, 2)]
OVER_Y = [(0, 2), (2, 0), (1, 3), (3, 1)]
OVER_CORE = [(0, 1), (1, 0)]


def send_x(v):
    return lax.ppermute(v, "mp", OVER_X)


def send_y(v):
    return lax.ppermute(v, "mp", OVER_Y)


def send_core(v):
    return lax.ppermute(v, "core", OVER_CORE)


def square():
    return lax.axis_size("mp") == 4


def tie(*values):
    return lax.optimization_barrier(values)


def block_orders():
    steps = jnp.arange(4, dtype=jnp.int32)
    if not square():
        return steps, steps
    me = lax.axis_index("mp").astype(jnp.int32)
    away = jnp.bitwise_xor(me, steps)
    return jnp.bitwise_xor(me, jnp.array([0, 2, 1, 3], jnp.int32)), (away % 2) * 2 + away // 2


def tile(size, most):
    while size % most:
        most //= 2
    return most


def column_product_kernel(left_ref, right_ref, out_ref):
    out_ref[...] = mm(left_ref[...], right_ref[...]).astype(out_ref.dtype)


def column_product(left, right, first, cols, dtype):
    rows, depth = left.shape
    tn = tile(cols, 256)
    return pl.pallas_call(
        column_product_kernel,
        name="column_product",
        grid=(cols // tn,),
        in_specs=[
            pl.BlockSpec((rows, depth), lambda j: (0, 0)),
            pl.BlockSpec((depth, tn), lambda j: (0, first // tn + j)),
        ],
        out_specs=pl.BlockSpec((rows, tn), lambda j: (0, j)),
        out_shape=jax.ShapeDtypeStruct((rows, cols), dtype),
        cost_estimate=pl.CostEstimate(
            flops=2 * rows * depth * cols, transcendentals=0, bytes_accessed=2 * (rows + cols) * depth + 4 * rows * cols
        ),
        compiler_params=pltpu.CompilerParams(vmem_limit_bytes=56 << 20),
    )(left, right)


def transposed_product_kernel(groups, added, left_ref, right_ref, *refs):
    outs = refs[-sum(len(g) for g in groups) :]
    steps = pl.num_programs(0) // len(groups)
    if len(left_ref.shape) == 2:
        total = mm_t(left_ref[...], right_ref[...])
    else:
        depth = left_ref.shape[2]
        total = mm_t(left_ref[0], right_ref[:, :depth]) + mm_t(left_ref[1], right_ref[:, depth:])
    if added:
        total = total + refs[0][...].astype(f32)
    size = total.shape[0] // 4
    for i, group in enumerate(groups):

        @pl.when(pl.program_id(0) // steps == i)
        def _(first=sum(len(g) for g in groups[:i]), group=group):
            for out, blocks in zip(outs[first : first + len(group)], group):
                for place, block in enumerate(blocks):
                    part = total[block * size : (block + 1) * size]
                    out[place * size : (place + 1) * size] = part.astype(out.dtype)


def transposed_product(left, sequence, rows, right, first, groups, add=None, earlier=()):
    depth = left.shape[-1]
    pair = left.ndim == 3
    deep = 2 * depth if pair else depth
    cols = right.shape[0] // len(groups)
    tn = tile(cols, 512)
    steps = cols // tn
    size = rows // 4
    adds = [] if add is None else [add]

    def at(i):
        return lambda j: (0, jnp.clip(j - i * steps, 0, steps - 1))

    return pl.pallas_call(
        functools.partial(transposed_product_kernel, groups, add is not None),
        name="transposed_product",
        grid=(len(groups) * steps,),
        in_specs=[
            pl.BlockSpec((2, rows, depth), lambda j: (0, sequence, 0))
            if pair
            else pl.BlockSpec((rows, depth), lambda j: (sequence, 0)),
            pl.BlockSpec((tn, deep), lambda j: (j, first // deep)),
        ]
        + [pl.BlockSpec((rows, tn), lambda j: (0, j))] * len(adds)
        + [pl.BlockSpec(memory_space=pl.ANY)] * len(earlier),
        out_specs=[
            pl.BlockSpec((len(blocks) * size, tn), at(i))
            for i, group in enumerate(groups)
            for blocks in group
        ],
        out_shape=[
            jax.ShapeDtypeStruct((len(blocks) * size, cols), f32 if blocks == (0,) else bf16)
            for group in groups
            for blocks in group
        ],
        cost_estimate=pl.CostEstimate(
            flops=2 * rows * deep * right.shape[0],
            transcendentals=0,
            bytes_accessed=2 * (rows + right.shape[0]) * deep + 2 * rows * right.shape[0],
        ),
        compiler_params=pltpu.CompilerParams(vmem_limit_bytes=56 << 20),
    )(left, right, *adds, *earlier)


WHOLE = (((0, 1, 2, 3),),)
PIECES = (((0,), (1,), (2, 3)), ((0,), (2,), (1, 3)))


def away_product(left, right, rows, earlier=()):
    return transposed_product(left, 1, rows, right, 0, WHOLE, earlier=earlier)[0]


def scatter_product(left, right, first, rows, add=None, earlier=()):
    groups = PIECES if square() else WHOLE
    return transposed_product(left, 0, rows, right, first, groups, add, earlier)


def add_away(pieces, away):
    if not square():
        return [(pieces[0].astype(f32) + away.astype(f32)).astype(bf16)]
    size, half = pieces[1].shape
    away = away.reshape(2, 2, size, 2 * half)
    parts = [
        away[0, 0, :, :half],
        away[0, 1, :, :half],
        away[1, :, :, :half].reshape(2 * size, half),
        away[0, 0, :, half:],
        away[1, 0, :, half:],
        away[:, 1, :, half:].reshape(2 * size, half),
    ]
    return [
        (piece.astype(f32) + part.astype(f32)).astype(piece.dtype) for piece, part in zip(pieces, parts)
    ]


def scatter_near(pieces):
    if not square():
        return ()
    return send_x(pieces[2]), send_y(pieces[5])


def scatter_middle(pieces, near):
    if not square():
        return ()
    own_a, y_a, _, own_b, x_b, _ = pieces
    size = own_a.shape[0]
    return (
        (y_a.astype(f32) + near[0][size:].astype(f32)).astype(bf16),
        (x_b.astype(f32) + near[1][size:].astype(f32)).astype(bf16),
    )


def scatter_far(middle):
    if not square():
        return ()
    return send_y(middle[0]), send_x(middle[1])


def scatter_end(pieces, near, far):
    if not square():
        return lax.psum_scatter(pieces[0], "mp", scatter_dimension=0, tiled=True).astype(f32)
    size = pieces[0].shape[0]
    kept = [
        own + got[:size].astype(f32) + last.astype(f32)
        for own, got, last in zip((pieces[0], pieces[3]), near, far)
    ]
    return jnp.concatenate(kept, axis=1)


def scatter_rows(pieces):
    near = scatter_near(pieces)
    return scatter_end(pieces, near, scatter_far(scatter_middle(pieces, near)))


def rows_backward_kernel(added, *refs):
    own, got, last = refs[0:2], refs[2:4], refs[4:6]
    v_ref, base_ref, gain_ref = refs[6 + added : 9 + added]
    g_ref, low_ref = refs[9 + added :]
    half = own[0].shape[1]
    width = 2 * half
    v = v_ref[...].astype(f32)
    r = lax.rsqrt(jnp.sum(v * v, axis=-1, keepdims=True) * (1.0 / width) + eps_norm)
    n = v * r
    parts = []
    for i in range(2):
        columns = slice(i * half, (i + 1) * half)
        d = own[i][...] + got[i][...].astype(f32) + last[i][...].astype(f32)
        if added:
            d = d + refs[6][:, columns].astype(f32)
        parts.append(d * gain_ref[:, columns])
    e = jnp.concatenate(parts, axis=1)
    inner = jnp.sum(e * n, axis=-1, keepdims=True) * (1.0 / width)
    g = base_ref[...].astype(f32) + r * (e - n * inner)
    g_ref[...] = g
    low_ref[...] = g.astype(bf16)


def rows_backward(pieces, near, far, away, v, base, gain):
    if not square():
        here = pieces[0].shape[0] // lax.axis_size("mp")
        d = scatter_end(pieces, near, far)

        def own(u):
            if u.shape[0] == here:
                return u
            return lax.dynamic_slice_in_dim(u, lax.axis_index("mp") * here, here, 0)

        v, base = own(v).astype(f32), own(base).astype(f32)
        r = lax.rsqrt(jnp.mean(v * v, axis=-1, keepdims=True) + eps_norm)
        n, e = v * r, d * gain
        g = base + r * (e - n * jnp.mean(e * n, axis=-1, keepdims=True))
        return g, g.astype(bf16)
    here, half = pieces[0].shape
    tm = tile(here, 64)
    narrow = pl.BlockSpec((tm, half), lambda i: (i, 0))
    wide = pl.BlockSpec((tm, 2 * half), lambda i: (i, 0))
    adds = [] if away is None else [away]
    return pl.pallas_call(
        functools.partial(rows_backward_kernel, len(adds)),
        name="rows_backward",
        grid=(here // tm,),
        in_specs=[narrow] * 6
        + [wide] * (len(adds) + 2)
        + [pl.BlockSpec((1, 2 * half), lambda i: (0, 0))],
        out_specs=[wide, wide],
        out_shape=[
            jax.ShapeDtypeStruct((here, 2 * half), f32),
            jax.ShapeDtypeStruct((here, 2 * half), bf16),
        ],
        cost_estimate=pl.CostEstimate(
            flops=40 * here * half, transcendentals=here, bytes_accessed=40 * here * half
        ),
        compiler_params=pltpu.CompilerParams(vmem_limit_bytes=40 << 20),
    )(pieces[0], pieces[3], *near, *far, *adds, v, base, gain.reshape(1, -1))


def assemble_kernel(order_ref, own, over_x, over_y, diag_a, diag_b, out_ref):
    half = diag_a.shape[1]
    for i, ref in enumerate([own, over_y, over_x]):

        @pl.when(pl.program_id(0) == i)
        def _(ref=ref):
            out_ref[...] = ref[...].astype(out_ref.dtype)

    @pl.when(pl.program_id(0) == 3)
    def _():
        out_ref[:, :half] = diag_a[...].astype(out_ref.dtype)
        out_ref[:, half:] = diag_b[...].astype(out_ref.dtype)


def assemble(order, pieces, dtype):
    here, width = pieces[0].shape
    return pl.pallas_call(
        assemble_kernel,
        name="assemble",
        grid_spec=pltpu.PrefetchScalarGridSpec(
            num_scalar_prefetch=1,
            grid=(4,),
            in_specs=[pl.BlockSpec((here, piece.shape[1]), lambda i, s: (0, 0)) for piece in pieces],
            out_specs=pl.BlockSpec((here, width), lambda i, s: (s[i], 0)),
        ),
        out_shape=jax.ShapeDtypeStruct((4 * here, width), dtype),
        cost_estimate=pl.CostEstimate(flops=0, transcendentals=0, bytes_accessed=20 * here * width),
        compiler_params=pltpu.CompilerParams(vmem_limit_bytes=40 << 20),
    )(order, *pieces)


def join_near_kernel(order_ref, own, over_x, over_y, out_ref):
    for i, ref in enumerate([own, over_y, over_x]):

        @pl.when(pl.program_id(0) == i)
        def _(ref=ref):
            out_ref[...] = ref[...].astype(out_ref.dtype)


def join_far_kernel(order_ref, diag_a, diag_b, near_ref, out_ref):
    half = diag_a.shape[1]
    out_ref[:, :half] = diag_a[...].astype(out_ref.dtype)
    out_ref[:, half:] = diag_b[...].astype(out_ref.dtype)


def join_near(pieces, dtype):
    here, width = pieces[0].shape
    return pl.pallas_call(
        join_near_kernel,
        name="join_near",
        grid_spec=pltpu.PrefetchScalarGridSpec(
            num_scalar_prefetch=1,
            grid=(3,),
            in_specs=[pl.BlockSpec((here, width), lambda i, s: (0, 0))] * 3,
            out_specs=pl.BlockSpec((here, width), lambda i, s: (s[i], 0)),
        ),
        out_shape=jax.ShapeDtypeStruct((4 * here, width), dtype),
        cost_estimate=pl.CostEstimate(flops=0, transcendentals=0, bytes_accessed=18 * here * width),
        compiler_params=pltpu.CompilerParams(vmem_limit_bytes=40 << 20),
    )(block_orders()[0], *pieces)


def join_far(pieces, near):
    here, half = pieces[0].shape
    return pl.pallas_call(
        join_far_kernel,
        name="join_far",
        grid_spec=pltpu.PrefetchScalarGridSpec(
            num_scalar_prefetch=1,
            grid=(1,),
            in_specs=[pl.BlockSpec((here, half), lambda i, s: (0, 0))] * 2
            + [pl.BlockSpec(memory_space=pl.ANY)],
            out_specs=pl.BlockSpec((here, 2 * half), lambda i, s: (s[3], 0)),
        ),
        out_shape=jax.ShapeDtypeStruct(near.shape, near.dtype),
        input_output_aliases={3: 0},
        cost_estimate=pl.CostEstimate(flops=0, transcendentals=0, bytes_accessed=12 * here * half),
        compiler_params=pltpu.CompilerParams(vmem_limit_bytes=40 << 20),
    )(block_orders()[0], *pieces, near)


def exchange_near(block):
    if not square():
        return (lax.all_gather(block, "mp", axis=0, tiled=True),)
    return send_x(block), send_y(block)


def exchange_middle(near):
    if not square():
        return ()
    half = near[0].shape[1] // 2
    return near[1][:, :half], near[0][:, half:]


def exchange_far(middle):
    if not square():
        return ()
    return send_x(middle[0]), send_y(middle[1])


def exchange_rows(block):
    near = exchange_near(block)
    return (block, *near, *exchange_far(exchange_middle(near)))


def join_rows(pieces, relative, dtype=bf16):
    if not square():
        return pieces[1].astype(dtype)
    order = jnp.arange(4, dtype=jnp.int32) if relative else block_orders()[0]
    return assemble(order, pieces, dtype)


SHORTEST = 512
FACTOR = HEAD_SIZE ** (-0.5)


def probabilities(queries, keys, i, size, seq_len):
    scores = mm_t(queries, keys)
    first = min(i * size, SHORTEST)
    shape = (size, (i + 1) * size - first)
    q_pos = i * size + lax.broadcasted_iota(jnp.int32, shape, 0)
    k_pos = first + lax.broadcasted_iota(jnp.int32, shape, 1)
    seen = jnp.where((k_pos <= q_pos) & (k_pos < seq_len), scores[:, first:], neg_large)
    if first:
        seen = jnp.concatenate([scores[:, :first], seen], axis=1)
    exps = jnp.exp(seen - jnp.max(seen, axis=-1, keepdims=True))
    return exps * (1.0 / jnp.sum(exps, axis=-1, keepdims=True))


def block_rows(order_ref, i, size):
    return pl.ds(pl.multiple_of(order_ref[i] * size, size), size)


def load_keys(order_ref, k_ref, v_ref, cos_ref, sin_ref, keys, values, size):
    for i in range(keys.shape[0] // size):
        rows = block_rows(order_ref, i, size)
        here = pl.ds(i * size, size)
        keys[here] = rotate(k_ref[rows], cos_ref[here], sin_ref[here]).astype(bf16)
        values[here] = v_ref[rows].astype(bf16)


def attention_forward_kernel(
    order_ref, len_ref, q_ref, k_ref, v_ref, cos_ref, sin_ref, out_ref, keys, values
):
    blocks = order_ref.shape[0]
    size = keys.shape[0] // blocks
    seq_len = len_ref[0]

    @pl.when(pl.program_id(0) == 0)
    def _():
        load_keys(order_ref, k_ref, v_ref, cos_ref, sin_ref, keys, values, size)

    for i in range(blocks):
        rows = block_rows(order_ref, i, size)
        here = pl.ds(i * size, size)
        upto = (i + 1) * size
        queries = (FACTOR * rotate(q_ref[rows], cos_ref[here], sin_ref[here])).astype(bf16)
        probs = probabilities(queries, keys[:upto], i, size, seq_len).astype(bf16)
        out_ref[rows] = mm(probs, values[:upto]).astype(bf16)


def attention_backward_kernel(
    order_ref, len_ref, q_ref, k_ref, v_ref, cos_ref, sin_ref, g_ref, out_ref, keys, values, d_keys, d_values
):
    blocks = order_ref.shape[0]
    size = keys.shape[0] // blocks
    seq_len = len_ref[0]
    step = pl.program_id(0)
    heads = pl.num_programs(0) - 2

    @pl.when(step == 0)
    def _():
        load_keys(order_ref, k_ref, v_ref, cos_ref, sin_ref, keys, values, size)
        d_keys[...] = jnp.zeros_like(d_keys)
        d_values[...] = jnp.zeros_like(d_values)

    @pl.when(step < heads)
    def _():
        for i in range(blocks):
            rows = block_rows(order_ref, i, size)
            here = pl.ds(i * size, size)
            upto = (i + 1) * size
            cos_b, sin_b = cos_ref[here], sin_ref[here]
            queries = (FACTOR * rotate(q_ref[rows], cos_b, sin_b)).astype(bf16)
            grads = g_ref[rows]
            probs = probabilities(queries, keys[:upto], i, size, seq_len)
            d_values[:upto] += mm_rows(probs.astype(bf16), grads)
            d_probs = mm_t(grads, values[:upto])
            inner = jnp.sum(probs * d_probs, axis=-1, keepdims=True)
            d_scores = (probs * (d_probs - inner)).astype(bf16)
            d_keys[:upto] += mm_rows(d_scores, queries)
            d_queries = FACTOR * mm(d_scores, keys[:upto])
            out_ref[rows] = rotate_back(d_queries, cos_b, sin_b).astype(bf16)

    @pl.when(step == heads)
    def _():
        for i in range(blocks):
            here = pl.ds(i * size, size)
            out_ref[block_rows(order_ref, i, size)] = rotate_back(
                d_keys[here], cos_ref[here], sin_ref[here]
            ).astype(bf16)

    @pl.when(step == heads + 1)
    def _():
        for i in range(blocks):
            out_ref[block_rows(order_ref, i, size)] = d_values[pl.ds(i * size, size)].astype(bf16)


def attention_specs(slots, heads):
    half = HEAD_SIZE // 2
    return [
        pl.BlockSpec((slots, HEAD_SIZE), lambda h, o, n: (0, jnp.minimum(h, heads - 1))),
        pl.BlockSpec((slots, HEAD_SIZE), lambda h, o, n: (0, heads)),
        pl.BlockSpec((slots, HEAD_SIZE), lambda h, o, n: (0, heads + 1)),
        pl.BlockSpec((slots, half), lambda h, o, n: (0, 0)),
        pl.BlockSpec((slots, half), lambda h, o, n: (0, 0)),
    ]


def attention_forward(order, length, qkv, tables):
    slots = qkv.shape[0]
    heads = qkv.shape[1] // HEAD_SIZE - 2
    return pl.pallas_call(
        attention_forward_kernel,
        name="attention_forward",
        grid_spec=pltpu.PrefetchScalarGridSpec(
            num_scalar_prefetch=2,
            grid=(heads,),
            in_specs=attention_specs(slots, heads),
            out_specs=pl.BlockSpec((slots, HEAD_SIZE), lambda h, o, n: (0, h)),
            scratch_shapes=[pltpu.VMEM((slots, HEAD_SIZE), bf16)] * 2,
        ),
        out_shape=jax.ShapeDtypeStruct((slots, heads * HEAD_SIZE), bf16),
        cost_estimate=pl.CostEstimate(
            flops=3 * heads * slots * slots * HEAD_SIZE,
            transcendentals=heads * slots * slots,
            bytes_accessed=8 * slots * HEAD_SIZE * (heads + 2),
        ),
        compiler_params=pltpu.CompilerParams(vmem_limit_bytes=56 << 20),
    )(order, length, qkv, qkv, qkv, *tables)


def attention_backward(order, length, qkv, tables, d_context):
    slots = qkv.shape[0]
    heads = qkv.shape[1] // HEAD_SIZE - 2
    return pl.pallas_call(
        attention_backward_kernel,
        name="attention_backward",
        grid_spec=pltpu.PrefetchScalarGridSpec(
            num_scalar_prefetch=2,
            grid=(heads + 2,),
            in_specs=attention_specs(slots, heads)
            + [pl.BlockSpec((slots, HEAD_SIZE), lambda h, o, n: (0, jnp.minimum(h, heads - 1)))],
            out_specs=pl.BlockSpec((slots, HEAD_SIZE), lambda h, o, n: (0, h)),
            scratch_shapes=[pltpu.VMEM((slots, HEAD_SIZE), bf16)] * 2
            + [pltpu.VMEM((slots, HEAD_SIZE), f32)] * 2,
        ),
        out_shape=jax.ShapeDtypeStruct((slots, (heads + 2) * HEAD_SIZE), bf16),
        cost_estimate=pl.CostEstimate(
            flops=7 * heads * slots * slots * HEAD_SIZE,
            transcendentals=heads * slots * slots,
            bytes_accessed=8 * slots * HEAD_SIZE * (heads + 2),
        ),
        compiler_params=pltpu.CompilerParams(vmem_limit_bytes=56 << 20),
    )(order, length, qkv, qkv, qkv, *tables, d_context)


def attention_products_kernel(g1_ref, context_ref, h_ref, d_qkv_ref, *refs):
    out_ref = refs[-1]
    cols = context_ref.shape[1]
    out_ref[:, :cols] = mm_rows(g1_ref[...], context_ref[...]).astype(bf16)
    out_ref[:, cols:] = mm_rows(h_ref[...], d_qkv_ref[...]).astype(bf16)


def attention_products(g1, context, h, d_qkv, *earlier):
    rows, width = g1.shape
    cols, more = context.shape[1], d_qkv.shape[1]
    tm = tile(width, 512)
    return pl.pallas_call(
        attention_products_kernel,
        name="attention_products",
        grid=(width // tm,),
        in_specs=[
            pl.BlockSpec((rows, tm), lambda i: (0, i)),
            pl.BlockSpec((rows, cols), lambda i: (0, 0)),
            pl.BlockSpec((rows, tm), lambda i: (0, i)),
            pl.BlockSpec((rows, more), lambda i: (0, 0)),
        ]
        + [pl.BlockSpec(memory_space=pl.ANY)] * len(earlier),
        out_specs=pl.BlockSpec((tm, cols + more), lambda i: (i, 0)),
        out_shape=jax.ShapeDtypeStruct((width, cols + more), bf16),
        cost_estimate=pl.CostEstimate(
            flops=2 * rows * width * (cols + more),
            transcendentals=0,
            bytes_accessed=4 * rows * width + 2 * (rows + width) * (cols + more),
        ),
        compiler_params=pltpu.CompilerParams(vmem_limit_bytes=56 << 20),
    )(g1, context, h, d_qkv, *earlier)


def prepare_kernel(order_ref, len_ref, x_ref, grad_ref, x_out, grad_out):
    size = x_ref.shape[0]
    first = order_ref[pl.program_id(0)] * size
    pos = first + lax.broadcasted_iota(jnp.int32, (size, 1), 0)
    x_out[...] = x_ref[...]
    grad_out[...] = jnp.where(pos < len_ref[0], grad_ref[...].astype(f32), 0.0).astype(bf16)


def prepare(order, length, x_in, cotangent):
    slots, width = x_in.shape
    size = slots // 4
    source = pl.BlockSpec((size, width), lambda i, o, n: (o[i], 0))
    target = pl.BlockSpec((size, width), lambda i, o, n: (i, 0))
    return pl.pallas_call(
        prepare_kernel,
        name="prepare",
        grid_spec=pltpu.PrefetchScalarGridSpec(
            num_scalar_prefetch=2, grid=(4,), in_specs=[source] * 2, out_specs=[target] * 2
        ),
        out_shape=[jax.ShapeDtypeStruct(x_in.shape, bf16)] * 2,
        cost_estimate=pl.CostEstimate(flops=0, transcendentals=0, bytes_accessed=8 * slots * width),
        compiler_params=pltpu.CompilerParams(vmem_limit_bytes=40 << 20),
    )(order, length, x_in, cotangent)


def spread_heads(block):
    mp_size = lax.axis_size("mp")
    rows, n, heads, part = block.shape
    send = jnp.repeat(block, mp_size // heads, axis=2)
    got = lax.all_to_all(send, "mp", 2, 2, tiled=True)
    return got.reshape(rows, n * mp_size * part)


def attention_end_kernel(heads, grads_ref, q_ref, kv_ref, gain_ref, sums_ref, out_ref, q_out_ref, send_ref):
    cols = q_ref.shape[1]
    size = kv_ref.shape[1] // 2
    part = size // send_ref.shape[0]
    out_ref[...] = grads_ref[:, :cols].astype(f32).T
    q_grad = grads_ref[:, cols : 2 * cols].astype(f32)
    q_out_ref[...] = q_grad
    kv_grad = grads_ref[:, 2 * cols :]
    products = jnp.sum(q_grad * q_ref[...].astype(f32), axis=1, keepdims=True) + jnp.sum(
        kv_grad.astype(f32) * kv_ref[...].astype(f32), axis=1, keepdims=True
    )
    rows = products.shape[0]
    lane = lax.broadcasted_iota(jnp.int32, (rows, 2 * part), 1)
    extra = jnp.zeros((rows, 2 * part), f32)
    for i, v in enumerate([products / gain_ref[...].astype(f32), sums_ref[...]]):
        high = v.astype(bf16).astype(f32)
        extra = jnp.where(lane == 2 * i, high, jnp.where(lane == 2 * i + 1, v - high, extra))
    for m in range(send_ref.shape[0]):
        for i in range(2):
            first = i * size + m * part
            send_ref[m, :, i * part : (i + 1) * part] = kv_grad[:, first : first + part]
        send_ref[m, :, 2 * part :] = extra.astype(bf16)


def attention_end(grads, query_weight, kv_block, gain, ffn_sums):
    rows, cols = query_weight.shape
    mp_size = lax.axis_size("mp")
    part = kv_block.shape[1] // 2 // mp_size
    return pl.pallas_call(
        functools.partial(attention_end_kernel, KEY_VALUE_HEADS),
        name="attention_end",
        out_shape=[
            jax.ShapeDtypeStruct((cols, rows), f32),
            jax.ShapeDtypeStruct((rows, cols), f32),
            jax.ShapeDtypeStruct((mp_size, rows, 4 * part), bf16),
        ],
        cost_estimate=pl.CostEstimate(
            flops=8 * rows * cols, transcendentals=0, bytes_accessed=20 * rows * cols
        ),
        compiler_params=pltpu.CompilerParams(vmem_limit_bytes=40 << 20),
    )(grads, query_weight, kv_block, gain.reshape(-1, 1), ffn_sums.reshape(-1, 1))


def collect_heads(send, heads):
    mp_size, rows, width = send.shape
    part = width // 4
    got = lax.all_to_all(send, "mp", 0, 0, tiled=True).astype(f32)
    kept = jnp.sum(got[:, :, : 2 * part].reshape(heads, mp_size // heads, rows, 2 * part), axis=1)
    extra = jnp.sum(got[:, :, 2 * part : 2 * part + 4], axis=0)
    kept = jnp.transpose(kept, (1, 0, 2))
    return kept[:, :, :part], kept[:, :, part:], extra[:, 0] + extra[:, 1], extra[:, 2] + extra[:, 3]


def gather_dp(block):
    return lax.all_gather(block, DP, axis=0, tiled=True)


def reduce_dp(block):
    return lax.psum_scatter(block, DP, scatter_dimension=0, tiled=True)


def gather_z(block):
    return lax.all_gather(block, "z", axis=0, tiled=True)


def reduce_z(block):
    return lax.psum_scatter(block, "z", scatter_dimension=0, tiled=True)


def to_core(block):
    rows, n, cols = block.shape
    core = lax.axis_index("core")
    m = cols // 2
    own = lax.dynamic_slice_in_dim(block, core * m, m, 2).reshape(rows, n * m)
    away = lax.dynamic_slice_in_dim(block, (1 - core) * m, m, 2).reshape(rows, n * m)
    got = send_core(away)
    return jnp.concatenate([jnp.where(core == 0, own, got), jnp.where(core == 0, got, own)])


def own_half_kernel(transpose, core_ref, own_ref, got_ref, *refs):
    out_ref = refs[-1]
    value = jnp.where(pl.program_id(0) == core_ref[0], own_ref[...].astype(f32), got_ref[...].astype(f32))
    out_ref[...] = value.T if transpose else value


def from_core(block, n, transpose=False, earlier=()):
    rows = block.shape[0] // 2
    m = block.shape[1] // n
    core = lax.axis_index("core").astype(jnp.int32)
    got = send_core(lax.dynamic_slice_in_dim(block, (1 - core) * rows, rows, 0))
    out_block = (m, rows) if transpose else (rows, m)
    out_shape = (2 * m, rows) if transpose else (rows, 2 * m)
    return [
        pl.pallas_call(
            functools.partial(own_half_kernel, transpose),
            name="own_half",
            grid_spec=pltpu.PrefetchScalarGridSpec(
                num_scalar_prefetch=1,
                grid=(2,),
                in_specs=[
                    pl.BlockSpec((rows, m), lambda h, c, i=i: (c[0], i)),
                    pl.BlockSpec((rows, m), lambda h, c, i=i: (0, i)),
                ]
                + [pl.BlockSpec(memory_space=pl.ANY)] * len(earlier),
                out_specs=pl.BlockSpec(out_block, lambda h, c: (h, 0) if transpose else (0, h)),
            ),
            out_shape=jax.ShapeDtypeStruct(out_shape, f32),
            cost_estimate=pl.CostEstimate(flops=0, transcendentals=0, bytes_accessed=12 * rows * m),
            compiler_params=pltpu.CompilerParams(vmem_limit_bytes=40 << 20),
        )(core.reshape(1), block, got, *earlier)
        for i in range(n)
    ]


def ffn_forward_kernel(mine_ref, away_ref, g_ref, u_ref, hidden_ref, factor_ref):
    def run(h_ref):
        h = h_ref[...]
        gate = jnp.dot(h, g_ref[...], preferred_element_type=f32)
        up = jnp.dot(h, u_ref[...], preferred_element_type=f32)
        sig = 1.0 / (1.0 + jnp.exp(-gate))
        silu = gate * sig
        hidden_ref[...] = (silu * up).astype(bf16)
        factor_ref[0] = (up * sig * (1.0 + gate - silu)).astype(bf16)
        factor_ref[1] = silu.astype(bf16)

    pl.when(pl.program_id(0) == 0)(lambda: run(mine_ref))
    pl.when(pl.program_id(0) == 1)(lambda: run(away_ref))


def ffn_forward(mine, away, w_gu):
    rows, width = mine.shape
    ff = w_gu.shape[1] // 2
    tn = tile(ff, 256)
    return pl.pallas_call(
        ffn_forward_kernel,
        name="ffn_forward",
        grid=(2, ff // tn),
        in_specs=[
            pl.BlockSpec((rows, width), lambda i, j: (0, 0)),
            pl.BlockSpec((rows, width), lambda i, j: (0, 0)),
            pl.BlockSpec((width, tn), lambda i, j: (0, j)),
            pl.BlockSpec((width, tn), lambda i, j: (0, j + ff // tn)),
        ],
        out_specs=[
            pl.BlockSpec((rows, tn), lambda i, j: (i, j)),
            pl.BlockSpec((2, rows, tn), lambda i, j: (0, i, j)),
        ],
        out_shape=[
            jax.ShapeDtypeStruct((2 * rows, ff), bf16),
            jax.ShapeDtypeStruct((2, 2 * rows, ff), bf16),
        ],
        cost_estimate=pl.CostEstimate(
            flops=8 * rows * width * ff,
            transcendentals=2 * rows * ff,
            bytes_accessed=4 * (rows * width + width * ff + 3 * rows * ff),
        ),
        compiler_params=pltpu.CompilerParams(vmem_limit_bytes=56 << 20),
    )(mine, away, w_gu, w_gu)


def rows_product_kernel(mine_ref, away_ref, right_mine_ref, right_away_ref, *refs):
    out_ref = refs[-1]
    cols = right_mine_ref.shape[2]
    for i in range(2):
        out_ref[:, i * cols : (i + 1) * cols] = (
            mm_rows(mine_ref[...], right_mine_ref[i]) + mm_rows(away_ref[...], right_away_ref[i])
        ).astype(bf16)


def rows_product(mine, away, right, start, share, into=None, earlier=()):
    rows, width = mine.shape
    cols = 2 * right.shape[2]
    tm = tile(width // 4, 256)
    steps = share * width // 4 // tm
    begin = start * width // 4 // tm
    more = ([] if into is None else [into]) + list(earlier)
    return pl.pallas_call(
        rows_product_kernel,
        name="rows_product",
        grid=(steps,),
        in_specs=[
            pl.BlockSpec((rows, tm), lambda i: (0, begin + i)),
            pl.BlockSpec((rows, tm), lambda i: (0, begin + i)),
            pl.BlockSpec((2, rows, cols // 2), lambda i: (0, 0, 0)),
            pl.BlockSpec((2, rows, cols // 2), lambda i: (0, 1, 0)),
        ]
        + [pl.BlockSpec(memory_space=pl.ANY)] * len(more),
        out_specs=pl.BlockSpec((tm, cols), lambda i: (begin + i, 0)),
        out_shape=jax.ShapeDtypeStruct((width, cols), bf16),
        input_output_aliases={} if into is None else {4: 0},
        cost_estimate=pl.CostEstimate(
            flops=4 * rows * width * cols * share // 4,
            transcendentals=0,
            bytes_accessed=(4 * rows * width + 2 * width * cols) * share // 4 + 4 * rows * cols,
        ),
        compiler_params=pltpu.CompilerParams(vmem_limit_bytes=56 << 20),
    )(mine, away, right, right, *more)


def ffn_backward_kernel(grad_ref, d_ref, factor_ref, earlier_ref, out_ref):
    d_hidden = mm(grad_ref[...], d_ref[...])
    for i in range(2):
        out_ref[i] = (d_hidden * factor_ref[i].astype(f32)).astype(bf16)


def ffn_backward(grad, w_d, factors, earlier):
    rows, width = grad.shape
    ff = w_d.shape[1]
    tm, tn = tile(rows, 1024), tile(ff, 256)
    return pl.pallas_call(
        ffn_backward_kernel,
        name="ffn_backward",
        grid=(rows // tm, ff // tn),
        in_specs=[
            pl.BlockSpec((tm, width), lambda i, j: (i, 0)),
            pl.BlockSpec((width, tn), lambda i, j: (0, j)),
            pl.BlockSpec((2, tm, tn), lambda i, j: (0, i, j)),
            pl.BlockSpec(memory_space=pl.ANY),
        ],
        out_specs=pl.BlockSpec((2, tm, tn), lambda i, j: (0, i, j)),
        out_shape=jax.ShapeDtypeStruct((2, rows, ff), bf16),
        cost_estimate=pl.CostEstimate(
            flops=2 * rows * width * ff, transcendentals=0, bytes_accessed=2 * (rows * width + width * ff + 4 * rows * ff)
        ),
        compiler_params=pltpu.CompilerParams(vmem_limit_bytes=56 << 20),
    )(grad, w_d, factors, earlier)


def local(
    x_in,
    lengths,
    gain_attn,
    query_weight,
    key_projection_matrix,
    value_projection_matrix,
    out_weight,
    gain_ffn,
    gate_weight,
    up_weight,
    down_weight,
    cotangent,
):
    _, slots, width = x_in.shape
    mp_size = lax.axis_size("mp")
    me = lax.axis_index("mp")
    q_cols = query_weight.shape[1]
    here = slots // mp_size
    quarter = slots // 4
    tables = rope_tables(slots, HEAD_SIZE)
    sequence_block, relative_place = block_orders()

    def own_rows(v):
        return v[:here] if square() else lax.dynamic_slice_in_dim(v, me * here, here, 0)

    x_rel, grad_mine = prepare(sequence_block, lengths, x_in[0], cotangent[0])
    kv_block = spread_heads(jnp.stack([key_projection_matrix, value_projection_matrix], axis=1))
    w_attn = gather_dp(jnp.concatenate([query_weight, kv_block, out_weight.T], axis=1))
    o_first = q_cols + 2 * HEAD_SIZE
    ffn_block = to_core(jnp.stack([gate_weight, up_weight, down_weight.T], axis=1))
    ff = ffn_block.shape[1] // 3
    w_gu = gather_z(ffn_block[:, : 2 * ff])
    w_d = gather_z(ffn_block[:, 2 * ff :])
    gains = lax.all_gather(jnp.stack([gain_attn, gain_ffn]), DP, axis=1, tiled=True).astype(f32)
    g_attn, g_ffn = gains[0], gains[1]

    tok = x_rel.astype(f32)
    r1 = lax.rsqrt(jnp.mean(tok * tok, axis=-1, keepdims=True) + eps_norm)
    h_attn = (tok * r1 * g_attn).astype(bf16)
    grad_all = jnp.concatenate([grad_mine, send_core(grad_mine)])
    qkv = column_product(h_attn, w_attn, 0, o_first, f32)
    context = attention_forward(relative_place, lengths, qkv, tables)

    attn_rows = scatter_rows(scatter_product(context, w_attn, o_first, slots))
    tok_here = own_rows(x_rel).astype(f32)
    mid = tok_here + attn_rows
    r2 = lax.rsqrt(jnp.mean(mid * mid, axis=-1, keepdims=True) + eps_norm)
    n2 = mid * r2
    h_mine = join_rows(exchange_rows((n2 * g_ffn).astype(bf16)), True)
    h_away = send_core(h_mine)

    hidden, factors = ffn_forward(h_mine, h_away, w_gu)
    down_grad = mm_rows(grad_all, hidden).astype(bf16)
    down_out = reduce_z(down_grad)

    ffn_away = away_product(hidden, w_d, slots, (down_grad,))
    ffn_add = send_core(ffn_away)
    d_gu = ffn_backward(grad_all, w_d, factors, ffn_away)
    ffn_pieces = scatter_product(hidden, w_d, 0, slots, ffn_add, (d_gu,))
    ffn_near = scatter_near(ffn_pieces)
    gu_grad = rows_product(h_mine, h_away, d_gu, 0, 2, earlier=(ffn_pieces[-1],))
    h2_away = away_product(d_gu, w_gu, slots, (gu_grad,))
    ffn_middle = scatter_middle(ffn_pieces, ffn_near)
    gu_grad = rows_product(h_mine, h_away, d_gu, 2, 2, gu_grad, (h2_away, *ffn_middle))
    gu_grad, down_out = tie(gu_grad, down_out)
    gu_out = reduce_z(gu_grad)
    h2_add = send_core(h2_away)
    ffn_far = scatter_far(ffn_middle)
    h2_pieces = list(scatter_product(d_gu, w_gu, 0, slots, earlier=(gu_grad,)))
    h2_pieces[0], h2_add = tie(h2_pieces[0], h2_add)
    h2_summed = add_away(h2_pieces, h2_add)
    h2_summed[-1], ffn_far = tie(h2_summed[-1], ffn_far)
    ffn_rows = scatter_end(ffn_pieces, ffn_near, ffn_far)
    h2_near = scatter_near(h2_summed)
    h2_far = scatter_far(scatter_middle(h2_summed, h2_near))
    kept, h2_own = (h2_pieces, h2_add) if square() else (h2_summed, None)
    g1, g1_block = rows_backward(kept, h2_near, h2_far, h2_own, mid, grad_mine, g_ffn)
    g1_low = join_rows(exchange_rows(g1_block), True)

    layer_block, g1_low = tie((mid + ffn_rows).astype(bf16), g1_low)
    layer_near = exchange_near(layer_block)
    d_context = column_product(g1_low, w_attn, o_first, q_cols, bf16)
    d_qkv = attention_backward(relative_place, lengths, qkv, tables, d_context)
    layer_middle = exchange_middle(layer_near)
    attn_grads = attention_products(g1_low, context, h_attn, d_qkv, *layer_middle)
    attn_out = reduce_dp(attn_grads)
    layer_far = exchange_far(layer_middle)
    h1_pieces = scatter_product(d_qkv, w_attn, 0, slots, earlier=(attn_grads,))
    h1_pieces, layer_far = tie(h1_pieces, layer_far)
    layer_out = join_rows((layer_block, *layer_near, *layer_far), False)
    h1_near = scatter_near(h1_pieces)
    (down_out,) = from_core(down_out, 1, True)
    gate_out, up_out = from_core(gu_out, 2, earlier=(down_out,))
    h1_near, gate_out, up_out, layer_out = tie(h1_near, gate_out, up_out, layer_out)
    h1_far = scatter_far(scatter_middle(h1_pieces, h1_near))
    _, grad_block = rows_backward(h1_pieces, h1_near, h1_far, None, x_rel, g1, g_attn)
    grad_pieces = list(exchange_rows(grad_block))
    grad_pieces[0], attn_out = tie(grad_pieces[0], attn_out)

    rows_here = gain_attn.shape[0]

    ffn_sums = sum(
        jnp.sum(w.astype(f32) * g, axis=1) for w, g in [(gate_weight, gate_out), (up_weight, up_out)]
    ) / gain_ffn.astype(f32)
    out_out, q_out, send = attention_end(attn_out, query_weight, kv_block, gain_attn, ffn_sums)
    if square():
        joined = join_near(grad_pieces[:3], f32)
        *far_pieces, send, joined = tie(*grad_pieces[3:], send, joined)
    key_grad, value_grad, gain_attn_grad, gain_ffn_grad = collect_heads(send, KEY_VALUE_HEADS)
    if square():
        grad_input = join_far(far_pieces, joined)
    else:
        grad_input = grad_pieces[1].astype(f32)
    return (
        layer_out[None],
        grad_input[None],
        gain_attn_grad,
        q_out,
        key_grad,
        value_grad,
        out_out,
        gain_ffn_grad,
        gate_out,
        up_out,
        down_out,
    )


def solution(mesh):
    dp_size, mp_size = mesh.shape["dp"], mesh.shape["mp"]
    split = Mesh(mesh.devices.reshape(dp_size // 2, 2, mp_size), ("z", "core", "mp"))
    return jax.shard_map(
        local,
        mesh=split,
        in_specs=(
            P(DP, None, None),
            P(DP),
            P(DP),
            P(DP, "mp"),
            P(DP, None, "mp"),
            P(DP, None, "mp"),
            P("mp", DP),
            P(DP),
            P(DP, "mp"),
            P(DP, "mp"),
            P("mp", DP),
            P(DP, None, None),
        ),
        out_specs=(
            P(DP, None, None),
            P(DP, None, None),
            P(DP),
            P(DP, "mp"),
            P(DP, None, "mp"),
            P(DP, None, "mp"),
            P("mp", DP),
            P(DP),
            P(DP, "mp"),
            P(DP, "mp"),
            P("mp", DP),
        ),
        check_vma=False,
    )
```

```python
import functools

import jax
import jax.numpy as jnp
from jax import lax
from jax.experimental import pallas as pl
from jax.experimental.pallas import tpu as pltpu
from jax.sharding import Mesh, PartitionSpec as P

QUERY_HEADS = 8
KEY_VALUE_HEADS = 4
HEAD_SIZE = 256

eps_norm = 1e-06
rope_base = 1000042.0
neg_large = -1e30
bf16 = jnp.bfloat16
f32 = jnp.float32


def rope_tables(slot_length, size):
    half_size = size // 2
    inv_freq = rope_base ** (-(jnp.arange(half_size, dtype=f32) * 2.0 / size))
    angles = jnp.arange(slot_length, dtype=f32)[:, None] * inv_freq[None, :]
    return (jnp.cos(angles), jnp.sin(angles))


def rotate(values, cos_b, sin_b):
    half = values.shape[-1] // 2
    a, b = values[..., :half], values[..., half:]
    return jnp.concatenate([a * cos_b - b * sin_b, b * cos_b + a * sin_b], axis=-1)


def rotate_back(grads, cos_b, sin_b):
    half = grads.shape[-1] // 2
    a, b = grads[..., :half], grads[..., half:]
    return jnp.concatenate([a * cos_b + b * sin_b, b * cos_b - a * sin_b], axis=-1)


def mm(left, right):
    return lax.dot_general(left, right, (((1,), (0,)), ((), ())), preferred_element_type=f32)


def mm_t(left, right):
    return lax.dot_general(left, right, (((1,), (1,)), ((), ())), preferred_element_type=f32)


def mm_rows(left, right):
    return lax.dot_general(left, right, (((0,), (0,)), ((), ())), preferred_element_type=f32)


DP = ("z", "core")
OVER_X = [(0, 1), (1, 0), (2, 3), (3, 2)]
OVER_Y = [(0, 2), (2, 0), (1, 3), (3, 1)]
OVER_CORE = [(0, 1), (1, 0)]


def send_x(v):
    return lax.ppermute(v, "mp", OVER_X)


def send_y(v):
    return lax.ppermute(v, "mp", OVER_Y)


def send_core(v):
    return lax.ppermute(v, "core", OVER_CORE)


def square():
    return lax.axis_size("mp") == 4


def tie(*values):
    return lax.optimization_barrier(values)


def block_orders():
    steps = jnp.arange(4, dtype=jnp.int32)
    if not square():
        return steps, steps
    me = lax.axis_index("mp").astype(jnp.int32)
    away = jnp.bitwise_xor(me, steps)
    return jnp.bitwise_xor(me, jnp.array([0, 2, 1, 3], jnp.int32)), (away % 2) * 2 + away // 2


def tile(size, most):
    while size % most:
        most //= 2
    return most


def column_product_kernel(left_ref, right_ref, out_ref):
    out_ref[...] = mm(left_ref[...], right_ref[...]).astype(out_ref.dtype)


def column_product(left, right, first, cols, dtype):
    rows, depth = left.shape
    tn = tile(cols, 256)
    return pl.pallas_call(
        column_product_kernel,
        name="column_product",
        grid=(cols // tn,),
        in_specs=[
            pl.BlockSpec((rows, depth), lambda j: (0, 0)),
            pl.BlockSpec((depth, tn), lambda j: (0, first // tn + j)),
        ],
        out_specs=pl.BlockSpec((rows, tn), lambda j: (0, j)),
        out_shape=jax.ShapeDtypeStruct((rows, cols), dtype),
        cost_estimate=pl.CostEstimate(
            flops=2 * rows * depth * cols, transcendentals=0, bytes_accessed=2 * (rows + cols) * depth + 4 * rows * cols
        ),
        compiler_params=pltpu.CompilerParams(vmem_limit_bytes=56 << 20),
    )(left, right)


def transposed_product_kernel(groups, added, left_ref, right_ref, *refs):
    outs = refs[-sum(len(g) for g in groups) :]
    steps = pl.num_programs(0) // len(groups)
    if len(left_ref.shape) == 2:
        total = mm_t(left_ref[...], right_ref[...])
    else:
        depth = left_ref.shape[2]
        total = mm_t(left_ref[0], right_ref[:, :depth]) + mm_t(left_ref[1], right_ref[:, depth:])
    if added:
        total = total + refs[0][...].astype(f32)
    size = total.shape[0] // 4
    for i, group in enumerate(groups):

        @pl.when(pl.program_id(0) // steps == i)
        def _(first=sum(len(g) for g in groups[:i]), group=group):
            for out, blocks in zip(outs[first : first + len(group)], group):
                for place, block in enumerate(blocks):
                    part = total[block * size : (block + 1) * size]
                    out[place * size : (place + 1) * size] = part.astype(out.dtype)


def transposed_product(left, sequence, rows, right, first, groups, add=None, earlier=()):
    depth = left.shape[-1]
    pair = left.ndim == 3
    deep = 2 * depth if pair else depth
    cols = right.shape[0] // len(groups)
    tn = tile(cols, 512)
    steps = cols // tn
    size = rows // 4
    adds = [] if add is None else [add]

    def at(i):
        return lambda j: (0, jnp.clip(j - i * steps, 0, steps - 1))

    return pl.pallas_call(
        functools.partial(transposed_product_kernel, groups, add is not None),
        name="transposed_product",
        grid=(len(groups) * steps,),
        in_specs=[
            pl.BlockSpec((2, rows, depth), lambda j: (0, sequence, 0))
            if pair
            else pl.BlockSpec((rows, depth), lambda j: (sequence, 0)),
            pl.BlockSpec((tn, deep), lambda j: (j, first // deep)),
        ]
        + [pl.BlockSpec((rows, tn), lambda j: (0, j))] * len(adds)
        + [pl.BlockSpec(memory_space=pl.ANY)] * len(earlier),
        out_specs=[
            pl.BlockSpec((len(blocks) * size, tn), at(i))
            for i, group in enumerate(groups)
            for blocks in group
        ],
        out_shape=[
            jax.ShapeDtypeStruct((len(blocks) * size, cols), f32 if blocks == (0,) else bf16)
            for group in groups
            for blocks in group
        ],
        cost_estimate=pl.CostEstimate(
            flops=2 * rows * deep * right.shape[0],
            transcendentals=0,
            bytes_accessed=2 * (rows + right.shape[0]) * deep + 2 * rows * right.shape[0],
        ),
        compiler_params=pltpu.CompilerParams(vmem_limit_bytes=56 << 20),
    )(left, right, *adds, *earlier)


WHOLE = (((0, 1, 2, 3),),)
PIECES = (((0,), (1,), (2, 3)), ((0,), (2,), (1, 3)))


def away_product(left, right, rows, earlier=()):
    return transposed_product(left, 1, rows, right, 0, WHOLE, earlier=earlier)[0]


def scatter_product(left, right, first, rows, add=None, earlier=()):
    groups = PIECES if square() else WHOLE
    return transposed_product(left, 0, rows, right, first, groups, add, earlier)


def add_away(pieces, away):
    if not square():
        return [(pieces[0].astype(f32) + away.astype(f32)).astype(bf16)]
    size, half = pieces[1].shape
    away = away.reshape(2, 2, size, 2 * half)
    parts = [
        away[0, 0, :, :half],
        away[0, 1, :, :half],
        away[1, :, :, :half].reshape(2 * size, half),
        away[0, 0, :, half:],
        away[1, 0, :, half:],
        away[:, 1, :, half:].reshape(2 * size, half),
    ]
    return [
        (piece.astype(f32) + part.astype(f32)).astype(piece.dtype) for piece, part in zip(pieces, parts)
    ]


def scatter_near(pieces):
    if not square():
        return ()
    return send_x(pieces[2]), send_y(pieces[5])


def scatter_middle(pieces, near):
    if not square():
        return ()
    own_a, y_a, _, own_b, x_b, _ = pieces
    size = own_a.shape[0]
    return (
        (y_a.astype(f32) + near[0][size:].astype(f32)).astype(bf16),
        (x_b.astype(f32) + near[1][size:].astype(f32)).astype(bf16),
    )


def scatter_far(middle):
    if not square():
        return ()
    return send_y(middle[0]), send_x(middle[1])


def scatter_end(pieces, near, far):
    if not square():
        return lax.psum_scatter(pieces[0], "mp", scatter_dimension=0, tiled=True).astype(f32)
    size = pieces[0].shape[0]
    kept = [
        own + got[:size].astype(f32) + last.astype(f32)
        for own, got, last in zip((pieces[0], pieces[3]), near, far)
    ]
    return jnp.concatenate(kept, axis=1)


def scatter_rows(pieces):
    near = scatter_near(pieces)
    return scatter_end(pieces, near, scatter_far(scatter_middle(pieces, near)))


def rows_backward_kernel(added, *refs):
    own, got, last = refs[0:2], refs[2:4], refs[4:6]
    v_ref, base_ref, gain_ref = refs[6 + added : 9 + added]
    g_ref, low_ref = refs[9 + added :]
    half = own[0].shape[1]
    width = 2 * half
    v = v_ref[...].astype(f32)
    r = lax.rsqrt(jnp.sum(v * v, axis=-1, keepdims=True) * (1.0 / width) + eps_norm)
    n = v * r
    parts = []
    for i in range(2):
        columns = slice(i * half, (i + 1) * half)
        d = own[i][...] + got[i][...].astype(f32) + last[i][...].astype(f32)
        if added:
            d = d + refs[6][:, columns].astype(f32)
        parts.append(d * gain_ref[:, columns])
    e = jnp.concatenate(parts, axis=1)
    inner = jnp.sum(e * n, axis=-1, keepdims=True) * (1.0 / width)
    g = base_ref[...].astype(f32) + r * (e - n * inner)
    g_ref[...] = g
    low_ref[...] = g.astype(bf16)


def rows_backward(pieces, near, far, away, v, base, gain):
    if not square():
        here = pieces[0].shape[0] // lax.axis_size("mp")
        d = scatter_end(pieces, near, far)

        def own(u):
            if u.shape[0] == here:
                return u
            return lax.dynamic_slice_in_dim(u, lax.axis_index("mp") * here, here, 0)

        v, base = own(v).astype(f32), own(base).astype(f32)
        r = lax.rsqrt(jnp.mean(v * v, axis=-1, keepdims=True) + eps_norm)
        n, e = v * r, d * gain
        g = base + r * (e - n * jnp.mean(e * n, axis=-1, keepdims=True))
        return g, g.astype(bf16)
    here, half = pieces[0].shape
    tm = tile(here, 64)
    narrow = pl.BlockSpec((tm, half), lambda i: (i, 0))
    wide = pl.BlockSpec((tm, 2 * half), lambda i: (i, 0))
    adds = [] if away is None else [away]
    return pl.pallas_call(
        functools.partial(rows_backward_kernel, len(adds)),
        name="rows_backward",
        grid=(here // tm,),
        in_specs=[narrow] * 6
        + [wide] * (len(adds) + 2)
        + [pl.BlockSpec((1, 2 * half), lambda i: (0, 0))],
        out_specs=[wide, wide],
        out_shape=[
            jax.ShapeDtypeStruct((here, 2 * half), f32),
            jax.ShapeDtypeStruct((here, 2 * half), bf16),
        ],
        cost_estimate=pl.CostEstimate(
            flops=40 * here * half, transcendentals=here, bytes_accessed=40 * here * half
        ),
        compiler_params=pltpu.CompilerParams(vmem_limit_bytes=40 << 20),
    )(pieces[0], pieces[3], *near, *far, *adds, v, base, gain.reshape(1, -1))


def assemble_kernel(order_ref, own, over_x, over_y, diag_a, diag_b, out_ref):
    half = diag_a.shape[1]
    for i, ref in enumerate([own, over_y, over_x]):

        @pl.when(pl.program_id(0) == i)
        def _(ref=ref):
            out_ref[...] = ref[...].astype(out_ref.dtype)

    @pl.when(pl.program_id(0) == 3)
    def _():
        out_ref[:, :half] = diag_a[...].astype(out_ref.dtype)
        out_ref[:, half:] = diag_b[...].astype(out_ref.dtype)


def assemble(order, pieces, dtype):
    here, width = pieces[0].shape
    return pl.pallas_call(
        assemble_kernel,
        name="assemble",
        grid_spec=pltpu.PrefetchScalarGridSpec(
            num_scalar_prefetch=1,
            grid=(4,),
            in_specs=[pl.BlockSpec((here, piece.shape[1]), lambda i, s: (0, 0)) for piece in pieces],
            out_specs=pl.BlockSpec((here, width), lambda i, s: (s[i], 0)),
        ),
        out_shape=jax.ShapeDtypeStruct((4 * here, width), dtype),
        cost_estimate=pl.CostEstimate(flops=0, transcendentals=0, bytes_accessed=20 * here * width),
        compiler_params=pltpu.CompilerParams(vmem_limit_bytes=40 << 20),
    )(order, *pieces)


def join_near_kernel(order_ref, own, over_x, over_y, out_ref):
    for i, ref in enumerate([own, over_y, over_x]):

        @pl.when(pl.program_id(0) == i)
        def _(ref=ref):
            out_ref[...] = ref[...].astype(out_ref.dtype)


def join_far_kernel(order_ref, diag_a, diag_b, near_ref, out_ref):
    half = diag_a.shape[1]
    out_ref[:, :half] = diag_a[...].astype(out_ref.dtype)
    out_ref[:, half:] = diag_b[...].astype(out_ref.dtype)


def join_near(pieces, dtype):
    here, width = pieces[0].shape
    return pl.pallas_call(
        join_near_kernel,
        name="join_near",
        grid_spec=pltpu.PrefetchScalarGridSpec(
            num_scalar_prefetch=1,
            grid=(3,),
            in_specs=[pl.BlockSpec((here, width), lambda i, s: (0, 0))] * 3,
            out_specs=pl.BlockSpec((here, width), lambda i, s: (s[i], 0)),
        ),
        out_shape=jax.ShapeDtypeStruct((4 * here, width), dtype),
        cost_estimate=pl.CostEstimate(flops=0, transcendentals=0, bytes_accessed=18 * here * width),
        compiler_params=pltpu.CompilerParams(vmem_limit_bytes=40 << 20),
    )(block_orders()[0], *pieces)


def join_far(pieces, near):
    here, half = pieces[0].shape
    return pl.pallas_call(
        join_far_kernel,
        name="join_far",
        grid_spec=pltpu.PrefetchScalarGridSpec(
            num_scalar_prefetch=1,
            grid=(1,),
            in_specs=[pl.BlockSpec((here, half), lambda i, s: (0, 0))] * 2
            + [pl.BlockSpec(memory_space=pl.ANY)],
            out_specs=pl.BlockSpec((here, 2 * half), lambda i, s: (s[3], 0)),
        ),
        out_shape=jax.ShapeDtypeStruct(near.shape, near.dtype),
        input_output_aliases={3: 0},
        cost_estimate=pl.CostEstimate(flops=0, transcendentals=0, bytes_accessed=12 * here * half),
        compiler_params=pltpu.CompilerParams(vmem_limit_bytes=40 << 20),
    )(block_orders()[0], *pieces, near)


def exchange_near(block):
    if not square():
        return (lax.all_gather(block, "mp", axis=0, tiled=True),)
    return send_x(block), send_y(block)


def exchange_middle(near):
    if not square():
        return ()
    half = near[0].shape[1] // 2
    return near[1][:, :half], near[0][:, half:]


def exchange_far(middle):
    if not square():
        return ()
    return send_x(middle[0]), send_y(middle[1])


def exchange_rows(block):
    near = exchange_near(block)
    return (block, *near, *exchange_far(exchange_middle(near)))


def join_rows(pieces, relative, dtype=bf16):
    if not square():
        return pieces[1].astype(dtype)
    order = jnp.arange(4, dtype=jnp.int32) if relative else block_orders()[0]
    return assemble(order, pieces, dtype)


SHORTEST = 512
FACTOR = HEAD_SIZE ** (-0.5)


def probabilities(queries, keys, i, size, seq_len):
    scores = mm_t(queries, keys)
    first = min(i * size, SHORTEST)
    shape = (size, (i + 1) * size - first)
    q_pos = i * size + lax.broadcasted_iota(jnp.int32, shape, 0)
    k_pos = first + lax.broadcasted_iota(jnp.int32, shape, 1)
    seen = jnp.where((k_pos <= q_pos) & (k_pos < seq_len), scores[:, first:], neg_large)
    if first:
        seen = jnp.concatenate([scores[:, :first], seen], axis=1)
    exps = jnp.exp(seen - jnp.max(seen, axis=-1, keepdims=True))
    return exps * (1.0 / jnp.sum(exps, axis=-1, keepdims=True))


def block_rows(order_ref, i, size):
    return pl.ds(pl.multiple_of(order_ref[i] * size, size), size)


def load_keys(order_ref, k_ref, v_ref, cos_ref, sin_ref, keys, values, size):
    for i in range(keys.shape[0] // size):
        rows = block_rows(order_ref, i, size)
        here = pl.ds(i * size, size)
        keys[here] = rotate(k_ref[rows], cos_ref[here], sin_ref[here]).astype(bf16)
        values[here] = v_ref[rows].astype(bf16)


def attention_forward_kernel(
    order_ref, len_ref, q_ref, k_ref, v_ref, cos_ref, sin_ref, out_ref, keys, values
):
    blocks = order_ref.shape[0]
    size = keys.shape[0] // blocks
    seq_len = len_ref[0]

    @pl.when(pl.program_id(0) == 0)
    def _():
        load_keys(order_ref, k_ref, v_ref, cos_ref, sin_ref, keys, values, size)

    for i in range(blocks):
        rows = block_rows(order_ref, i, size)
        here = pl.ds(i * size, size)
        upto = (i + 1) * size
        queries = (FACTOR * rotate(q_ref[rows], cos_ref[here], sin_ref[here])).astype(bf16)
        probs = probabilities(queries, keys[:upto], i, size, seq_len).astype(bf16)
        out_ref[rows] = mm(probs, values[:upto]).astype(bf16)


def attention_backward_kernel(
    order_ref, len_ref, q_ref, k_ref, v_ref, cos_ref, sin_ref, g_ref, out_ref, keys, values, d_keys, d_values
):
    blocks = order_ref.shape[0]
    size = keys.shape[0] // blocks
    seq_len = len_ref[0]
    step = pl.program_id(0)
    heads = pl.num_programs(0) - 2

    @pl.when(step == 0)
    def _():
        load_keys(order_ref, k_ref, v_ref, cos_ref, sin_ref, keys, values, size)
        d_keys[...] = jnp.zeros_like(d_keys)
        d_values[...] = jnp.zeros_like(d_values)

    @pl.when(step < heads)
    def _():
        for i in range(blocks):
            rows = block_rows(order_ref, i, size)
            here = pl.ds(i * size, size)
            upto = (i + 1) * size
            cos_b, sin_b = cos_ref[here], sin_ref[here]
            queries = (FACTOR * rotate(q_ref[rows], cos_b, sin_b)).astype(bf16)
            grads = g_ref[rows]
            probs = probabilities(queries, keys[:upto], i, size, seq_len)
            d_values[:upto] += mm_rows(probs.astype(bf16), grads)
            d_probs = mm_t(grads, values[:upto])
            inner = jnp.sum(probs * d_probs, axis=-1, keepdims=True)
            d_scores = (probs * (d_probs - inner)).astype(bf16)
            d_keys[:upto] += mm_rows(d_scores, queries)
            d_queries = FACTOR * mm(d_scores, keys[:upto])
            out_ref[rows] = rotate_back(d_queries, cos_b, sin_b).astype(bf16)

    @pl.when(step == heads)
    def _():
        for i in range(blocks):
            here = pl.ds(i * size, size)
            out_ref[block_rows(order_ref, i, size)] = rotate_back(
                d_keys[here], cos_ref[here], sin_ref[here]
            ).astype(bf16)

    @pl.when(step == heads + 1)
    def _():
        for i in range(blocks):
            out_ref[block_rows(order_ref, i, size)] = d_values[pl.ds(i * size, size)].astype(bf16)


def attention_specs(slots, heads):
    half = HEAD_SIZE // 2
    return [
        pl.BlockSpec((slots, HEAD_SIZE), lambda h, o, n: (0, jnp.minimum(h, heads - 1))),
        pl.BlockSpec((slots, HEAD_SIZE), lambda h, o, n: (0, heads)),
        pl.BlockSpec((slots, HEAD_SIZE), lambda h, o, n: (0, heads + 1)),
        pl.BlockSpec((slots, half), lambda h, o, n: (0, 0)),
        pl.BlockSpec((slots, half), lambda h, o, n: (0, 0)),
    ]


def attention_forward(order, length, qkv, tables):
    slots = qkv.shape[0]
    heads = qkv.shape[1] // HEAD_SIZE - 2
    return pl.pallas_call(
        attention_forward_kernel,
        name="attention_forward",
        grid_spec=pltpu.PrefetchScalarGridSpec(
            num_scalar_prefetch=2,
            grid=(heads,),
            in_specs=attention_specs(slots, heads),
            out_specs=pl.BlockSpec((slots, HEAD_SIZE), lambda h, o, n: (0, h)),
            scratch_shapes=[pltpu.VMEM((slots, HEAD_SIZE), bf16)] * 2,
        ),
        out_shape=jax.ShapeDtypeStruct((slots, heads * HEAD_SIZE), bf16),
        cost_estimate=pl.CostEstimate(
            flops=3 * heads * slots * slots * HEAD_SIZE,
            transcendentals=heads * slots * slots,
            bytes_accessed=8 * slots * HEAD_SIZE * (heads + 2),
        ),
        compiler_params=pltpu.CompilerParams(vmem_limit_bytes=56 << 20),
    )(order, length, qkv, qkv, qkv, *tables)


def attention_backward(order, length, qkv, tables, d_context):
    slots = qkv.shape[0]
    heads = qkv.shape[1] // HEAD_SIZE - 2
    return pl.pallas_call(
        attention_backward_kernel,
        name="attention_backward",
        grid_spec=pltpu.PrefetchScalarGridSpec(
            num_scalar_prefetch=2,
            grid=(heads + 2,),
            in_specs=attention_specs(slots, heads)
            + [pl.BlockSpec((slots, HEAD_SIZE), lambda h, o, n: (0, jnp.minimum(h, heads - 1)))],
            out_specs=pl.BlockSpec((slots, HEAD_SIZE), lambda h, o, n: (0, h)),
            scratch_shapes=[pltpu.VMEM((slots, HEAD_SIZE), bf16)] * 2
            + [pltpu.VMEM((slots, HEAD_SIZE), f32)] * 2,
        ),
        out_shape=jax.ShapeDtypeStruct((slots, (heads + 2) * HEAD_SIZE), bf16),
        cost_estimate=pl.CostEstimate(
            flops=7 * heads * slots * slots * HEAD_SIZE,
            transcendentals=heads * slots * slots,
            bytes_accessed=8 * slots * HEAD_SIZE * (heads + 2),
        ),
        compiler_params=pltpu.CompilerParams(vmem_limit_bytes=56 << 20),
    )(order, length, qkv, qkv, qkv, *tables, d_context)


def attention_products_kernel(g1_ref, context_ref, h_ref, d_qkv_ref, *refs):
    out_ref = refs[-1]
    cols = context_ref.shape[1]
    out_ref[:, :cols] = mm_rows(g1_ref[...], context_ref[...]).astype(bf16)
    out_ref[:, cols:] = mm_rows(h_ref[...], d_qkv_ref[...]).astype(bf16)


def attention_products(g1, context, h, d_qkv, *earlier):
    rows, width = g1.shape
    cols, more = context.shape[1], d_qkv.shape[1]
    tm = tile(width, 512)
    return pl.pallas_call(
        attention_products_kernel,
        name="attention_products",
        grid=(width // tm,),
        in_specs=[
            pl.BlockSpec((rows, tm), lambda i: (0, i)),
            pl.BlockSpec((rows, cols), lambda i: (0, 0)),
            pl.BlockSpec((rows, tm), lambda i: (0, i)),
            pl.BlockSpec((rows, more), lambda i: (0, 0)),
        ]
        + [pl.BlockSpec(memory_space=pl.ANY)] * len(earlier),
        out_specs=pl.BlockSpec((tm, cols + more), lambda i: (i, 0)),
        out_shape=jax.ShapeDtypeStruct((width, cols + more), bf16),
        cost_estimate=pl.CostEstimate(
            flops=2 * rows * width * (cols + more),
            transcendentals=0,
            bytes_accessed=4 * rows * width + 2 * (rows + width) * (cols + more),
        ),
        compiler_params=pltpu.CompilerParams(vmem_limit_bytes=56 << 20),
    )(g1, context, h, d_qkv, *earlier)


def prepare_kernel(order_ref, len_ref, x_ref, grad_ref, x_out, grad_out):
    size = x_ref.shape[0]
    first = order_ref[pl.program_id(0)] * size
    pos = first + lax.broadcasted_iota(jnp.int32, (size, 1), 0)
    x_out[...] = x_ref[...]
    grad_out[...] = jnp.where(pos < len_ref[0], grad_ref[...].astype(f32), 0.0).astype(bf16)


def prepare(order, length, x_in, cotangent):
    slots, width = x_in.shape
    size = slots // 4
    source = pl.BlockSpec((size, width), lambda i, o, n: (o[i], 0))
    target = pl.BlockSpec((size, width), lambda i, o, n: (i, 0))
    return pl.pallas_call(
        prepare_kernel,
        name="prepare",
        grid_spec=pltpu.PrefetchScalarGridSpec(
            num_scalar_prefetch=2, grid=(4,), in_specs=[source] * 2, out_specs=[target] * 2
        ),
        out_shape=[jax.ShapeDtypeStruct(x_in.shape, bf16)] * 2,
        cost_estimate=pl.CostEstimate(flops=0, transcendentals=0, bytes_accessed=8 * slots * width),
        compiler_params=pltpu.CompilerParams(vmem_limit_bytes=40 << 20),
    )(order, length, x_in, cotangent)


def spread_heads(block):
    mp_size = lax.axis_size("mp")
    rows, n, heads, part = block.shape
    send = jnp.repeat(block, mp_size // heads, axis=2)
    got = lax.all_to_all(send, "mp", 2, 2, tiled=True)
    return got.reshape(rows, n * mp_size * part)


def attention_end_kernel(heads, grads_ref, q_ref, kv_ref, gain_ref, sums_ref, out_ref, q_out_ref, send_ref):
    cols = q_ref.shape[1]
    size = kv_ref.shape[1] // 2
    part = size // send_ref.shape[0]
    out_ref[...] = grads_ref[:, :cols].astype(f32).T
    q_grad = grads_ref[:, cols : 2 * cols].astype(f32)
    q_out_ref[...] = q_grad
    kv_grad = grads_ref[:, 2 * cols :]
    products = jnp.sum(q_grad * q_ref[...].astype(f32), axis=1, keepdims=True) + jnp.sum(
        kv_grad.astype(f32) * kv_ref[...].astype(f32), axis=1, keepdims=True
    )
    rows = products.shape[0]
    lane = lax.broadcasted_iota(jnp.int32, (rows, 2 * part), 1)
    extra = jnp.zeros((rows, 2 * part), f32)
    for i, v in enumerate([products / gain_ref[...].astype(f32), sums_ref[...]]):
        high = v.astype(bf16).astype(f32)
        extra = jnp.where(lane == 2 * i, high, jnp.where(lane == 2 * i + 1, v - high, extra))
    for m in range(send_ref.shape[0]):
        for i in range(2):
            first = i * size + m * part
            send_ref[m, :, i * part : (i + 1) * part] = kv_grad[:, first : first + part]
        send_ref[m, :, 2 * part :] = extra.astype(bf16)


def attention_end(grads, query_weight, kv_block, gain, ffn_sums):
    rows, cols = query_weight.shape
    mp_size = lax.axis_size("mp")
    part = kv_block.shape[1] // 2 // mp_size
    return pl.pallas_call(
        functools.partial(attention_end_kernel, KEY_VALUE_HEADS),
        name="attention_end",
        out_shape=[
            jax.ShapeDtypeStruct((cols, rows), f32),
            jax.ShapeDtypeStruct((rows, cols), f32),
            jax.ShapeDtypeStruct((mp_size, rows, 4 * part), bf16),
        ],
        cost_estimate=pl.CostEstimate(
            flops=8 * rows * cols, transcendentals=0, bytes_accessed=20 * rows * cols
        ),
        compiler_params=pltpu.CompilerParams(vmem_limit_bytes=40 << 20),
    )(grads, query_weight, kv_block, gain.reshape(-1, 1), ffn_sums.reshape(-1, 1))


def collect_heads(send, heads):
    mp_size, rows, width = send.shape
    part = width // 4
    got = lax.all_to_all(send, "mp", 0, 0, tiled=True).astype(f32)
    kept = jnp.sum(got[:, :, : 2 * part].reshape(heads, mp_size // heads, rows, 2 * part), axis=1)
    extra = jnp.sum(got[:, :, 2 * part : 2 * part + 4], axis=0)
    kept = jnp.transpose(kept, (1, 0, 2))
    return kept[:, :, :part], kept[:, :, part:], extra[:, 0] + extra[:, 1], extra[:, 2] + extra[:, 3]


def gather_dp(block):
    return lax.all_gather(block, DP, axis=0, tiled=True)


def reduce_dp(block):
    return lax.psum_scatter(block, DP, scatter_dimension=0, tiled=True)


def gather_z(block):
    return lax.all_gather(block, "z", axis=0, tiled=True)


def reduce_z(block):
    return lax.psum_scatter(block, "z", scatter_dimension=0, tiled=True)


def to_core(block):
    rows, n, cols = block.shape
    core = lax.axis_index("core")
    m = cols // 2
    own = lax.dynamic_slice_in_dim(block, core * m, m, 2).reshape(rows, n * m)
    away = lax.dynamic_slice_in_dim(block, (1 - core) * m, m, 2).reshape(rows, n * m)
    got = send_core(away)
    return jnp.concatenate([jnp.where(core == 0, own, got), jnp.where(core == 0, got, own)])


def own_half_kernel(transpose, core_ref, own_ref, got_ref, *refs):
    out_ref = refs[-1]
    value = jnp.where(pl.program_id(0) == core_ref[0], own_ref[...].astype(f32), got_ref[...].astype(f32))
    out_ref[...] = value.T if transpose else value


def from_core(block, n, transpose=False, earlier=()):
    rows = block.shape[0] // 2
    m = block.shape[1] // n
    core = lax.axis_index("core").astype(jnp.int32)
    got = send_core(lax.dynamic_slice_in_dim(block, (1 - core) * rows, rows, 0))
    out_block = (m, rows) if transpose else (rows, m)
    out_shape = (2 * m, rows) if transpose else (rows, 2 * m)
    return [
        pl.pallas_call(
            functools.partial(own_half_kernel, transpose),
            name="own_half",
            grid_spec=pltpu.PrefetchScalarGridSpec(
                num_scalar_prefetch=1,
                grid=(2,),
                in_specs=[
                    pl.BlockSpec((rows, m), lambda h, c, i=i: (c[0], i)),
                    pl.BlockSpec((rows, m), lambda h, c, i=i: (0, i)),
                ]
                + [pl.BlockSpec(memory_space=pl.ANY)] * len(earlier),
                out_specs=pl.BlockSpec(out_block, lambda h, c: (h, 0) if transpose else (0, h)),
            ),
            out_shape=jax.ShapeDtypeStruct(out_shape, f32),
            cost_estimate=pl.CostEstimate(flops=0, transcendentals=0, bytes_accessed=12 * rows * m),
            compiler_params=pltpu.CompilerParams(vmem_limit_bytes=40 << 20),
        )(core.reshape(1), block, got, *earlier)
        for i in range(n)
    ]


def ffn_forward_kernel(mine_ref, away_ref, g_ref, u_ref, hidden_ref, factor_ref):
    def run(h_ref):
        h = h_ref[...]
        gate = jnp.dot(h, g_ref[...], preferred_element_type=f32)
        up = jnp.dot(h, u_ref[...], preferred_element_type=f32)
        sig = 1.0 / (1.0 + jnp.exp(-gate))
        silu = gate * sig
        hidden_ref[...] = (silu * up).astype(bf16)
        factor_ref[0] = (up * sig * (1.0 + gate - silu)).astype(bf16)
        factor_ref[1] = silu.astype(bf16)

    pl.when(pl.program_id(0) == 0)(lambda: run(mine_ref))
    pl.when(pl.program_id(0) == 1)(lambda: run(away_ref))


def ffn_forward(mine, away, w_gu):
    rows, width = mine.shape
    ff = w_gu.shape[1] // 2
    tn = tile(ff, 256)
    return pl.pallas_call(
        ffn_forward_kernel,
        name="ffn_forward",
        grid=(2, ff // tn),
        in_specs=[
            pl.BlockSpec((rows, width), lambda i, j: (0, 0)),
            pl.BlockSpec((rows, width), lambda i, j: (0, 0)),
            pl.BlockSpec((width, tn), lambda i, j: (0, j)),
            pl.BlockSpec((width, tn), lambda i, j: (0, j + ff // tn)),
        ],
        out_specs=[
            pl.BlockSpec((rows, tn), lambda i, j: (i, j)),
            pl.BlockSpec((2, rows, tn), lambda i, j: (0, i, j)),
        ],
        out_shape=[
            jax.ShapeDtypeStruct((2 * rows, ff), bf16),
            jax.ShapeDtypeStruct((2, 2 * rows, ff), bf16),
        ],
        cost_estimate=pl.CostEstimate(
            flops=8 * rows * width * ff,
            transcendentals=2 * rows * ff,
            bytes_accessed=4 * (rows * width + width * ff + 3 * rows * ff),
        ),
        compiler_params=pltpu.CompilerParams(vmem_limit_bytes=56 << 20),
    )(mine, away, w_gu, w_gu)


def rows_product_kernel(mine_ref, away_ref, right_mine_ref, right_away_ref, *refs):
    out_ref = refs[-1]
    cols = right_mine_ref.shape[2]
    for i in range(2):
        out_ref[:, i * cols : (i + 1) * cols] = (
            mm_rows(mine_ref[...], right_mine_ref[i]) + mm_rows(away_ref[...], right_away_ref[i])
        ).astype(bf16)


def rows_product(mine, away, right, start, share, into=None, earlier=()):
    rows, width = mine.shape
    cols = 2 * right.shape[2]
    tm = tile(width // 4, 256)
    steps = share * width // 4 // tm
    begin = start * width // 4 // tm
    more = ([] if into is None else [into]) + list(earlier)
    return pl.pallas_call(
        rows_product_kernel,
        name="rows_product",
        grid=(steps,),
        in_specs=[
            pl.BlockSpec((rows, tm), lambda i: (0, begin + i)),
            pl.BlockSpec((rows, tm), lambda i: (0, begin + i)),
            pl.BlockSpec((2, rows, cols // 2), lambda i: (0, 0, 0)),
            pl.BlockSpec((2, rows, cols // 2), lambda i: (0, 1, 0)),
        ]
        + [pl.BlockSpec(memory_space=pl.ANY)] * len(more),
        out_specs=pl.BlockSpec((tm, cols), lambda i: (begin + i, 0)),
        out_shape=jax.ShapeDtypeStruct((width, cols), bf16),
        input_output_aliases={} if into is None else {4: 0},
        cost_estimate=pl.CostEstimate(
            flops=4 * rows * width * cols * share // 4,
            transcendentals=0,
            bytes_accessed=(4 * rows * width + 2 * width * cols) * share // 4 + 4 * rows * cols,
        ),
        compiler_params=pltpu.CompilerParams(vmem_limit_bytes=56 << 20),
    )(mine, away, right, right, *more)


def ffn_backward_kernel(grad_ref, d_ref, factor_ref, earlier_ref, out_ref):
    d_hidden = mm(grad_ref[...], d_ref[...])
    for i in range(2):
        out_ref[i] = (d_hidden * factor_ref[i].astype(f32)).astype(bf16)


def ffn_backward(grad, w_d, factors, earlier):
    rows, width = grad.shape
    ff = w_d.shape[1]
    tm, tn = tile(rows, 1024), tile(ff, 256)
    return pl.pallas_call(
        ffn_backward_kernel,
        name="ffn_backward",
        grid=(rows // tm, ff // tn),
        in_specs=[
            pl.BlockSpec((tm, width), lambda i, j: (i, 0)),
            pl.BlockSpec((width, tn), lambda i, j: (0, j)),
            pl.BlockSpec((2, tm, tn), lambda i, j: (0, i, j)),
            pl.BlockSpec(memory_space=pl.ANY),
        ],
        out_specs=pl.BlockSpec((2, tm, tn), lambda i, j: (0, i, j)),
        out_shape=jax.ShapeDtypeStruct((2, rows, ff), bf16),
        cost_estimate=pl.CostEstimate(
            flops=2 * rows * width * ff, transcendentals=0, bytes_accessed=2 * (rows * width + width * ff + 4 * rows * ff)
        ),
        compiler_params=pltpu.CompilerParams(vmem_limit_bytes=56 << 20),
    )(grad, w_d, factors, earlier)


def local(
    x_in,
    lengths,
    gain_attn,
    query_weight,
    key_projection_matrix,
    value_projection_matrix,
    out_weight,
    gain_ffn,
    gate_weight,
    up_weight,
    down_weight,
    cotangent,
):
    _, slots, width = x_in.shape
    mp_size = lax.axis_size("mp")
    me = lax.axis_index("mp")
    q_cols = query_weight.shape[1]
    here = slots // mp_size
    quarter = slots // 4
    tables = rope_tables(slots, HEAD_SIZE)
    sequence_block, relative_place = block_orders()

    def own_rows(v):
        return v[:here] if square() else lax.dynamic_slice_in_dim(v, me * here, here, 0)

    x_rel, grad_mine = prepare(sequence_block, lengths, x_in[0], cotangent[0])
    kv_block = spread_heads(jnp.stack([key_projection_matrix, value_projection_matrix], axis=1))
    w_attn = gather_dp(jnp.concatenate([query_weight, kv_block, out_weight.T], axis=1))
    o_first = q_cols + 2 * HEAD_SIZE
    ffn_block = to_core(jnp.stack([gate_weight, up_weight, down_weight.T], axis=1))
    ff = ffn_block.shape[1] // 3
    w_gu = gather_z(ffn_block[:, : 2 * ff])
    w_d = gather_z(ffn_block[:, 2 * ff :])
    gains = lax.all_gather(jnp.stack([gain_attn, gain_ffn]), DP, axis=1, tiled=True).astype(f32)
    g_attn, g_ffn = gains[0], gains[1]

    tok = x_rel.astype(f32)
    r1 = lax.rsqrt(jnp.mean(tok * tok, axis=-1, keepdims=True) + eps_norm)
    h_attn = (tok * r1 * g_attn).astype(bf16)
    grad_all = jnp.concatenate([grad_mine, send_core(grad_mine)])
    qkv = column_product(h_attn, w_attn, 0, o_first, f32)
    context = attention_forward(relative_place, lengths, qkv, tables)

    attn_rows = scatter_rows(scatter_product(context, w_attn, o_first, slots))
    tok_here = own_rows(x_rel).astype(f32)
    mid = tok_here + attn_rows
    r2 = lax.rsqrt(jnp.mean(mid * mid, axis=-1, keepdims=True) + eps_norm)
    n2 = mid * r2
    h_mine = join_rows(exchange_rows((n2 * g_ffn).astype(bf16)), True)
    h_away = send_core(h_mine)

    hidden, factors = ffn_forward(h_mine, h_away, w_gu)
    down_grad = mm_rows(grad_all, hidden).astype(bf16)
    down_out = reduce_z(down_grad)

    ffn_away = away_product(hidden, w_d, slots, (down_grad,))
    ffn_add = send_core(ffn_away)
    d_gu = ffn_backward(grad_all, w_d, factors, ffn_away)
    ffn_pieces = scatter_product(hidden, w_d, 0, slots, ffn_add, (d_gu,))
    ffn_near = scatter_near(ffn_pieces)
    gu_grad = rows_product(h_mine, h_away, d_gu, 0, 2, earlier=(ffn_pieces[-1],))
    h2_away = away_product(d_gu, w_gu, slots, (gu_grad,))
    ffn_middle = scatter_middle(ffn_pieces, ffn_near)
    gu_grad = rows_product(h_mine, h_away, d_gu, 2, 2, gu_grad, (h2_away, *ffn_middle))
    gu_grad, down_out = tie(gu_grad, down_out)
    gu_out = reduce_z(gu_grad)
    h2_add = send_core(h2_away)
    ffn_far = scatter_far(ffn_middle)
    h2_pieces = list(scatter_product(d_gu, w_gu, 0, slots, earlier=(gu_grad,)))
    h2_pieces[0], h2_add = tie(h2_pieces[0], h2_add)
    h2_summed = add_away(h2_pieces, h2_add)
    h2_summed[-1], ffn_far = tie(h2_summed[-1], ffn_far)
    ffn_rows = scatter_end(ffn_pieces, ffn_near, ffn_far)
    h2_near = scatter_near(h2_summed)
    h2_far = scatter_far(scatter_middle(h2_summed, h2_near))
    kept, h2_own = (h2_pieces, h2_add) if square() else (h2_summed, None)
    g1, g1_block = rows_backward(kept, h2_near, h2_far, h2_own, mid, grad_mine, g_ffn)
    g1_low = join_rows(exchange_rows(g1_block), True)

    layer_block, g1_low = tie((mid + ffn_rows).astype(bf16), g1_low)
    layer_near = exchange_near(layer_block)
    d_context = column_product(g1_low, w_attn, o_first, q_cols, bf16)
    d_qkv = attention_backward(relative_place, lengths, qkv, tables, d_context)
    d_qkv, layer_near = tie(d_qkv, layer_near)
    layer_middle = exchange_middle(layer_near)
    layer_far = exchange_far(layer_middle)
    h1_pieces = list(scatter_product(d_qkv, w_attn, 0, slots))
    attn_grads = attention_products(g1_low, context, h_attn, d_qkv, h1_pieces[0])
    h1_pieces[-1], layer_far = tie(h1_pieces[-1], layer_far)
    layer_out = join_rows((layer_block, *layer_near, *layer_far), False)
    h1_near = scatter_near(h1_pieces)
    h1_near, layer_out, attn_grads = tie(h1_near, layer_out, attn_grads)
    attn_out = reduce_dp(attn_grads)
    h1_far = scatter_far(scatter_middle(h1_pieces, h1_near))
    _, grad_block = rows_backward(h1_pieces, h1_near, h1_far, None, x_rel, g1, g_attn)
    grad_pieces = list(exchange_rows(grad_block))
    grad_pieces[0], gu_out, down_out = tie(grad_pieces[0], gu_out, down_out)
    (down_out,) = from_core(down_out, 1, True)
    gate_out, up_out = from_core(gu_out, 2, earlier=(down_out,))

    rows_here = gain_attn.shape[0]

    ffn_sums = sum(
        jnp.sum(w.astype(f32) * g, axis=1) for w, g in [(gate_weight, gate_out), (up_weight, up_out)]
    ) / gain_ffn.astype(f32)
    if square():
        joined = join_near(grad_pieces[:3], f32)
        *far_pieces, attn_out, joined, ffn_sums = tie(*grad_pieces[3:], attn_out, joined, ffn_sums)
    out_out, q_out, send = attention_end(attn_out, query_weight, kv_block, gain_attn, ffn_sums)
    key_grad, value_grad, gain_attn_grad, gain_ffn_grad = collect_heads(send, KEY_VALUE_HEADS)
    if square():
        grad_input = join_far(far_pieces, joined)
    else:
        grad_input = grad_pieces[1].astype(f32)
    return (
        layer_out[None],
        grad_input[None],
        gain_attn_grad,
        q_out,
        key_grad,
        value_grad,
        out_out,
        gain_ffn_grad,
        gate_out,
        up_out,
        down_out,
    )


def solution(mesh):
    dp_size, mp_size = mesh.shape["dp"], mesh.shape["mp"]
    split = Mesh(mesh.devices.reshape(dp_size // 2, 2, mp_size), ("z", "core", "mp"))
    return jax.shard_map(
        local,
        mesh=split,
        in_specs=(
            P(DP, None, None),
            P(DP),
            P(DP),
            P(DP, "mp"),
            P(DP, None, "mp"),
            P(DP, None, "mp"),
            P("mp", DP),
            P(DP),
            P(DP, "mp"),
            P(DP, "mp"),
            P("mp", DP),
            P(DP, None, None),
        ),
        out_specs=(
            P(DP, None, None),
            P(DP, None, None),
            P(DP),
            P(DP, "mp"),
            P(DP, None, "mp"),
            P(DP, None, "mp"),
            P("mp", DP),
            P(DP),
            P(DP, "mp"),
            P(DP, "mp"),
            P("mp", DP),
        ),
        check_vma=False,
    )
```

```python
import functools

import jax
import jax.numpy as jnp
from jax import lax
from jax.experimental import pallas as pl
from jax.experimental.pallas import tpu as pltpu
from jax.sharding import Mesh, PartitionSpec as P

QUERY_HEADS = 8
KEY_VALUE_HEADS = 4
HEAD_SIZE = 256

eps_norm = 1e-06
rope_base = 1000042.0
neg_large = -1e30
bf16 = jnp.bfloat16
f32 = jnp.float32


def rope_tables(slot_length, size):
    half_size = size // 2
    inv_freq = rope_base ** (-(jnp.arange(half_size, dtype=f32) * 2.0 / size))
    angles = jnp.arange(slot_length, dtype=f32)[:, None] * inv_freq[None, :]
    return (jnp.cos(angles), jnp.sin(angles))


def rotate(values, cos_b, sin_b):
    half = values.shape[-1] // 2
    a, b = values[..., :half], values[..., half:]
    return jnp.concatenate([a * cos_b - b * sin_b, b * cos_b + a * sin_b], axis=-1)


def rotate_back(grads, cos_b, sin_b):
    half = grads.shape[-1] // 2
    a, b = grads[..., :half], grads[..., half:]
    return jnp.concatenate([a * cos_b + b * sin_b, b * cos_b - a * sin_b], axis=-1)


def mm(left, right):
    return lax.dot_general(left, right, (((1,), (0,)), ((), ())), preferred_element_type=f32)


def mm_t(left, right):
    return lax.dot_general(left, right, (((1,), (1,)), ((), ())), preferred_element_type=f32)


def mm_rows(left, right):
    return lax.dot_general(left, right, (((0,), (0,)), ((), ())), preferred_element_type=f32)


DP = ("z", "core")
OVER_X = [(0, 1), (1, 0), (2, 3), (3, 2)]
OVER_Y = [(0, 2), (2, 0), (1, 3), (3, 1)]
OVER_CORE = [(0, 1), (1, 0)]


def send_x(v):
    return lax.ppermute(v, "mp", OVER_X)


def send_y(v):
    return lax.ppermute(v, "mp", OVER_Y)


def send_core(v):
    return lax.ppermute(v, "core", OVER_CORE)


def square():
    return lax.axis_size("mp") == 4


def tie(*values):
    return lax.optimization_barrier(values)


def block_orders():
    steps = jnp.arange(4, dtype=jnp.int32)
    if not square():
        return steps, steps
    me = lax.axis_index("mp").astype(jnp.int32)
    away = jnp.bitwise_xor(me, steps)
    return jnp.bitwise_xor(me, jnp.array([0, 2, 1, 3], jnp.int32)), (away % 2) * 2 + away // 2


def tile(size, most):
    while size % most:
        most //= 2
    return most


def column_product_kernel(left_ref, right_ref, out_ref):
    out_ref[...] = mm(left_ref[...], right_ref[...]).astype(out_ref.dtype)


def column_product(left, right, first, cols, dtype):
    rows, depth = left.shape
    tn = tile(cols, 256)
    return pl.pallas_call(
        column_product_kernel,
        name="column_product",
        grid=(cols // tn,),
        in_specs=[
            pl.BlockSpec((rows, depth), lambda j: (0, 0)),
            pl.BlockSpec((depth, tn), lambda j: (0, first // tn + j)),
        ],
        out_specs=pl.BlockSpec((rows, tn), lambda j: (0, j)),
        out_shape=jax.ShapeDtypeStruct((rows, cols), dtype),
        cost_estimate=pl.CostEstimate(
            flops=2 * rows * depth * cols, transcendentals=0, bytes_accessed=2 * (rows + cols) * depth + 4 * rows * cols
        ),
        compiler_params=pltpu.CompilerParams(vmem_limit_bytes=56 << 20),
    )(left, right)


def transposed_product_kernel(groups, added, left_ref, right_ref, *refs):
    outs = refs[-sum(len(g) for g in groups) :]
    steps = pl.num_programs(0) // len(groups)
    if len(left_ref.shape) == 2:
        total = mm_t(left_ref[...], right_ref[...])
    else:
        depth = left_ref.shape[2]
        total = mm_t(left_ref[0], right_ref[:, :depth]) + mm_t(left_ref[1], right_ref[:, depth:])
    if added:
        total = total + refs[0][...].astype(f32)
    size = total.shape[0] // 4
    for i, group in enumerate(groups):

        @pl.when(pl.program_id(0) // steps == i)
        def _(first=sum(len(g) for g in groups[:i]), group=group):
            for out, blocks in zip(outs[first : first + len(group)], group):
                for place, block in enumerate(blocks):
                    part = total[block * size : (block + 1) * size]
                    out[place * size : (place + 1) * size] = part.astype(out.dtype)


def transposed_product(left, sequence, rows, right, first, groups, add=None, earlier=()):
    depth = left.shape[-1]
    pair = left.ndim == 3
    deep = 2 * depth if pair else depth
    cols = right.shape[0] // len(groups)
    tn = tile(cols, 512)
    steps = cols // tn
    size = rows // 4
    adds = [] if add is None else [add]

    def at(i):
        return lambda j: (0, jnp.clip(j - i * steps, 0, steps - 1))

    return pl.pallas_call(
        functools.partial(transposed_product_kernel, groups, add is not None),
        name="transposed_product",
        grid=(len(groups) * steps,),
        in_specs=[
            pl.BlockSpec((2, rows, depth), lambda j: (0, sequence, 0))
            if pair
            else pl.BlockSpec((rows, depth), lambda j: (sequence, 0)),
            pl.BlockSpec((tn, deep), lambda j: (j, first // deep)),
        ]
        + [pl.BlockSpec((rows, tn), lambda j: (0, j))] * len(adds)
        + [pl.BlockSpec(memory_space=pl.ANY)] * len(earlier),
        out_specs=[
            pl.BlockSpec((len(blocks) * size, tn), at(i))
            for i, group in enumerate(groups)
            for blocks in group
        ],
        out_shape=[
            jax.ShapeDtypeStruct((len(blocks) * size, cols), f32 if blocks == (0,) else bf16)
            for group in groups
            for blocks in group
        ],
        cost_estimate=pl.CostEstimate(
            flops=2 * rows * deep * right.shape[0],
            transcendentals=0,
            bytes_accessed=2 * (rows + right.shape[0]) * deep + 2 * rows * right.shape[0],
        ),
        compiler_params=pltpu.CompilerParams(vmem_limit_bytes=56 << 20),
    )(left, right, *adds, *earlier)


WHOLE = (((0, 1, 2, 3),),)
PIECES = (((0,), (1,), (2, 3)), ((0,), (2,), (1, 3)))


def away_product(left, right, rows, earlier=()):
    return transposed_product(left, 1, rows, right, 0, WHOLE, earlier=earlier)[0]


def scatter_product(left, right, first, rows, add=None, earlier=()):
    groups = PIECES if square() else WHOLE
    return transposed_product(left, 0, rows, right, first, groups, add, earlier)


def add_away(pieces, away):
    if not square():
        return [(pieces[0].astype(f32) + away.astype(f32)).astype(bf16)]
    size, half = pieces[1].shape
    away = away.reshape(2, 2, size, 2 * half)
    parts = [
        away[0, 0, :, :half],
        away[0, 1, :, :half],
        away[1, :, :, :half].reshape(2 * size, half),
        away[0, 0, :, half:],
        away[1, 0, :, half:],
        away[:, 1, :, half:].reshape(2 * size, half),
    ]
    return [
        (piece.astype(f32) + part.astype(f32)).astype(piece.dtype) for piece, part in zip(pieces, parts)
    ]


def scatter_near(pieces):
    if not square():
        return ()
    return send_x(pieces[2]), send_y(pieces[5])


def scatter_middle(pieces, near):
    if not square():
        return ()
    own_a, y_a, _, own_b, x_b, _ = pieces
    size = own_a.shape[0]
    return (
        (y_a.astype(f32) + near[0][size:].astype(f32)).astype(bf16),
        (x_b.astype(f32) + near[1][size:].astype(f32)).astype(bf16),
    )


def scatter_far(middle):
    if not square():
        return ()
    return send_y(middle[0]), send_x(middle[1])


def scatter_end(pieces, near, far):
    if not square():
        return lax.psum_scatter(pieces[0], "mp", scatter_dimension=0, tiled=True).astype(f32)
    size = pieces[0].shape[0]
    kept = [
        own + got[:size].astype(f32) + last.astype(f32)
        for own, got, last in zip((pieces[0], pieces[3]), near, far)
    ]
    return jnp.concatenate(kept, axis=1)


def scatter_rows(pieces):
    near = scatter_near(pieces)
    return scatter_end(pieces, near, scatter_far(scatter_middle(pieces, near)))


def rows_backward_kernel(added, *refs):
    own, got, last = refs[0:2], refs[2:4], refs[4:6]
    v_ref, base_ref, gain_ref = refs[6 + added : 9 + added]
    g_ref, low_ref = refs[9 + added :]
    half = own[0].shape[1]
    width = 2 * half
    v = v_ref[...].astype(f32)
    r = lax.rsqrt(jnp.sum(v * v, axis=-1, keepdims=True) * (1.0 / width) + eps_norm)
    n = v * r
    parts = []
    for i in range(2):
        columns = slice(i * half, (i + 1) * half)
        d = own[i][...] + got[i][...].astype(f32) + last[i][...].astype(f32)
        if added:
            d = d + refs[6][:, columns].astype(f32)
        parts.append(d * gain_ref[:, columns])
    e = jnp.concatenate(parts, axis=1)
    inner = jnp.sum(e * n, axis=-1, keepdims=True) * (1.0 / width)
    g = base_ref[...].astype(f32) + r * (e - n * inner)
    g_ref[...] = g
    low_ref[...] = g.astype(bf16)


def rows_backward(pieces, near, far, away, v, base, gain):
    if not square():
        here = pieces[0].shape[0] // lax.axis_size("mp")
        d = scatter_end(pieces, near, far)

        def own(u):
            if u.shape[0] == here:
                return u
            return lax.dynamic_slice_in_dim(u, lax.axis_index("mp") * here, here, 0)

        v, base = own(v).astype(f32), own(base).astype(f32)
        r = lax.rsqrt(jnp.mean(v * v, axis=-1, keepdims=True) + eps_norm)
        n, e = v * r, d * gain
        g = base + r * (e - n * jnp.mean(e * n, axis=-1, keepdims=True))
        return g, g.astype(bf16)
    here, half = pieces[0].shape
    tm = tile(here, 64)
    narrow = pl.BlockSpec((tm, half), lambda i: (i, 0))
    wide = pl.BlockSpec((tm, 2 * half), lambda i: (i, 0))
    adds = [] if away is None else [away]
    return pl.pallas_call(
        functools.partial(rows_backward_kernel, len(adds)),
        name="rows_backward",
        grid=(here // tm,),
        in_specs=[narrow] * 6
        + [wide] * (len(adds) + 2)
        + [pl.BlockSpec((1, 2 * half), lambda i: (0, 0))],
        out_specs=[wide, wide],
        out_shape=[
            jax.ShapeDtypeStruct((here, 2 * half), f32),
            jax.ShapeDtypeStruct((here, 2 * half), bf16),
        ],
        cost_estimate=pl.CostEstimate(
            flops=40 * here * half, transcendentals=here, bytes_accessed=40 * here * half
        ),
        compiler_params=pltpu.CompilerParams(vmem_limit_bytes=40 << 20),
    )(pieces[0], pieces[3], *near, *far, *adds, v, base, gain.reshape(1, -1))


def assemble_kernel(order_ref, own, over_x, over_y, diag_a, diag_b, out_ref):
    half = diag_a.shape[1]
    for i, ref in enumerate([own, over_y, over_x]):

        @pl.when(pl.program_id(0) == i)
        def _(ref=ref):
            out_ref[...] = ref[...].astype(out_ref.dtype)

    @pl.when(pl.program_id(0) == 3)
    def _():
        out_ref[:, :half] = diag_a[...].astype(out_ref.dtype)
        out_ref[:, half:] = diag_b[...].astype(out_ref.dtype)


def assemble(order, pieces, dtype):
    here, width = pieces[0].shape
    return pl.pallas_call(
        assemble_kernel,
        name="assemble",
        grid_spec=pltpu.PrefetchScalarGridSpec(
            num_scalar_prefetch=1,
            grid=(4,),
            in_specs=[pl.BlockSpec((here, piece.shape[1]), lambda i, s: (0, 0)) for piece in pieces],
            out_specs=pl.BlockSpec((here, width), lambda i, s: (s[i], 0)),
        ),
        out_shape=jax.ShapeDtypeStruct((4 * here, width), dtype),
        cost_estimate=pl.CostEstimate(flops=0, transcendentals=0, bytes_accessed=20 * here * width),
        compiler_params=pltpu.CompilerParams(vmem_limit_bytes=40 << 20),
    )(order, *pieces)


def join_near_kernel(order_ref, own, over_x, over_y, out_ref):
    for i, ref in enumerate([own, over_y, over_x]):

        @pl.when(pl.program_id(0) == i)
        def _(ref=ref):
            out_ref[...] = ref[...].astype(out_ref.dtype)


def join_far_kernel(order_ref, diag_a, diag_b, near_ref, out_ref):
    half = diag_a.shape[1]
    out_ref[:, :half] = diag_a[...].astype(out_ref.dtype)
    out_ref[:, half:] = diag_b[...].astype(out_ref.dtype)


def join_near(pieces, dtype):
    here, width = pieces[0].shape
    return pl.pallas_call(
        join_near_kernel,
        name="join_near",
        grid_spec=pltpu.PrefetchScalarGridSpec(
            num_scalar_prefetch=1,
            grid=(3,),
            in_specs=[pl.BlockSpec((here, width), lambda i, s: (0, 0))] * 3,
            out_specs=pl.BlockSpec((here, width), lambda i, s: (s[i], 0)),
        ),
        out_shape=jax.ShapeDtypeStruct((4 * here, width), dtype),
        cost_estimate=pl.CostEstimate(flops=0, transcendentals=0, bytes_accessed=18 * here * width),
        compiler_params=pltpu.CompilerParams(vmem_limit_bytes=40 << 20),
    )(block_orders()[0], *pieces)


def join_far(pieces, near):
    here, half = pieces[0].shape
    return pl.pallas_call(
        join_far_kernel,
        name="join_far",
        grid_spec=pltpu.PrefetchScalarGridSpec(
            num_scalar_prefetch=1,
            grid=(1,),
            in_specs=[pl.BlockSpec((here, half), lambda i, s: (0, 0))] * 2
            + [pl.BlockSpec(memory_space=pl.ANY)],
            out_specs=pl.BlockSpec((here, 2 * half), lambda i, s: (s[3], 0)),
        ),
        out_shape=jax.ShapeDtypeStruct(near.shape, near.dtype),
        input_output_aliases={3: 0},
        cost_estimate=pl.CostEstimate(flops=0, transcendentals=0, bytes_accessed=12 * here * half),
        compiler_params=pltpu.CompilerParams(vmem_limit_bytes=40 << 20),
    )(block_orders()[0], *pieces, near)


def exchange_near(block):
    if not square():
        return (lax.all_gather(block, "mp", axis=0, tiled=True),)
    return send_x(block), send_y(block)


def exchange_middle(near):
    if not square():
        return ()
    half = near[0].shape[1] // 2
    return near[1][:, :half], near[0][:, half:]


def exchange_far(middle):
    if not square():
        return ()
    return send_x(middle[0]), send_y(middle[1])


def exchange_rows(block):
    near = exchange_near(block)
    return (block, *near, *exchange_far(exchange_middle(near)))


def join_rows(pieces, relative, dtype=bf16):
    if not square():
        return pieces[1].astype(dtype)
    order = jnp.arange(4, dtype=jnp.int32) if relative else block_orders()[0]
    return assemble(order, pieces, dtype)


SHORTEST = 512
FACTOR = HEAD_SIZE ** (-0.5)


def probabilities(queries, keys, i, size, seq_len):
    scores = mm_t(queries, keys)
    first = min(i * size, SHORTEST)
    shape = (size, (i + 1) * size - first)
    q_pos = i * size + lax.broadcasted_iota(jnp.int32, shape, 0)
    k_pos = first + lax.broadcasted_iota(jnp.int32, shape, 1)
    seen = jnp.where((k_pos <= q_pos) & (k_pos < seq_len), scores[:, first:], neg_large)
    if first:
        seen = jnp.concatenate([scores[:, :first], seen], axis=1)
    exps = jnp.exp(seen - jnp.max(seen, axis=-1, keepdims=True))
    return exps * (1.0 / jnp.sum(exps, axis=-1, keepdims=True))


def block_rows(order_ref, i, size):
    return pl.ds(pl.multiple_of(order_ref[i] * size, size), size)


def load_keys(order_ref, k_ref, v_ref, cos_ref, sin_ref, keys, values, size):
    for i in range(keys.shape[0] // size):
        rows = block_rows(order_ref, i, size)
        here = pl.ds(i * size, size)
        keys[here] = rotate(k_ref[rows], cos_ref[here], sin_ref[here]).astype(bf16)
        values[here] = v_ref[rows].astype(bf16)


def attention_forward_kernel(
    order_ref, len_ref, q_ref, k_ref, v_ref, cos_ref, sin_ref, out_ref, keys, values
):
    blocks = order_ref.shape[0]
    size = keys.shape[0] // blocks
    seq_len = len_ref[0]

    @pl.when(pl.program_id(0) == 0)
    def _():
        load_keys(order_ref, k_ref, v_ref, cos_ref, sin_ref, keys, values, size)

    for i in range(blocks):
        rows = block_rows(order_ref, i, size)
        here = pl.ds(i * size, size)
        upto = (i + 1) * size
        queries = (FACTOR * rotate(q_ref[rows], cos_ref[here], sin_ref[here])).astype(bf16)
        probs = probabilities(queries, keys[:upto], i, size, seq_len).astype(bf16)
        out_ref[rows] = mm(probs, values[:upto]).astype(bf16)


def attention_backward_kernel(
    order_ref, len_ref, q_ref, k_ref, v_ref, cos_ref, sin_ref, g_ref, out_ref, keys, values, d_keys, d_values
):
    blocks = order_ref.shape[0]
    size = keys.shape[0] // blocks
    seq_len = len_ref[0]
    step = pl.program_id(0)
    heads = pl.num_programs(0) - 2

    @pl.when(step == 0)
    def _():
        load_keys(order_ref, k_ref, v_ref, cos_ref, sin_ref, keys, values, size)
        d_keys[...] = jnp.zeros_like(d_keys)
        d_values[...] = jnp.zeros_like(d_values)

    @pl.when(step < heads)
    def _():
        for i in range(blocks):
            rows = block_rows(order_ref, i, size)
            here = pl.ds(i * size, size)
            upto = (i + 1) * size
            cos_b, sin_b = cos_ref[here], sin_ref[here]
            queries = (FACTOR * rotate(q_ref[rows], cos_b, sin_b)).astype(bf16)
            grads = g_ref[rows]
            probs = probabilities(queries, keys[:upto], i, size, seq_len)
            d_values[:upto] += mm_rows(probs.astype(bf16), grads)
            d_probs = mm_t(grads, values[:upto])
            inner = jnp.sum(probs * d_probs, axis=-1, keepdims=True)
            d_scores = (probs * (d_probs - inner)).astype(bf16)
            d_keys[:upto] += mm_rows(d_scores, queries)
            d_queries = FACTOR * mm(d_scores, keys[:upto])
            out_ref[rows] = rotate_back(d_queries, cos_b, sin_b).astype(bf16)

    @pl.when(step == heads)
    def _():
        for i in range(blocks):
            here = pl.ds(i * size, size)
            out_ref[block_rows(order_ref, i, size)] = rotate_back(
                d_keys[here], cos_ref[here], sin_ref[here]
            ).astype(bf16)

    @pl.when(step == heads + 1)
    def _():
        for i in range(blocks):
            out_ref[block_rows(order_ref, i, size)] = d_values[pl.ds(i * size, size)].astype(bf16)


def attention_specs(slots, heads):
    half = HEAD_SIZE // 2
    return [
        pl.BlockSpec((slots, HEAD_SIZE), lambda h, o, n: (0, jnp.minimum(h, heads - 1))),
        pl.BlockSpec((slots, HEAD_SIZE), lambda h, o, n: (0, heads)),
        pl.BlockSpec((slots, HEAD_SIZE), lambda h, o, n: (0, heads + 1)),
        pl.BlockSpec((slots, half), lambda h, o, n: (0, 0)),
        pl.BlockSpec((slots, half), lambda h, o, n: (0, 0)),
    ]


def attention_forward(order, length, qkv, tables):
    slots = qkv.shape[0]
    heads = qkv.shape[1] // HEAD_SIZE - 2
    return pl.pallas_call(
        attention_forward_kernel,
        name="attention_forward",
        grid_spec=pltpu.PrefetchScalarGridSpec(
            num_scalar_prefetch=2,
            grid=(heads,),
            in_specs=attention_specs(slots, heads),
            out_specs=pl.BlockSpec((slots, HEAD_SIZE), lambda h, o, n: (0, h)),
            scratch_shapes=[pltpu.VMEM((slots, HEAD_SIZE), bf16)] * 2,
        ),
        out_shape=jax.ShapeDtypeStruct((slots, heads * HEAD_SIZE), bf16),
        cost_estimate=pl.CostEstimate(
            flops=3 * heads * slots * slots * HEAD_SIZE,
            transcendentals=heads * slots * slots,
            bytes_accessed=8 * slots * HEAD_SIZE * (heads + 2),
        ),
        compiler_params=pltpu.CompilerParams(vmem_limit_bytes=56 << 20),
    )(order, length, qkv, qkv, qkv, *tables)


def attention_backward(order, length, qkv, tables, d_context):
    slots = qkv.shape[0]
    heads = qkv.shape[1] // HEAD_SIZE - 2
    return pl.pallas_call(
        attention_backward_kernel,
        name="attention_backward",
        grid_spec=pltpu.PrefetchScalarGridSpec(
            num_scalar_prefetch=2,
            grid=(heads + 2,),
            in_specs=attention_specs(slots, heads)
            + [pl.BlockSpec((slots, HEAD_SIZE), lambda h, o, n: (0, jnp.minimum(h, heads - 1)))],
            out_specs=pl.BlockSpec((slots, HEAD_SIZE), lambda h, o, n: (0, h)),
            scratch_shapes=[pltpu.VMEM((slots, HEAD_SIZE), bf16)] * 2
            + [pltpu.VMEM((slots, HEAD_SIZE), f32)] * 2,
        ),
        out_shape=jax.ShapeDtypeStruct((slots, (heads + 2) * HEAD_SIZE), bf16),
        cost_estimate=pl.CostEstimate(
            flops=7 * heads * slots * slots * HEAD_SIZE,
            transcendentals=heads * slots * slots,
            bytes_accessed=8 * slots * HEAD_SIZE * (heads + 2),
        ),
        compiler_params=pltpu.CompilerParams(vmem_limit_bytes=56 << 20),
    )(order, length, qkv, qkv, qkv, *tables, d_context)


def attention_products_kernel(g1_ref, context_ref, h_ref, d_qkv_ref, *refs):
    out_ref = refs[-1]
    cols = context_ref.shape[1]
    out_ref[:, :cols] = mm_rows(g1_ref[...], context_ref[...]).astype(bf16)
    out_ref[:, cols:] = mm_rows(h_ref[...], d_qkv_ref[...]).astype(bf16)


def attention_products(g1, context, h, d_qkv, *earlier):
    rows, width = g1.shape
    cols, more = context.shape[1], d_qkv.shape[1]
    tm = tile(width, 512)
    return pl.pallas_call(
        attention_products_kernel,
        name="attention_products",
        grid=(width // tm,),
        in_specs=[
            pl.BlockSpec((rows, tm), lambda i: (0, i)),
            pl.BlockSpec((rows, cols), lambda i: (0, 0)),
            pl.BlockSpec((rows, tm), lambda i: (0, i)),
            pl.BlockSpec((rows, more), lambda i: (0, 0)),
        ]
        + [pl.BlockSpec(memory_space=pl.ANY)] * len(earlier),
        out_specs=pl.BlockSpec((tm, cols + more), lambda i: (i, 0)),
        out_shape=jax.ShapeDtypeStruct((width, cols + more), bf16),
        cost_estimate=pl.CostEstimate(
            flops=2 * rows * width * (cols + more),
            transcendentals=0,
            bytes_accessed=4 * rows * width + 2 * (rows + width) * (cols + more),
        ),
        compiler_params=pltpu.CompilerParams(vmem_limit_bytes=56 << 20),
    )(g1, context, h, d_qkv, *earlier)


def prepare_kernel(order_ref, len_ref, x_ref, grad_ref, x_out, grad_out):
    size = x_ref.shape[0]
    first = order_ref[pl.program_id(0)] * size
    pos = first + lax.broadcasted_iota(jnp.int32, (size, 1), 0)
    x_out[...] = x_ref[...]
    grad_out[...] = jnp.where(pos < len_ref[0], grad_ref[...].astype(f32), 0.0).astype(bf16)


def prepare(order, length, x_in, cotangent):
    slots, width = x_in.shape
    size = slots // 4
    source = pl.BlockSpec((size, width), lambda i, o, n: (o[i], 0))
    target = pl.BlockSpec((size, width), lambda i, o, n: (i, 0))
    return pl.pallas_call(
        prepare_kernel,
        name="prepare",
        grid_spec=pltpu.PrefetchScalarGridSpec(
            num_scalar_prefetch=2, grid=(4,), in_specs=[source] * 2, out_specs=[target] * 2
        ),
        out_shape=[jax.ShapeDtypeStruct(x_in.shape, bf16)] * 2,
        cost_estimate=pl.CostEstimate(flops=0, transcendentals=0, bytes_accessed=8 * slots * width),
        compiler_params=pltpu.CompilerParams(vmem_limit_bytes=40 << 20),
    )(order, length, x_in, cotangent)


def spread_heads(block):
    mp_size = lax.axis_size("mp")
    rows, n, heads, part = block.shape
    send = jnp.repeat(block, mp_size // heads, axis=2)
    got = lax.all_to_all(send, "mp", 2, 2, tiled=True)
    return got.reshape(rows, n * mp_size * part)


def attention_end_kernel(heads, grads_ref, q_ref, kv_ref, gain_ref, sums_ref, out_ref, q_out_ref, send_ref):
    cols = q_ref.shape[1]
    size = kv_ref.shape[1] // 2
    part = size // send_ref.shape[0]
    out_ref[...] = grads_ref[:, :cols].astype(f32).T
    q_grad = grads_ref[:, cols : 2 * cols].astype(f32)
    q_out_ref[...] = q_grad
    kv_grad = grads_ref[:, 2 * cols :]
    products = jnp.sum(q_grad * q_ref[...].astype(f32), axis=1, keepdims=True) + jnp.sum(
        kv_grad.astype(f32) * kv_ref[...].astype(f32), axis=1, keepdims=True
    )
    rows = products.shape[0]
    lane = lax.broadcasted_iota(jnp.int32, (rows, 2 * part), 1)
    extra = jnp.zeros((rows, 2 * part), f32)
    for i, v in enumerate([products / gain_ref[...].astype(f32), sums_ref[...]]):
        high = v.astype(bf16).astype(f32)
        extra = jnp.where(lane == 2 * i, high, jnp.where(lane == 2 * i + 1, v - high, extra))
    for m in range(send_ref.shape[0]):
        for i in range(2):
            first = i * size + m * part
            send_ref[m, :, i * part : (i + 1) * part] = kv_grad[:, first : first + part]
        send_ref[m, :, 2 * part :] = extra.astype(bf16)


def attention_end(grads, query_weight, kv_block, gain, ffn_sums):
    rows, cols = query_weight.shape
    mp_size = lax.axis_size("mp")
    part = kv_block.shape[1] // 2 // mp_size
    return pl.pallas_call(
        functools.partial(attention_end_kernel, KEY_VALUE_HEADS),
        name="attention_end",
        out_shape=[
            jax.ShapeDtypeStruct((cols, rows), f32),
            jax.ShapeDtypeStruct((rows, cols), f32),
            jax.ShapeDtypeStruct((mp_size, rows, 4 * part), bf16),
        ],
        cost_estimate=pl.CostEstimate(
            flops=8 * rows * cols, transcendentals=0, bytes_accessed=20 * rows * cols
        ),
        compiler_params=pltpu.CompilerParams(vmem_limit_bytes=40 << 20),
    )(grads, query_weight, kv_block, gain.reshape(-1, 1), ffn_sums.reshape(-1, 1))


def collect_heads(send, heads):
    mp_size, rows, width = send.shape
    part = width // 4
    got = lax.all_to_all(send, "mp", 0, 0, tiled=True).astype(f32)
    kept = jnp.sum(got[:, :, : 2 * part].reshape(heads, mp_size // heads, rows, 2 * part), axis=1)
    extra = jnp.sum(got[:, :, 2 * part : 2 * part + 4], axis=0)
    kept = jnp.transpose(kept, (1, 0, 2))
    return kept[:, :, :part], kept[:, :, part:], extra[:, 0] + extra[:, 1], extra[:, 2] + extra[:, 3]


def gather_dp(block):
    return lax.all_gather(block, DP, axis=0, tiled=True)


def reduce_dp(block):
    return lax.psum_scatter(block, DP, scatter_dimension=0, tiled=True)


def gather_z(block):
    return lax.all_gather(block, "z", axis=0, tiled=True)


def reduce_z(block):
    return lax.psum_scatter(block, "z", scatter_dimension=0, tiled=True)


def to_core(block):
    rows, n, cols = block.shape
    core = lax.axis_index("core")
    m = cols // 2
    own = lax.dynamic_slice_in_dim(block, core * m, m, 2).reshape(rows, n * m)
    away = lax.dynamic_slice_in_dim(block, (1 - core) * m, m, 2).reshape(rows, n * m)
    got = send_core(away)
    return jnp.concatenate([jnp.where(core == 0, own, got), jnp.where(core == 0, got, own)])


def own_half_kernel(transpose, core_ref, own_ref, got_ref, *refs):
    out_ref = refs[-1]
    value = jnp.where(pl.program_id(0) == core_ref[0], own_ref[...].astype(f32), got_ref[...].astype(f32))
    out_ref[...] = value.T if transpose else value


def from_core(block, n, transpose=False, earlier=()):
    rows = block.shape[0] // 2
    m = block.shape[1] // n
    core = lax.axis_index("core").astype(jnp.int32)
    got = send_core(lax.dynamic_slice_in_dim(block, (1 - core) * rows, rows, 0))
    out_block = (m, rows) if transpose else (rows, m)
    out_shape = (2 * m, rows) if transpose else (rows, 2 * m)
    return [
        pl.pallas_call(
            functools.partial(own_half_kernel, transpose),
            name="own_half",
            grid_spec=pltpu.PrefetchScalarGridSpec(
                num_scalar_prefetch=1,
                grid=(2,),
                in_specs=[
                    pl.BlockSpec((rows, m), lambda h, c, i=i: (c[0], i)),
                    pl.BlockSpec((rows, m), lambda h, c, i=i: (0, i)),
                ]
                + [pl.BlockSpec(memory_space=pl.ANY)] * len(earlier),
                out_specs=pl.BlockSpec(out_block, lambda h, c: (h, 0) if transpose else (0, h)),
            ),
            out_shape=jax.ShapeDtypeStruct(out_shape, f32),
            cost_estimate=pl.CostEstimate(flops=0, transcendentals=0, bytes_accessed=12 * rows * m),
            compiler_params=pltpu.CompilerParams(vmem_limit_bytes=40 << 20),
        )(core.reshape(1), block, got, *earlier)
        for i in range(n)
    ]


def ffn_forward_kernel(mine_ref, away_ref, g_ref, u_ref, hidden_ref, factor_ref):
    def run(h_ref):
        h = h_ref[...]
        gate = jnp.dot(h, g_ref[...], preferred_element_type=f32)
        up = jnp.dot(h, u_ref[...], preferred_element_type=f32)
        sig = 1.0 / (1.0 + jnp.exp(-gate))
        silu = gate * sig
        hidden_ref[...] = (silu * up).astype(bf16)
        factor_ref[0] = (up * sig * (1.0 + gate - silu)).astype(bf16)
        factor_ref[1] = silu.astype(bf16)

    pl.when(pl.program_id(0) == 0)(lambda: run(mine_ref))
    pl.when(pl.program_id(0) == 1)(lambda: run(away_ref))


def ffn_forward(mine, away, w_gu):
    rows, width = mine.shape
    ff = w_gu.shape[1] // 2
    tn = tile(ff, 256)
    return pl.pallas_call(
        ffn_forward_kernel,
        name="ffn_forward",
        grid=(2, ff // tn),
        in_specs=[
            pl.BlockSpec((rows, width), lambda i, j: (0, 0)),
            pl.BlockSpec((rows, width), lambda i, j: (0, 0)),
            pl.BlockSpec((width, tn), lambda i, j: (0, j)),
            pl.BlockSpec((width, tn), lambda i, j: (0, j + ff // tn)),
        ],
        out_specs=[
            pl.BlockSpec((rows, tn), lambda i, j: (i, j)),
            pl.BlockSpec((2, rows, tn), lambda i, j: (0, i, j)),
        ],
        out_shape=[
            jax.ShapeDtypeStruct((2 * rows, ff), bf16),
            jax.ShapeDtypeStruct((2, 2 * rows, ff), bf16),
        ],
        cost_estimate=pl.CostEstimate(
            flops=8 * rows * width * ff,
            transcendentals=2 * rows * ff,
            bytes_accessed=4 * (rows * width + width * ff + 3 * rows * ff),
        ),
        compiler_params=pltpu.CompilerParams(vmem_limit_bytes=56 << 20),
    )(mine, away, w_gu, w_gu)


def rows_product_kernel(mine_ref, away_ref, right_mine_ref, right_away_ref, *refs):
    out_ref = refs[-1]
    cols = right_mine_ref.shape[2]
    for i in range(2):
        out_ref[:, i * cols : (i + 1) * cols] = (
            mm_rows(mine_ref[...], right_mine_ref[i]) + mm_rows(away_ref[...], right_away_ref[i])
        ).astype(bf16)


def rows_product(mine, away, right, start, share, into=None, earlier=()):
    rows, width = mine.shape
    cols = 2 * right.shape[2]
    tm = tile(width // 4, 256)
    steps = share * width // 4 // tm
    begin = start * width // 4 // tm
    more = ([] if into is None else [into]) + list(earlier)
    return pl.pallas_call(
        rows_product_kernel,
        name="rows_product",
        grid=(steps,),
        in_specs=[
            pl.BlockSpec((rows, tm), lambda i: (0, begin + i)),
            pl.BlockSpec((rows, tm), lambda i: (0, begin + i)),
            pl.BlockSpec((2, rows, cols // 2), lambda i: (0, 0, 0)),
            pl.BlockSpec((2, rows, cols // 2), lambda i: (0, 1, 0)),
        ]
        + [pl.BlockSpec(memory_space=pl.ANY)] * len(more),
        out_specs=pl.BlockSpec((tm, cols), lambda i: (begin + i, 0)),
        out_shape=jax.ShapeDtypeStruct((width, cols), bf16),
        input_output_aliases={} if into is None else {4: 0},
        cost_estimate=pl.CostEstimate(
            flops=4 * rows * width * cols * share // 4,
            transcendentals=0,
            bytes_accessed=(4 * rows * width + 2 * width * cols) * share // 4 + 4 * rows * cols,
        ),
        compiler_params=pltpu.CompilerParams(vmem_limit_bytes=56 << 20),
    )(mine, away, right, right, *more)


def ffn_backward_kernel(grad_ref, d_ref, factor_ref, earlier_ref, out_ref):
    d_hidden = mm(grad_ref[...], d_ref[...])
    for i in range(2):
        out_ref[i] = (d_hidden * factor_ref[i].astype(f32)).astype(bf16)


def ffn_backward(grad, w_d, factors, earlier):
    rows, width = grad.shape
    ff = w_d.shape[1]
    tm, tn = tile(rows, 1024), tile(ff, 256)
    return pl.pallas_call(
        ffn_backward_kernel,
        name="ffn_backward",
        grid=(rows // tm, ff // tn),
        in_specs=[
            pl.BlockSpec((tm, width), lambda i, j: (i, 0)),
            pl.BlockSpec((width, tn), lambda i, j: (0, j)),
            pl.BlockSpec((2, tm, tn), lambda i, j: (0, i, j)),
            pl.BlockSpec(memory_space=pl.ANY),
        ],
        out_specs=pl.BlockSpec((2, tm, tn), lambda i, j: (0, i, j)),
        out_shape=jax.ShapeDtypeStruct((2, rows, ff), bf16),
        cost_estimate=pl.CostEstimate(
            flops=2 * rows * width * ff, transcendentals=0, bytes_accessed=2 * (rows * width + width * ff + 4 * rows * ff)
        ),
        compiler_params=pltpu.CompilerParams(vmem_limit_bytes=56 << 20),
    )(grad, w_d, factors, earlier)


def local(
    x_in,
    lengths,
    gain_attn,
    query_weight,
    key_projection_matrix,
    value_projection_matrix,
    out_weight,
    gain_ffn,
    gate_weight,
    up_weight,
    down_weight,
    cotangent,
):
    _, slots, width = x_in.shape
    mp_size = lax.axis_size("mp")
    me = lax.axis_index("mp")
    q_cols = query_weight.shape[1]
    here = slots // mp_size
    quarter = slots // 4
    tables = rope_tables(slots, HEAD_SIZE)
    sequence_block, relative_place = block_orders()

    def own_rows(v):
        return v[:here] if square() else lax.dynamic_slice_in_dim(v, me * here, here, 0)

    x_rel, grad_mine = prepare(sequence_block, lengths, x_in[0], cotangent[0])
    kv_block = spread_heads(jnp.stack([key_projection_matrix, value_projection_matrix], axis=1))
    w_attn = gather_dp(jnp.concatenate([query_weight, kv_block, out_weight.T], axis=1))
    o_first = q_cols + 2 * HEAD_SIZE
    ffn_block = to_core(jnp.stack([gate_weight, up_weight, down_weight.T], axis=1))
    ff = ffn_block.shape[1] // 3
    w_gu = gather_z(ffn_block[:, : 2 * ff])
    w_d = gather_z(ffn_block[:, 2 * ff :])
    gains = lax.all_gather(jnp.stack([gain_attn, gain_ffn]), DP, axis=1, tiled=True).astype(f32)
    g_attn, g_ffn = gains[0], gains[1]

    tok = x_rel.astype(f32)
    r1 = lax.rsqrt(jnp.mean(tok * tok, axis=-1, keepdims=True) + eps_norm)
    h_attn = (tok * r1 * g_attn).astype(bf16)
    grad_all = jnp.concatenate([grad_mine, send_core(grad_mine)])
    qkv = column_product(h_attn, w_attn, 0, o_first, f32)
    context = attention_forward(relative_place, lengths, qkv, tables)

    attn_rows = scatter_rows(scatter_product(context, w_attn, o_first, slots))
    tok_here = own_rows(x_rel).astype(f32)
    mid = tok_here + attn_rows
    r2 = lax.rsqrt(jnp.mean(mid * mid, axis=-1, keepdims=True) + eps_norm)
    n2 = mid * r2
    h_mine = join_rows(exchange_rows((n2 * g_ffn).astype(bf16)), True)
    h_away = send_core(h_mine)

    hidden, factors = ffn_forward(h_mine, h_away, w_gu)
    down_grad = mm_rows(grad_all, hidden).astype(bf16)
    down_out = reduce_z(down_grad)

    ffn_away = away_product(hidden, w_d, slots, (down_grad,))
    ffn_add = send_core(ffn_away)
    d_gu = ffn_backward(grad_all, w_d, factors, ffn_away)
    ffn_pieces = scatter_product(hidden, w_d, 0, slots, ffn_add, (d_gu,))
    ffn_near = scatter_near(ffn_pieces)
    gu_grad = rows_product(h_mine, h_away, d_gu, 0, 2, earlier=(ffn_pieces[-1],))
    h2_away = away_product(d_gu, w_gu, slots, (gu_grad,))
    ffn_middle = scatter_middle(ffn_pieces, ffn_near)
    gu_grad = rows_product(h_mine, h_away, d_gu, 2, 2, gu_grad, (h2_away, *ffn_middle))
    gu_grad, down_out = tie(gu_grad, down_out)
    gu_out = reduce_z(gu_grad)
    h2_add = send_core(h2_away)
    ffn_far = scatter_far(ffn_middle)
    h2_pieces = list(scatter_product(d_gu, w_gu, 0, slots, earlier=(gu_grad,)))
    h2_pieces[0], h2_add = tie(h2_pieces[0], h2_add)
    h2_summed = add_away(h2_pieces, h2_add)
    h2_summed[-1], ffn_far = tie(h2_summed[-1], ffn_far)
    ffn_rows = scatter_end(ffn_pieces, ffn_near, ffn_far)
    h2_near = scatter_near(h2_summed)
    h2_far = scatter_far(scatter_middle(h2_summed, h2_near))
    kept, h2_own = (h2_pieces, h2_add) if square() else (h2_summed, None)
    g1, g1_block = rows_backward(kept, h2_near, h2_far, h2_own, mid, grad_mine, g_ffn)
    g1_low = join_rows(exchange_rows(g1_block), True)

    layer_block, g1_low = tie((mid + ffn_rows).astype(bf16), g1_low)
    layer_near = exchange_near(layer_block)
    d_context = column_product(g1_low, w_attn, o_first, q_cols, bf16)
    d_qkv = attention_backward(relative_place, lengths, qkv, tables, d_context)
    d_qkv, layer_near = tie(d_qkv, layer_near)
    layer_middle = exchange_middle(layer_near)
    layer_far = exchange_far(layer_middle)
    h1_pieces = list(scatter_product(d_qkv, w_attn, 0, slots))
    attn_grads = attention_products(g1_low, context, h_attn, d_qkv, h1_pieces[0])
    h1_pieces[-1], layer_far = tie(h1_pieces[-1], layer_far)
    layer_out = join_rows((layer_block, *layer_near, *layer_far), False)
    h1_near = scatter_near(h1_pieces)
    if square():
        first, attn_grads = tie(h1_near[0], attn_grads)
        *h1_near, layer_out = tie(first, h1_near[1], layer_out)
    attn_out = reduce_dp(attn_grads)
    h1_far = scatter_far(scatter_middle(h1_pieces, h1_near))
    _, grad_block = rows_backward(h1_pieces, h1_near, h1_far, None, x_rel, g1, g_attn)
    grad_pieces = list(exchange_rows(grad_block))
    grad_pieces[0], gu_out, down_out = tie(grad_pieces[0], gu_out, down_out)
    (down_out,) = from_core(down_out, 1, True)
    gate_out, up_out = from_core(gu_out, 2, earlier=(down_out,))

    rows_here = gain_attn.shape[0]

    ffn_sums = sum(
        jnp.sum(w.astype(f32) * g, axis=1) for w, g in [(gate_weight, gate_out), (up_weight, up_out)]
    ) / gain_ffn.astype(f32)
    if square():
        joined = join_near(grad_pieces[:3], f32)
        *far_pieces, attn_out, joined, ffn_sums = tie(*grad_pieces[3:], attn_out, joined, ffn_sums)
    out_out, q_out, send = attention_end(attn_out, query_weight, kv_block, gain_attn, ffn_sums)
    key_grad, value_grad, gain_attn_grad, gain_ffn_grad = collect_heads(send, KEY_VALUE_HEADS)
    if square():
        grad_input = join_far(far_pieces, joined)
    else:
        grad_input = grad_pieces[1].astype(f32)
    return (
        layer_out[None],
        grad_input[None],
        gain_attn_grad,
        q_out,
        key_grad,
        value_grad,
        out_out,
        gain_ffn_grad,
        gate_out,
        up_out,
        down_out,
    )


def solution(mesh):
    dp_size, mp_size = mesh.shape["dp"], mesh.shape["mp"]
    split = Mesh(mesh.devices.reshape(dp_size // 2, 2, mp_size), ("z", "core", "mp"))
    return jax.shard_map(
        local,
        mesh=split,
        in_specs=(
            P(DP, None, None),
            P(DP),
            P(DP),
            P(DP, "mp"),
            P(DP, None, "mp"),
            P(DP, None, "mp"),
            P("mp", DP),
            P(DP),
            P(DP, "mp"),
            P(DP, "mp"),
            P("mp", DP),
            P(DP, None, None),
        ),
        out_specs=(
            P(DP, None, None),
            P(DP, None, None),
            P(DP),
            P(DP, "mp"),
            P(DP, None, "mp"),
            P(DP, None, "mp"),
            P("mp", DP),
            P(DP),
            P(DP, "mp"),
            P(DP, "mp"),
            P("mp", DP),
        ),
        check_vma=False,
    )
```
